32 devices in a mesh: dp: 2 (over x), pipe: 4 (over z), expert: 4 (over y, core).
Axes of the slice: x: 2, y: 2, z: 4, core: 2. Of those that a mesh axis runs over, the one named last changes fastest.
Arguments:
- tokens: bfloat16 [1024, 2048], P(('dp', 'expert')), may hold values from -6 to 6
- cotangent: bfloat16 [1024, 2048], P(('dp', 'expert')), may hold values from -6 to 6
- owner_ids: int32 [4, 1024, 4], P('pipe', ('dp', 'expert')), may hold values from 0 to 7, all different within a row; in each aligned block of 32 rows (0 to 31, 32 to 63, ..., all dimensions but the last counted through in order) at most 20 rows name the same one
- gate_weights: bfloat16 [4, 1024, 4], P('pipe', ('dp', 'expert')), may hold values from 0.049804688 to 0.25
- norm_gain: float32 [4, 2048], P('pipe'), may hold values from 0.5 to 1.5
- w_gate: bfloat16 [4, 8, 2048, 384], P('pipe', ('dp', 'expert')), may hold values from -0.125 to 0.125
- w_up: bfloat16 [4, 8, 2048, 384], P('pipe', ('dp', 'expert')), may hold values from -0.125 to 0.125
- w_down: bfloat16 [4, 8, 384, 2048], P('pipe', ('dp', 'expert')), may hold values from -0.3125 to 0.3125
Outputs:
- segment_out: bfloat16 [4, 1024, 2048], P('pipe', ('dp', 'expert'))
- segment_grad: bfloat16 [4, 1024, 2048], P('pipe', ('dp', 'expert'))
- gain_grad: float32 [4, 2048], P('pipe')
The draws below stay inside these ranges and needn't reach their ends.
Inputs may be any that keep to these rules, and one draw needn't show every extreme that they name: `owner_ids`: each row names 4 different owners. In each aligned block of 32 rows (layers in order, then tokens) no owner is named by more than 20 rows, and that bound is reached.
All inputs are finite; a program needn't handle non-finite values.
Results may differ from the reference program's by a relative error of at most 0.014.
Values may be sent and summed in bfloat16 or wider, within the bound.
No kernel may reach another device: no remote copies, remote signals or barrier semaphores. Data moves between devices by JAX's collectives and lax.ppermute only.
A program may use at most 128 MiB of HBM per device.

```python
import math
import jax
import jax.numpy as jnp
import numpy as np
from jax import lax

D = 2048
FF = 384
EXP_DEV = 1
ROUTE_OWNERS = 4
MB_ROWS = 32
OWNERS = 8
EXPERTS = 8
CAP = 20
TOKENS = 1024
LAYERS = 4


def levels(rng, extent, cuts, smallest, largest):
    def one(dim, shards_of):
        heights = jax.random.uniform(jax.random.fold_in(jax.random.fold_in(rng, 6), dim), (shards_of,), jnp.float32, smallest / len(cuts), largest / len(cuts))
        return jnp.repeat(jnp.exp(heights), extent[dim] // shards_of).reshape((-1,) + (1,) * (len(extent) - dim - 1))

    loudness = one(*cuts[0])
    for cut in cuts[1:]:
        loudness = loudness * one(*cut)
    return loudness


def routed_block(key, own, number, rows, number_of, top, limit, slope):
    ranking = jax.random.permutation(key, number_of)
    crowded, usual = load_shares(number_of, rows * top, limit, slope, True), load_shares(number_of, rows * top, limit, slope, False)
    places = jnp.arange(number_of)

    def named(sizes, turn):
        used = int((sizes > 0).sum())
        fixed = max(1, used // 4)
        shifted = fixed + (places - fixed + turn * (used - fixed)) % max(1, number_of - fixed)
        return jnp.zeros((number_of,), jnp.int32).at[ranking[jnp.where(places < fixed, places, shifted)]].set(jnp.asarray(sizes, jnp.int32))

    sizes = jnp.where(number % 4 == 0, named(crowded, number // 4), named(usual, number - number // 4 - 1))
    mixed = jax.random.permutation(jax.random.fold_in(own, 3), number_of)
    source_of, receiver = mixed[0:number_of // 2 * 2:2], mixed[1:number_of // 2 * 2:2]
    margin = jnp.minimum(sizes[source_of] - 1, limit - sizes[receiver]) // 2
    margin = jnp.where((source_of == ranking[0]) | (receiver == ranking[0]) | (sizes[receiver] == 0), 0, jnp.maximum(margin, 0))
    shifted = jax.random.randint(jax.random.fold_in(own, 4), (number_of // 2,), 0, 1 << 20) % (margin + 1)
    sizes = sizes.at[source_of].add(-shifted).at[receiver].add(shifted)
    members = jnp.searchsorted(jnp.cumsum(sizes), jnp.arange(rows * top), side="right").astype(jnp.int32)
    listing = members.reshape(top, rows).T
    listing = listing[jax.random.permutation(jax.random.fold_in(own, 1), rows)]
    turn = jax.random.randint(jax.random.fold_in(own, 2), (rows, 1), 0, top)
    return jnp.take_along_axis(listing, (jnp.arange(top)[None, :] + turn) % top, axis=1)


def load_shares(count, total, limit, skew, full):
    weights = [(1 << 20) // math.isqrt(rank ** skew) + 1 for rank in range(1, count + 1)]
    largest = limit if full else min(limit, max(-(-total // count), total * weights[0] // sum(weights)))
    least = 1 if total - largest >= count - 1 else 0
    holding, spare = [largest] + [least] * (count - 1), total - largest - least * (count - 1)
    while spare > 0:
        candidates = [i for i in range(1, count) if holding[i] < largest] or [i for i in range(1, count) if holding[i] < limit]
        mass, left = sum([weights[i] for i in candidates]), spare
        for i in candidates:
            more = min(limit - holding[i], max(1, left * weights[i] // mass), spare)
            holding[i] = holding[i] + more
            spare = spare - more
    return np.array(holding)


def centred(stream_key, extent, spread, reach, pieces=(), kind=jnp.bfloat16):
    result = spread * jax.random.normal(stream_key, extent, jnp.float32)
    if pieces:
        result = result * levels(stream_key, extent, pieces, -0.22, 0.18)
    return jnp.clip(result, -reach, reach).astype(kind)


def setup_inputs(seed: int = 0) -> dict:
    key_of = jax.random.split(jax.random.key(seed), 9)
    tokens = centred(key_of[0], (TOKENS, D), 1.0, 6.0, ((0, 8),))
    cotangent = centred(key_of[1], (TOKENS, D), 1.0, 6.0, ((0, 8),))
    owner_ids_keys = jax.random.split(jax.random.fold_in(key_of[2], 1), LAYERS * TOKENS // MB_ROWS)
    owner_ids_turns = jax.random.permutation(jax.random.fold_in(key_of[2], 3), LAYERS * TOKENS // MB_ROWS)
    owner_ids = jax.vmap(lambda own, number: routed_block(jax.random.fold_in(key_of[2], 2), own, number, MB_ROWS, OWNERS, ROUTE_OWNERS, CAP, 1))(owner_ids_keys, owner_ids_turns).reshape((LAYERS, TOKENS, ROUTE_OWNERS))
    gate_weights = jnp.clip(0.049804688 + 0.20019531 * jax.random.uniform(key_of[3], (LAYERS, TOKENS, EXP_DEV * ROUTE_OWNERS), jnp.float32) ** levels(key_of[3], (LAYERS, TOKENS, EXP_DEV * ROUTE_OWNERS), ((0, 4), (1, 8)), -0.2, 0.2), 0.049804688, 0.25).astype(jnp.bfloat16)
    norm_gain = jnp.clip(1.0 + 0.1 * jax.random.normal(key_of[4], (LAYERS, D), jnp.float32), 0.5, 1.5)
    w_gate = centred(key_of[5], (LAYERS, EXPERTS, D, FF), D ** -0.5, 0.125, ((0, 4), (1, 8)))
    w_up = centred(key_of[6], (LAYERS, EXPERTS, D, FF), D ** -0.5, 0.125, ((0, 4), (1, 8)))
    w_down = centred(key_of[7], (LAYERS, EXPERTS, FF, D), FF ** -0.5, 0.3125, ((0, 4), (1, 8)))
    return dict(tokens=tokens, cotangent=cotangent, owner_ids=owner_ids, gate_weights=gate_weights, norm_gain=norm_gain, w_gate=w_gate, w_up=w_up, w_down=w_down)


epsilon = 1e-06

def inverse_rms(values):
    return lax.rsqrt(lax.optimization_barrier(jnp.mean(values * values, axis=-1, keepdims=True)) + epsilon)

def owner_rows(layer_ids, owner, bound):
    hit_mask = jnp.any(layer_ids == owner, axis=1)
    row_index = jnp.nonzero(hit_mask, size=bound, fill_value=0)[0].astype(jnp.int32)
    hit_count = jnp.sum(hit_mask.astype(jnp.int32))
    is_valid = jnp.arange(bound, dtype=jnp.int32) < hit_count
    chosen = (jnp.take(layer_ids, row_index, axis=0) == owner).astype(jnp.int32)
    which_slot = jnp.argmax(chosen, axis=1).astype(jnp.int32)
    return (row_index, is_valid, which_slot)

def pick_pairs(layer_gates, row_index, which_slot):
    gate_rows = jnp.take(layer_gates, row_index, axis=0)
    columns = (EXP_DEV * which_slot[:, None] + jnp.arange(EXP_DEV, dtype=jnp.int32)[None, :]).astype(jnp.int32)
    return jnp.take_along_axis(gate_rows, columns, axis=1).astype(jnp.float32)

def contract_last(left, right):
    return lax.dot_general(left, right, (((1,), (1,)), ((), ())), preferred_element_type=jnp.float32)

def layer_forward(layer_in, layer_ids, layer_gates, gain_row, gate_mats, up_mats, down_mats):
    x_float = layer_in.astype(jnp.float32)
    scale = inverse_rms(x_float)
    normed = (x_float * scale * gain_row).astype(jnp.bfloat16)
    bound = TOKENS // MB_ROWS * CAP

    def per_owner(branch, owner):
        row_index, is_valid, which_slot = owner_rows(layer_ids, owner, bound)
        picked = jnp.take(normed, row_index, axis=0)
        pairs = pick_pairs(layer_gates, row_index, which_slot)
        summed = jnp.zeros((bound, D), jnp.float32)
        for expert in range(EXP_DEV):
            number = owner * EXP_DEV + expert
            gate_pre = jnp.dot(picked, lax.dynamic_index_in_dim(gate_mats, number, 0, keepdims=False), preferred_element_type=jnp.float32)
            up_pre = jnp.dot(picked, lax.dynamic_index_in_dim(up_mats, number, 0, keepdims=False), preferred_element_type=jnp.float32)
            hidden = (jax.nn.silu(gate_pre) * up_pre).astype(jnp.bfloat16)
            projected = jnp.dot(hidden, lax.dynamic_index_in_dim(down_mats, number, 0, keepdims=False), preferred_element_type=jnp.float32)
            summed = summed + pairs[:, expert:expert + 1] * projected
        rounded = lax.optimization_barrier(summed.astype(jnp.bfloat16)).astype(jnp.float32)
        rounded = jnp.where(is_valid[:, None], rounded, 0.0)
        return (branch.at[row_index].add(rounded), None)
    branch, _ = lax.scan(per_owner, jnp.zeros((TOKENS, D), jnp.float32), jnp.arange(OWNERS, dtype=jnp.int32))
    return (x_float + branch).astype(jnp.bfloat16)

def layer_backward(layer_in, grad_in, layer_ids, layer_gates, gain_row, gate_mats, up_mats, down_mats):
    x_float = layer_in.astype(jnp.float32)
    scale = inverse_rms(x_float)
    normed = (x_float * scale * gain_row).astype(jnp.bfloat16)
    bound = TOKENS // MB_ROWS * CAP

    def per_owner(branch, owner):
        row_index, is_valid, which_slot = owner_rows(layer_ids, owner, bound)
        picked = jnp.take(normed, row_index, axis=0)
        grads = jnp.take(grad_in, row_index, axis=0)
        pairs = pick_pairs(layer_gates, row_index, which_slot)
        summed = jnp.zeros((bound, D), jnp.float32)
        for expert in range(EXP_DEV):
            number = owner * EXP_DEV + expert
            gate_mat = lax.dynamic_index_in_dim(gate_mats, number, 0, keepdims=False)
            up_mat = lax.dynamic_index_in_dim(up_mats, number, 0, keepdims=False)
            down_mat = lax.dynamic_index_in_dim(down_mats, number, 0, keepdims=False)
            gate_pre = jnp.dot(picked, gate_mat, preferred_element_type=jnp.float32)
            up_pre = jnp.dot(picked, up_mat, preferred_element_type=jnp.float32)
            q_vals = contract_last(grads, down_mat)
            sigma = jax.nn.sigmoid(gate_pre)
            weight = pairs[:, expert:expert + 1]
            d_gate = (q_vals * weight * up_pre * sigma * (1.0 + gate_pre * (1.0 - sigma))).astype(jnp.bfloat16)
            d_up = (q_vals * weight * gate_pre * sigma).astype(jnp.bfloat16)
            summed = summed + contract_last(d_gate, gate_mat) + contract_last(d_up, up_mat)
        rounded = lax.optimization_barrier(summed.astype(jnp.bfloat16)).astype(jnp.float32)
        rounded = jnp.where(is_valid[:, None], rounded, 0.0)
        return (branch.at[row_index].add(rounded), None)
    normed_grad, _ = lax.scan(per_owner, jnp.zeros((TOKENS, D), jnp.float32), jnp.arange(OWNERS, dtype=jnp.int32))
    weighted = gain_row * normed_grad
    grad_x = grad_in.astype(jnp.float32) + scale * weighted - x_float * scale * scale * scale * lax.optimization_barrier(jnp.mean(weighted * x_float, axis=-1, keepdims=True))
    gain_part = lax.optimization_barrier(jnp.sum(normed_grad * x_float * scale, axis=0))
    return (grad_x.astype(jnp.bfloat16), gain_part)

def reference(tokens, cotangent, owner_ids, gate_weights, norm_gain, w_gate, w_up, w_down):
    inputs_list = []
    outputs_list = []
    current = tokens
    for layer in range(LAYERS):
        inputs_list.append(current)
        current = layer_forward(current, owner_ids[layer], gate_weights[layer], norm_gain[layer], w_gate[layer], w_up[layer], w_down[layer])
        outputs_list.append(current)
    grads_list = [None] * LAYERS
    gains_list = [None] * LAYERS
    flowing = cotangent
    for layer in range(LAYERS - 1, -1, -1):
        flowing, gain_part = layer_backward(inputs_list[layer], flowing, owner_ids[layer], gate_weights[layer], norm_gain[layer], w_gate[layer], w_up[layer], w_down[layer])
        grads_list[layer] = flowing
        gains_list[layer] = gain_part
    return (jnp.stack(outputs_list), jnp.stack(grads_list), jnp.stack(gains_list))
```

```python
import jax
import jax.numpy as jnp
from jax import lax
from jax.sharding import PartitionSpec as P

MICRO = 4


epsilon = 1e-06


def from_behind(value, axis, steps):
    count = lax.axis_size(axis)
    leading, last = (max(0, -steps), min(count, count - steps))
    return lax.ppermute(value, axis, [(source, source + steps) for source in range(leading, last)])


def inverse_rms(values):
    return lax.rsqrt(jnp.mean(values * values, axis=-1, keepdims=True) + epsilon)


def contract_last(left, right):
    return lax.dot_general(
        left, right, (((1,), (1,)), ((), ())), preferred_element_type=jnp.float32
    )


def route_tables(ids_part, owners, capacity):
    owner_range = jnp.arange(owners, dtype=jnp.int32)
    onehot = (ids_part[:, :, None] == owner_range[None, None, :]).astype(jnp.int32)
    member = jnp.sum(onehot, axis=1)
    position = jnp.cumsum(member, axis=0) - member
    slot_range = jnp.arange(capacity, dtype=jnp.int32)
    placed = (position[:, :, None] == slot_range[None, None, :]) & (member[:, :, None] > 0)
    placing = jnp.transpose(placed, (1, 2, 0)).astype(jnp.bfloat16)
    return (onehot.astype(jnp.float32), placing)


def gate_slots(onehot, gates_part, placing, experts_here):
    gate_pairs = gates_part.astype(jnp.float32).reshape(gates_part.shape[0], -1, experts_here)
    chosen = jnp.einsum("rjo,rjc->roc", onehot, gate_pairs)
    return jnp.einsum("okr,roc->okc", placing.astype(jnp.float32), chosen).astype(jnp.bfloat16)


def send_rows(row_block, pair_block):
    got_rows, got_pairs = (
        lax.all_to_all(row_block, ("dp", "expert"), split_axis=0, concat_axis=0, tiled=True),
        lax.all_to_all(pair_block, ("dp", "expert"), split_axis=0, concat_axis=0, tiled=True),
    )
    return (got_rows, got_pairs)


def return_rows(row_block):
    return lax.all_to_all(row_block, ("dp", "expert"), split_axis=0, concat_axis=0, tiled=True)


def send_grads(row_block):
    return lax.all_to_all(row_block, ("dp", "expert"), split_axis=0, concat_axis=0, tiled=True)


def return_grads(row_block):
    return lax.all_to_all(row_block, ("dp", "expert"), split_axis=0, concat_axis=0, tiled=True)


def expert_forward(flat_rows, flat_pairs, joint_mats, down_mats):
    hidden_width = down_mats.shape[1]
    joint_pre = jnp.dot(flat_rows, joint_mats[0], preferred_element_type=jnp.float32)
    gate_pre = joint_pre[:, :hidden_width]
    up_pre = joint_pre[:, hidden_width:]
    hidden = (jax.nn.silu(gate_pre) * up_pre).astype(jnp.bfloat16)
    projected = jnp.dot(hidden, down_mats[0], preferred_element_type=jnp.float32)
    term = flat_pairs.astype(jnp.float32) * projected
    kept_both = [joint_pre]
    return (term.astype(jnp.bfloat16), jnp.stack(kept_both))


def expert_backward(grad_rows, flat_pairs, joint_keep, joint_mats, down_mats):
    hidden_width = down_mats.shape[1]
    q_vals = contract_last(grad_rows, down_mats[0])
    gate_pre = joint_keep[0][:, :hidden_width]
    up_pre = joint_keep[0][:, hidden_width:]
    sigma = jax.nn.sigmoid(gate_pre)
    weight = flat_pairs.astype(jnp.float32)
    d_gate = (q_vals * weight * up_pre * sigma * (1.0 + gate_pre * (1.0 - sigma))).astype(
        jnp.bfloat16
    )
    d_up = (q_vals * weight * gate_pre * sigma).astype(jnp.bfloat16)
    joint_grad = jnp.concatenate([d_gate, d_up], axis=1)
    term = contract_last(joint_grad, joint_mats[0])
    return term.astype(jnp.bfloat16)


def slot_body(tokens, cotangent, owner_ids, gate_weights, norm_gain, w_gate, w_up, w_down):
    segments = lax.axis_size("pipe")
    segment_index = lax.axis_index("pipe")
    owners = lax.axis_size("dp") * lax.axis_size("expert")
    tok_rows = tokens.shape[0]
    width = tokens.shape[1]
    micro_rows = tok_rows // MICRO
    route_count = owner_ids.shape[2]
    capacity = max(2, (5 * micro_rows * route_count + 4 * owners - 1) // (4 * owners))
    slot_count = owners * capacity
    gain_row = norm_gain[0]
    joint_mats = jnp.concatenate([w_gate[0], w_up[0]], axis=2)
    down_mats = w_down[0]
    layer_ids = owner_ids[0]
    layer_gates = gate_weights[0]
    experts_here = joint_mats.shape[0]
    joint_width = joint_mats.shape[2]

    def skip_forward(operands):
        return (
            jnp.zeros((slot_count, width), jnp.bfloat16),
            jnp.zeros((experts_here, slot_count, joint_width), jnp.float32),
        )

    def run_forward(operands):
        return expert_forward(operands[0], operands[1], joint_mats, down_mats)

    def skip_backward(operands):
        return jnp.zeros((slot_count, width), jnp.bfloat16)

    def run_backward(operands):
        return expert_backward(operands[0], operands[1], operands[2], joint_mats, down_mats)

    def timing(micro):
        is_valid = (micro >= 0) & (micro < MICRO)
        slot_pick = jnp.where(is_valid, micro, MICRO)
        start_row = jnp.clip(micro, 0, MICRO - 1) * micro_rows
        return (is_valid, slot_pick, start_row)

    layer_outs = jnp.zeros((MICRO + 1, micro_rows, width), jnp.bfloat16)
    layer_ins = jnp.zeros((MICRO + 1, micro_rows, width), jnp.bfloat16)
    kept_joint = jnp.zeros((MICRO + 1, experts_here, slot_count, joint_width), jnp.float32)
    kept_pairs = jnp.zeros((MICRO + 1, slot_count, experts_here), jnp.bfloat16)
    grad_outs = jnp.zeros((MICRO + 1, micro_rows, width), jnp.bfloat16)
    gain_sum = jnp.zeros((width,), jnp.float32)
    ticks = MICRO + segments - 1
    incoming = jnp.zeros((micro_rows, width), jnp.bfloat16)
    for tick_num in range(ticks):
        forward_is_valid, forward_slot_pick, forward_start_row = timing(tick_num - segment_index)
        forward_own_part = lax.dynamic_slice_in_dim(tokens, forward_start_row, micro_rows, 0)
        forward_layer_in = jnp.where(segment_index == 0, forward_own_part, incoming)
        forward_ids_part = lax.dynamic_slice_in_dim(layer_ids, forward_start_row, micro_rows, 0)
        gates_part = lax.dynamic_slice_in_dim(layer_gates, forward_start_row, micro_rows, 0)
        forward_x_float = forward_layer_in.astype(jnp.float32)
        forward_scale = inverse_rms(forward_x_float)
        normed = (forward_x_float * forward_scale * gain_row).astype(jnp.bfloat16)
        forward_onehot, forward_placing = route_tables(forward_ids_part, owners, capacity)
        row_block = jnp.einsum(
            "okr,rd->okd", forward_placing, normed, preferred_element_type=jnp.float32
        ).astype(jnp.bfloat16)
        pair_block = gate_slots(forward_onehot, gates_part, forward_placing, experts_here)
        f_valid, f_pick, layer_in, x_float, f_placing, row_block, pair_block = (
            forward_is_valid,
            forward_slot_pick,
            forward_layer_in,
            forward_x_float,
            forward_placing,
            row_block,
            pair_block,
        )
        got_rows, got_pairs = send_rows(row_block, pair_block)
        flat_rows = got_rows.reshape(slot_count, width)
        flat_pairs = got_pairs.reshape(slot_count, experts_here)
        result, joint_pre = lax.cond(f_valid, run_forward, skip_forward, (flat_rows, flat_pairs))
        returned = return_rows(result.reshape(owners, capacity, width))
        branch = jnp.einsum("okr,okd->rd", f_placing, returned, preferred_element_type=jnp.float32)
        layer_out = (x_float + branch).astype(jnp.bfloat16)
        layer_outs = lax.dynamic_update_index_in_dim(layer_outs, layer_out, f_pick, 0)
        layer_ins = lax.dynamic_update_index_in_dim(layer_ins, layer_in, f_pick, 0)
        kept_joint = lax.dynamic_update_index_in_dim(kept_joint, joint_pre, f_pick, 0)
        kept_pairs = lax.dynamic_update_index_in_dim(kept_pairs, flat_pairs, f_pick, 0)
        if tick_num + 1 < ticks:
            incoming = from_behind(layer_out, "pipe", 1)
    incoming = jnp.zeros((micro_rows, width), jnp.bfloat16)
    for tick_num in range(ticks):
        backward_is_valid, backward_slot_pick, backward_start_row = timing(
            tick_num - (segments - 1 - segment_index)
        )
        own_part = lax.dynamic_slice_in_dim(cotangent, backward_start_row, micro_rows, 0)
        backward_grad_in = jnp.where(segment_index == segments - 1, own_part, incoming)
        ids_part = lax.dynamic_slice_in_dim(layer_ids, backward_start_row, micro_rows, 0)
        backward_layer_in = lax.dynamic_index_in_dim(
            layer_ins, backward_slot_pick, 0, keepdims=False
        )
        backward_x_float = backward_layer_in.astype(jnp.float32)
        backward_scale = inverse_rms(backward_x_float)
        _, backward_placing = route_tables(ids_part, owners, capacity)
        grad_block = jnp.einsum(
            "okr,rd->okd", backward_placing, backward_grad_in, preferred_element_type=jnp.float32
        ).astype(jnp.bfloat16)
        b_valid, b_pick, grad_in, bx_float, b_scale, b_placing, grad_block = (
            backward_is_valid,
            backward_slot_pick,
            backward_grad_in,
            backward_x_float,
            backward_scale,
            backward_placing,
            grad_block,
        )
        got_grads = send_grads(grad_block).reshape(slot_count, width)
        joint_keep = lax.dynamic_index_in_dim(kept_joint, b_pick, 0, keepdims=False)
        pair_keep = lax.dynamic_index_in_dim(kept_pairs, b_pick, 0, keepdims=False)
        owner_grad = lax.cond(
            b_valid, run_backward, skip_backward, (got_grads, pair_keep, joint_keep)
        )
        returned = return_grads(owner_grad.reshape(owners, capacity, width))
        normed_grad = jnp.einsum(
            "okr,okd->rd", b_placing, returned, preferred_element_type=jnp.float32
        )
        weighted = gain_row * normed_grad
        grad_x = (
            grad_in.astype(jnp.float32)
            + b_scale * weighted
            - bx_float
            * b_scale
            * b_scale
            * b_scale
            * jnp.mean(weighted * bx_float, axis=-1, keepdims=True)
        )
        gain_term = jnp.where(b_valid, jnp.sum(normed_grad * bx_float * b_scale, axis=0), 0.0)
        grad_bf, gain_term = (grad_x.astype(jnp.bfloat16), gain_term)
        grad_outs = lax.dynamic_update_index_in_dim(grad_outs, grad_bf, b_pick, 0)
        gain_sum = gain_sum + gain_term
        if tick_num + 1 < ticks:
            incoming = from_behind(grad_bf, "pipe", -1)
    gain_grad = lax.psum(gain_sum, ("dp", "expert"))
    segment_out = layer_outs[:MICRO].reshape(1, tok_rows, width)
    segment_grad = grad_outs[:MICRO].reshape(1, tok_rows, width)
    return (segment_out, segment_grad, gain_grad.reshape(1, width))


def swap_cores(value):
    count = lax.axis_size("expert")
    return lax.ppermute(value, "expert", [(e, e ^ 1) for e in range(count)])


def device_number(dp, pipe, expert):
    return (dp * lax.axis_size("pipe") + pipe) * lax.axis_size("expert") + expert


def shifted(value, dp_step, chip_step, pipe_step):
    dps, pipes, experts = (lax.axis_size(name) for name in ("dp", "pipe", "expert"))
    pairs = []
    for dp in range(dps):
        for pipe in range(pipes):
            for expert in range(experts):
                target = device_number(
                    (dp + dp_step) % dps,
                    (pipe + pipe_step) % pipes,
                    (expert + 2 * chip_step) % experts,
                )
                pairs.append((device_number(dp, pipe, expert), target))
    return lax.ppermute(value, ("dp", "pipe", "expert"), pairs)


def chip_steps():
    dps, chips = lax.axis_size("dp"), lax.axis_size("expert") // 2
    steps = [(d, c) for d in range(dps) for c in range(chips)]
    return sorted(steps[1:], key=lambda step: -(step[0] + step[1]))


def spread(rows):
    return [rows] + [shifted(rows, d, c, 0) for d, c in chip_steps()]


def collect(blocks):
    dps, chips = lax.axis_size("dp"), lax.axis_size("expert") // 2
    back = [shifted(block, -d % dps, -c % chips, 0) for block, (d, c) in zip(blocks[1:], chip_steps())]
    return [blocks[0]] + back


def dense_body(tokens, cotangent, owner_ids, gate_weights, norm_gain, w_gate, w_up, w_down):
    f32, bf16 = jnp.float32, jnp.bfloat16
    stages = lax.axis_size("pipe")
    stage = lax.axis_index("pipe")
    owners = lax.axis_size("dp") * lax.axis_size("expert")
    me = lax.axis_index("dp") * lax.axis_size("expert") + lax.axis_index("expert")
    tok_rows, width = tokens.shape
    rows = tok_rows // MICRO
    ff = w_down.shape[2]
    gain = norm_gain[0][None, :]
    ticks = MICRO + stages - 1

    pair_gate, pair_up, pair_down = (swap_cores(w[0, 0]) for w in (w_gate, w_up, w_down))
    joint = jnp.concatenate([w_gate[0, 0], pair_gate, w_up[0, 0], pair_up], axis=1)
    down = jnp.concatenate([w_down[0, 0], pair_down], axis=0)

    owner_range = jnp.arange(owners, dtype=jnp.int32)
    onehot = owner_ids[0][:, :, None] == owner_range
    table = jnp.sum(jnp.where(onehot, gate_weights[0].astype(f32)[:, :, None], 0.0), axis=1).astype(bf16)
    tables = jnp.stack(spread(table)).astype(f32)
    mine = jnp.sum(jnp.where(owner_range == me, tables, 0.0), axis=2)
    theirs = jnp.sum(jnp.where(owner_range == (me ^ 1), tables, 0.0), axis=2)
    pair = jnp.stack([mine, theirs], axis=-1)
    blocks = pair.shape[0]
    pair = pair.reshape(blocks, MICRO, rows, 2).transpose(1, 0, 2, 3).reshape(MICRO, blocks * rows, 2)
    padded = jnp.pad(pair, ((stages - 1, stages - 1), (0, 0), (0, 0)))
    forward_pairs = lax.dynamic_slice_in_dim(padded, stages - 1 - stage, ticks, 0)
    backward_pairs = lax.dynamic_slice_in_dim(padded, stage, ticks, 0)

    def wide(pairs):
        return jnp.repeat(pairs, ff, axis=1)

    def pick(saved, tick):
        first = tick - (2 * stages - 1)
        found = None
        for s in range(stages):
            at = first + 2 * s
            if 0 <= at < ticks and at < tick:
                found = saved[at] if found is None else jnp.where(stage == s, saved[at], found)
        return found

    pres, ins, outs, grads = [], [], [], []
    gain_sum = jnp.zeros((width,), f32)
    behind = ahead = None
    for tick in range(MICRO + 2 * stages - 1):
        if tick < ticks:
            if tick == 0:
                here = tokens[:rows]
            elif tick < MICRO:
                here = jnp.where(stage == 0, tokens[tick * rows:(tick + 1) * rows], behind)
            else:
                here = behind
            x = here.astype(f32)
            normed = (x * inverse_rms(x) * gain).astype(bf16)
            flat = jnp.concatenate(spread(normed), axis=0)
            pre = jnp.dot(flat, joint, preferred_element_type=f32)
            hidden = jax.nn.silu(pre[:, :2 * ff]) * pre[:, 2 * ff:] * wide(forward_pairs[tick])
            partial = jnp.dot(hidden.astype(bf16), down, preferred_element_type=f32).astype(bf16)
            parts = collect([partial[k * rows:(k + 1) * rows] for k in range(blocks)])
            out = (x + sum(p.astype(f32) for p in parts)).astype(bf16)
            pres.append(pre)
            ins.append(here)
            outs.append(out)
            if tick + 1 < ticks:
                behind_next = shifted(out, 0, 0, 1)
        if tick >= stages:
            number = tick - stages
            if number == 0:
                grad = cotangent[:rows]
            elif number < MICRO:
                grad = jnp.where(stage == stages - 1, cotangent[number * rows:(number + 1) * rows], ahead)
            else:
                grad = ahead
            x = pick(ins, tick).astype(f32)
            scale = inverse_rms(x)
            pre = pick(pres, tick)
            gate_pre, up_pre = pre[:, :2 * ff], pre[:, 2 * ff:]
            sigma = jax.nn.sigmoid(gate_pre)
            weight = wide(backward_pairs[number])
            gate_rate = weight * up_pre * sigma * (1.0 + gate_pre * (1.0 - sigma))
            up_rate = weight * gate_pre * sigma
            flat = jnp.concatenate(spread(grad), axis=0)
            q = contract_last(flat, down)
            both = jnp.concatenate([(q * gate_rate).astype(bf16), (q * up_rate).astype(bf16)], axis=1)
            partial = contract_last(both, joint).astype(bf16)
            parts = collect([partial[k * rows:(k + 1) * rows] for k in range(blocks)])
            normed_grad = sum(p.astype(f32) for p in parts)
            weighted = gain * normed_grad
            grad_x = (
                grad.astype(f32)
                + scale * weighted
                - x * scale * scale * scale * jnp.mean(weighted * x, axis=-1, keepdims=True)
            ).astype(bf16)
            gain_sum = gain_sum + jnp.sum(normed_grad * x * scale, axis=0)
            grads.append(grad_x)
            if number + 1 < ticks:
                ahead = shifted(grad_x, 0, 0, -1)
        if tick + 1 < ticks:
            behind = behind_next
    gain_grad = lax.psum(gain_sum, ("dp", "expert"))
    segment_out = lax.dynamic_slice_in_dim(jnp.concatenate(outs), stage * rows, tok_rows, 0)
    segment_grad = lax.dynamic_slice_in_dim(jnp.concatenate(grads), (stages - 1 - stage) * rows, tok_rows, 0)
    return (segment_out[None], segment_grad[None], gain_grad[None])


def body(tokens, cotangent, owner_ids, *rest):
    owners = lax.axis_size("dp") * lax.axis_size("expert")
    routed_densely = owners <= 2 * owner_ids.shape[2] and lax.axis_size("expert") % 2 == 0
    plan = dense_body if routed_densely else slot_body
    return plan(tokens, cotangent, owner_ids, *rest)


def solution(mesh):
    in_specs = (
        P(("dp", "expert"), None),
        P(("dp", "expert"), None),
        P("pipe", ("dp", "expert"), None),
        P("pipe", ("dp", "expert"), None),
        P("pipe", None),
        P("pipe", ("dp", "expert"), None, None),
        P("pipe", ("dp", "expert"), None, None),
        P("pipe", ("dp", "expert"), None, None),
    )
    out_specs = (
        P("pipe", ("dp", "expert"), None),
        P("pipe", ("dp", "expert"), None),
        P("pipe", None),
    )
    return jax.shard_map(body, mesh=mesh, in_specs=in_specs, out_specs=out_specs, check_vma=False)
```

```python
import jax
import jax.numpy as jnp
from jax import lax
from jax.experimental import pallas as pl
from jax.experimental.pallas import tpu as pltpu
import functools
from jax.sharding import PartitionSpec as P

MICRO = 4
LIMIT = 24 * 1024 * 1024


epsilon = 1e-06


def from_behind(value, axis, steps):
    count = lax.axis_size(axis)
    leading, last = (max(0, -steps), min(count, count - steps))
    return lax.ppermute(value, axis, [(source, source + steps) for source in range(leading, last)])


def inverse_rms(values):
    return lax.rsqrt(jnp.mean(values * values, axis=-1, keepdims=True) + epsilon)


def contract_last(left, right):
    return lax.dot_general(
        left, right, (((1,), (1,)), ((), ())), preferred_element_type=jnp.float32
    )


def route_tables(ids_part, owners, capacity):
    owner_range = jnp.arange(owners, dtype=jnp.int32)
    onehot = (ids_part[:, :, None] == owner_range[None, None, :]).astype(jnp.int32)
    member = jnp.sum(onehot, axis=1)
    position = jnp.cumsum(member, axis=0) - member
    slot_range = jnp.arange(capacity, dtype=jnp.int32)
    placed = (position[:, :, None] == slot_range[None, None, :]) & (member[:, :, None] > 0)
    placing = jnp.transpose(placed, (1, 2, 0)).astype(jnp.bfloat16)
    return (onehot.astype(jnp.float32), placing)


def gate_slots(onehot, gates_part, placing, experts_here):
    gate_pairs = gates_part.astype(jnp.float32).reshape(gates_part.shape[0], -1, experts_here)
    chosen = jnp.einsum("rjo,rjc->roc", onehot, gate_pairs)
    return jnp.einsum("okr,roc->okc", placing.astype(jnp.float32), chosen).astype(jnp.bfloat16)


def send_rows(row_block, pair_block):
    got_rows, got_pairs = (
        lax.all_to_all(row_block, ("dp", "expert"), split_axis=0, concat_axis=0, tiled=True),
        lax.all_to_all(pair_block, ("dp", "expert"), split_axis=0, concat_axis=0, tiled=True),
    )
    return (got_rows, got_pairs)


def return_rows(row_block):
    return lax.all_to_all(row_block, ("dp", "expert"), split_axis=0, concat_axis=0, tiled=True)


def send_grads(row_block):
    return lax.all_to_all(row_block, ("dp", "expert"), split_axis=0, concat_axis=0, tiled=True)


def return_grads(row_block):
    return lax.all_to_all(row_block, ("dp", "expert"), split_axis=0, concat_axis=0, tiled=True)


def expert_forward(flat_rows, flat_pairs, joint_mats, down_mats):
    hidden_width = down_mats.shape[1]
    joint_pre = jnp.dot(flat_rows, joint_mats[0], preferred_element_type=jnp.float32)
    gate_pre = joint_pre[:, :hidden_width]
    up_pre = joint_pre[:, hidden_width:]
    hidden = (jax.nn.silu(gate_pre) * up_pre).astype(jnp.bfloat16)
    projected = jnp.dot(hidden, down_mats[0], preferred_element_type=jnp.float32)
    term = flat_pairs.astype(jnp.float32) * projected
    kept_both = [joint_pre]
    return (term.astype(jnp.bfloat16), jnp.stack(kept_both))


def expert_backward(grad_rows, flat_pairs, joint_keep, joint_mats, down_mats):
    hidden_width = down_mats.shape[1]
    q_vals = contract_last(grad_rows, down_mats[0])
    gate_pre = joint_keep[0][:, :hidden_width]
    up_pre = joint_keep[0][:, hidden_width:]
    sigma = jax.nn.sigmoid(gate_pre)
    weight = flat_pairs.astype(jnp.float32)
    d_gate = (q_vals * weight * up_pre * sigma * (1.0 + gate_pre * (1.0 - sigma))).astype(
        jnp.bfloat16
    )
    d_up = (q_vals * weight * gate_pre * sigma).astype(jnp.bfloat16)
    joint_grad = jnp.concatenate([d_gate, d_up], axis=1)
    term = contract_last(joint_grad, joint_mats[0])
    return term.astype(jnp.bfloat16)


def slot_body(tokens, cotangent, owner_ids, gate_weights, norm_gain, w_gate, w_up, w_down):
    segments = lax.axis_size("pipe")
    segment_index = lax.axis_index("pipe")
    owners = lax.axis_size("dp") * lax.axis_size("expert")
    tok_rows = tokens.shape[0]
    width = tokens.shape[1]
    micro_rows = tok_rows // MICRO
    route_count = owner_ids.shape[2]
    capacity = max(2, (5 * micro_rows * route_count + 4 * owners - 1) // (4 * owners))
    slot_count = owners * capacity
    gain_row = norm_gain[0]
    joint_mats = jnp.concatenate([w_gate[0], w_up[0]], axis=2)
    down_mats = w_down[0]
    layer_ids = owner_ids[0]
    layer_gates = gate_weights[0]
    experts_here = joint_mats.shape[0]
    joint_width = joint_mats.shape[2]

    def skip_forward(operands):
        return (
            jnp.zeros((slot_count, width), jnp.bfloat16),
            jnp.zeros((experts_here, slot_count, joint_width), jnp.float32),
        )

    def run_forward(operands):
        return expert_forward(operands[0], operands[1], joint_mats, down_mats)

    def skip_backward(operands):
        return jnp.zeros((slot_count, width), jnp.bfloat16)

    def run_backward(operands):
        return expert_backward(operands[0], operands[1], operands[2], joint_mats, down_mats)

    def timing(micro):
        is_valid = (micro >= 0) & (micro < MICRO)
        slot_pick = jnp.where(is_valid, micro, MICRO)
        start_row = jnp.clip(micro, 0, MICRO - 1) * micro_rows
        return (is_valid, slot_pick, start_row)

    layer_outs = jnp.zeros((MICRO + 1, micro_rows, width), jnp.bfloat16)
    layer_ins = jnp.zeros((MICRO + 1, micro_rows, width), jnp.bfloat16)
    kept_joint = jnp.zeros((MICRO + 1, experts_here, slot_count, joint_width), jnp.float32)
    kept_pairs = jnp.zeros((MICRO + 1, slot_count, experts_here), jnp.bfloat16)
    grad_outs = jnp.zeros((MICRO + 1, micro_rows, width), jnp.bfloat16)
    gain_sum = jnp.zeros((width,), jnp.float32)
    ticks = MICRO + segments - 1
    incoming = jnp.zeros((micro_rows, width), jnp.bfloat16)
    for tick_num in range(ticks):
        forward_is_valid, forward_slot_pick, forward_start_row = timing(tick_num - segment_index)
        forward_own_part = lax.dynamic_slice_in_dim(tokens, forward_start_row, micro_rows, 0)
        forward_layer_in = jnp.where(segment_index == 0, forward_own_part, incoming)
        forward_ids_part = lax.dynamic_slice_in_dim(layer_ids, forward_start_row, micro_rows, 0)
        gates_part = lax.dynamic_slice_in_dim(layer_gates, forward_start_row, micro_rows, 0)
        forward_x_float = forward_layer_in.astype(jnp.float32)
        forward_scale = inverse_rms(forward_x_float)
        normed = (forward_x_float * forward_scale * gain_row).astype(jnp.bfloat16)
        forward_onehot, forward_placing = route_tables(forward_ids_part, owners, capacity)
        row_block = jnp.einsum(
            "okr,rd->okd", forward_placing, normed, preferred_element_type=jnp.float32
        ).astype(jnp.bfloat16)
        pair_block = gate_slots(forward_onehot, gates_part, forward_placing, experts_here)
        f_valid, f_pick, layer_in, x_float, f_placing, row_block, pair_block = (
            forward_is_valid,
            forward_slot_pick,
            forward_layer_in,
            forward_x_float,
            forward_placing,
            row_block,
            pair_block,
        )
        got_rows, got_pairs = send_rows(row_block, pair_block)
        flat_rows = got_rows.reshape(slot_count, width)
        flat_pairs = got_pairs.reshape(slot_count, experts_here)
        result, joint_pre = lax.cond(f_valid, run_forward, skip_forward, (flat_rows, flat_pairs))
        returned = return_rows(result.reshape(owners, capacity, width))
        branch = jnp.einsum("okr,okd->rd", f_placing, returned, preferred_element_type=jnp.float32)
        layer_out = (x_float + branch).astype(jnp.bfloat16)
        layer_outs = lax.dynamic_update_index_in_dim(layer_outs, layer_out, f_pick, 0)
        layer_ins = lax.dynamic_update_index_in_dim(layer_ins, layer_in, f_pick, 0)
        kept_joint = lax.dynamic_update_index_in_dim(kept_joint, joint_pre, f_pick, 0)
        kept_pairs = lax.dynamic_update_index_in_dim(kept_pairs, flat_pairs, f_pick, 0)
        if tick_num + 1 < ticks:
            incoming = from_behind(layer_out, "pipe", 1)
    incoming = jnp.zeros((micro_rows, width), jnp.bfloat16)
    for tick_num in range(ticks):
        backward_is_valid, backward_slot_pick, backward_start_row = timing(
            tick_num - (segments - 1 - segment_index)
        )
        own_part = lax.dynamic_slice_in_dim(cotangent, backward_start_row, micro_rows, 0)
        backward_grad_in = jnp.where(segment_index == segments - 1, own_part, incoming)
        ids_part = lax.dynamic_slice_in_dim(layer_ids, backward_start_row, micro_rows, 0)
        backward_layer_in = lax.dynamic_index_in_dim(
            layer_ins, backward_slot_pick, 0, keepdims=False
        )
        backward_x_float = backward_layer_in.astype(jnp.float32)
        backward_scale = inverse_rms(backward_x_float)
        _, backward_placing = route_tables(ids_part, owners, capacity)
        grad_block = jnp.einsum(
            "okr,rd->okd", backward_placing, backward_grad_in, preferred_element_type=jnp.float32
        ).astype(jnp.bfloat16)
        b_valid, b_pick, grad_in, bx_float, b_scale, b_placing, grad_block = (
            backward_is_valid,
            backward_slot_pick,
            backward_grad_in,
            backward_x_float,
            backward_scale,
            backward_placing,
            grad_block,
        )
        got_grads = send_grads(grad_block).reshape(slot_count, width)
        joint_keep = lax.dynamic_index_in_dim(kept_joint, b_pick, 0, keepdims=False)
        pair_keep = lax.dynamic_index_in_dim(kept_pairs, b_pick, 0, keepdims=False)
        owner_grad = lax.cond(
            b_valid, run_backward, skip_backward, (got_grads, pair_keep, joint_keep)
        )
        returned = return_grads(owner_grad.reshape(owners, capacity, width))
        normed_grad = jnp.einsum(
            "okr,okd->rd", b_placing, returned, preferred_element_type=jnp.float32
        )
        weighted = gain_row * normed_grad
        grad_x = (
            grad_in.astype(jnp.float32)
            + b_scale * weighted
            - bx_float
            * b_scale
            * b_scale
            * b_scale
            * jnp.mean(weighted * bx_float, axis=-1, keepdims=True)
        )
        gain_term = jnp.where(b_valid, jnp.sum(normed_grad * bx_float * b_scale, axis=0), 0.0)
        grad_bf, gain_term = (grad_x.astype(jnp.bfloat16), gain_term)
        grad_outs = lax.dynamic_update_index_in_dim(grad_outs, grad_bf, b_pick, 0)
        gain_sum = gain_sum + gain_term
        if tick_num + 1 < ticks:
            incoming = from_behind(grad_bf, "pipe", -1)
    gain_grad = lax.psum(gain_sum, ("dp", "expert"))
    segment_out = layer_outs[:MICRO].reshape(1, tok_rows, width)
    segment_grad = grad_outs[:MICRO].reshape(1, tok_rows, width)
    return (segment_out, segment_grad, gain_grad.reshape(1, width))


def swap_cores(value):
    count = lax.axis_size("expert")
    return lax.ppermute(value, "expert", [(e, e ^ 1) for e in range(count)])


def device_number(dp, pipe, expert):
    return (dp * lax.axis_size("pipe") + pipe) * lax.axis_size("expert") + expert


def shifted(value, dp_step, chip_step, pipe_step):
    dps, pipes, experts = (lax.axis_size(name) for name in ("dp", "pipe", "expert"))
    pairs = []
    for dp in range(dps):
        for pipe in range(pipes):
            for expert in range(experts):
                target = device_number(
                    (dp + dp_step) % dps,
                    (pipe + pipe_step) % pipes,
                    (expert + 2 * chip_step) % experts,
                )
                pairs.append((device_number(dp, pipe, expert), target))
    return lax.ppermute(value, ("dp", "pipe", "expert"), pairs)


def chip_steps():
    dps, chips = lax.axis_size("dp"), lax.axis_size("expert") // 2
    steps = [(d, c) for d in range(dps) for c in range(chips)]
    return sorted(steps[1:], key=lambda step: -(step[0] + step[1]))


def spread(rows):
    return [rows] + [shifted(rows, d, c, 0) for d, c in chip_steps()]


def collect(blocks):
    dps, chips = lax.axis_size("dp"), lax.axis_size("expert") // 2
    back = [shifted(block, -d % dps, -c % chips, 0) for block, (d, c) in zip(blocks[1:], chip_steps())]
    return [blocks[0]] + back


VMEM = pl.BlockSpec(memory_space=pltpu.VMEM)
CHUNK = 256


def cost(*arrays, flops):
    moved = sum(a.size * a.dtype.itemsize for a in arrays)
    return pl.CostEstimate(flops=flops, bytes_accessed=moved, transcendentals=0)


def forward_kernel(blocks, *refs):
    row_refs, (pair_ref, gain_ref, joint_ref, down_ref) = refs[:blocks], refs[blocks:blocks + 4]
    pre_ref, own_ref = refs[blocks + 4:blocks + 6]
    part_refs, (flat, hidden) = refs[blocks + 6:-2], refs[-2:]
    rows = row_refs[0].shape[0]
    both = down_ref.shape[0]
    width = flat.shape[1]
    gain = gain_ref[...]
    for k, row_ref in enumerate(row_refs):
        x = row_ref[...].astype(jnp.float32)
        flat[k * rows:(k + 1) * rows, :] = (x * inverse_rms(x) * gain).astype(jnp.bfloat16)
    own_weight, pair_weight = pair_ref[:, 0:1], pair_ref[:, 1:2]
    for start in range(0, both, CHUNK):
        gates, ups = slice(start, start + CHUNK), slice(both + start, both + start + CHUNK)
        gate_pre = jnp.dot(flat[...], joint_ref[:, gates], preferred_element_type=jnp.float32)
        up_pre = jnp.dot(flat[...], joint_ref[:, ups], preferred_element_type=jnp.float32)
        pre_ref[:, gates] = gate_pre
        pre_ref[:, ups] = up_pre
        column = start + lax.broadcasted_iota(jnp.int32, gate_pre.shape, 1)
        weight = jnp.where(column < both // 2, own_weight, pair_weight)
        hidden[:, gates] = (jax.nn.silu(gate_pre) * up_pre * weight).astype(jnp.bfloat16)
    for start in range(0, width, CHUNK):
        columns = slice(start, start + CHUNK)
        partial = jnp.dot(hidden[...], down_ref[:, columns], preferred_element_type=jnp.float32)
        own_ref[:, columns] = row_refs[0][:, columns].astype(jnp.float32) + partial[:rows]
        for k, part_ref in enumerate(part_refs):
            part_ref[:, columns] = partial[(k + 1) * rows:(k + 2) * rows].astype(jnp.bfloat16)


def backward_kernel(blocks, *refs):
    row_refs, (gate_ref, up_ref, joint_ref, down_ref) = refs[:blocks], refs[blocks:blocks + 4]
    own_ref = refs[blocks + 4]
    part_refs, (flat, hidden) = refs[blocks + 5:-2], refs[-2:]
    rows = row_refs[0].shape[0]
    both = down_ref.shape[0]
    width = flat.shape[1]
    for k, row_ref in enumerate(row_refs):
        flat[k * rows:(k + 1) * rows, :] = row_ref[...]
    for start in range(0, both, CHUNK):
        gates, ups = slice(start, start + CHUNK), slice(both + start, both + start + CHUNK)
        q = contract_last(flat[...], down_ref[gates, :])
        hidden[:, gates] = (q * gate_ref[:, gates]).astype(jnp.bfloat16)
        hidden[:, ups] = (q * up_ref[:, gates]).astype(jnp.bfloat16)
    for start in range(0, width, CHUNK):
        columns = slice(start, start + CHUNK)
        partial = contract_last(hidden[...], joint_ref[columns, :])
        own_ref[:, columns] = partial[:rows]
        for k, part_ref in enumerate(part_refs):
            part_ref[:, columns] = partial[(k + 1) * rows:(k + 2) * rows].astype(jnp.bfloat16)


def forward_experts(row_blocks, pair, gain, joint, down):
    blocks, (rows, width) = len(row_blocks), row_blocks[0].shape
    total, both = blocks * rows, down.shape[0]
    outs = [jax.ShapeDtypeStruct((total, 2 * both), jnp.float32), jax.ShapeDtypeStruct((rows, width), jnp.float32)]
    outs += [jax.ShapeDtypeStruct((rows, width), jnp.bfloat16)] * (blocks - 1)
    pre, *parts = pl.pallas_call(
        functools.partial(forward_kernel, blocks),
        out_shape=outs,
        in_specs=[VMEM] * (blocks + 4),
        out_specs=[VMEM] * len(outs),
        scratch_shapes=[pltpu.VMEM((total, width), jnp.bfloat16), pltpu.VMEM((total, both), jnp.bfloat16)],
        compiler_params=pltpu.CompilerParams(vmem_limit_bytes=LIMIT),
        cost_estimate=cost(joint, down, *outs, flops=6 * total * width * both),
        name="experts_forward",
    )(*row_blocks, pair, gain, joint, down)
    return pre, parts


def backward_experts(row_blocks, gate_rate, up_rate, joint, down):
    blocks, (rows, width) = len(row_blocks), row_blocks[0].shape
    total, both = blocks * rows, down.shape[0]
    outs = [jax.ShapeDtypeStruct((rows, width), jnp.float32)]
    outs += [jax.ShapeDtypeStruct((rows, width), jnp.bfloat16)] * (blocks - 1)
    return pl.pallas_call(
        functools.partial(backward_kernel, blocks),
        out_shape=outs,
        in_specs=[VMEM] * (blocks + 4),
        out_specs=[VMEM] * len(outs),
        scratch_shapes=[pltpu.VMEM((total, width), jnp.bfloat16), pltpu.VMEM((total, 2 * both), jnp.bfloat16)],
        compiler_params=pltpu.CompilerParams(vmem_limit_bytes=LIMIT),
        cost_estimate=cost(joint, down, gate_rate, up_rate, *outs, flops=6 * total * width * both),
        name="experts_backward",
    )(*row_blocks, gate_rate, up_rate, joint, down)


def dense_body(tokens, cotangent, owner_ids, gate_weights, norm_gain, w_gate, w_up, w_down):
    f32, bf16 = jnp.float32, jnp.bfloat16
    stages = lax.axis_size("pipe")
    stage = lax.axis_index("pipe")
    owners = lax.axis_size("dp") * lax.axis_size("expert")
    me = lax.axis_index("dp") * lax.axis_size("expert") + lax.axis_index("expert")
    tok_rows, width = tokens.shape
    rows = tok_rows // MICRO
    ff = w_down.shape[2]
    gain = norm_gain[0][None, :]
    ticks = MICRO + stages - 1

    pair_gate, pair_up, pair_down = (swap_cores(w[0, 0]) for w in (w_gate, w_up, w_down))
    joint = jnp.concatenate([w_gate[0, 0], pair_gate, w_up[0, 0], pair_up], axis=1)
    down = jnp.concatenate([w_down[0, 0], pair_down], axis=0)

    owner_range = jnp.arange(owners, dtype=jnp.int32)
    onehot = owner_ids[0][:, :, None] == owner_range
    table = jnp.sum(jnp.where(onehot, gate_weights[0].astype(f32)[:, :, None], 0.0), axis=1).astype(bf16)
    tables = jnp.stack(spread(table)).astype(f32)
    mine = jnp.sum(jnp.where(owner_range == me, tables, 0.0), axis=2)
    theirs = jnp.sum(jnp.where(owner_range == (me ^ 1), tables, 0.0), axis=2)
    pair = jnp.stack([mine, theirs], axis=-1)
    blocks = pair.shape[0]
    pair = pair.reshape(blocks, MICRO, rows, 2).transpose(1, 0, 2, 3).reshape(MICRO, blocks * rows, 2)
    padded = jnp.pad(pair, ((stages - 1, stages - 1), (0, 0), (0, 0)))
    forward_pairs = lax.dynamic_slice_in_dim(padded, stages - 1 - stage, ticks, 0)
    backward_pairs = lax.dynamic_slice_in_dim(padded, stage, ticks, 0)

    def choose(options):
        found = None
        for s, value in options:
            found = value if found is None else jnp.where(stage == s, value, found)
        return found

    def pick(saved, tick):
        first = tick - (2 * stages - 1)
        return choose([(s, saved[first + 2 * s]) for s in range(stages) if 0 <= first + 2 * s < min(ticks, tick)])

    pres, ins, outs, grads = [], [], [], []
    gain_sum = jnp.zeros((width,), f32)
    behind = ahead = None
    for tick in range(MICRO + 2 * stages - 1):
        if tick < ticks:
            if tick == 0:
                here = tokens[:rows]
            elif tick < MICRO:
                here = jnp.where(stage == 0, tokens[tick * rows:(tick + 1) * rows], behind)
            else:
                here = behind
            pre, parts = forward_experts(spread(here), forward_pairs[tick], gain, joint, down)
            out = sum(p.astype(f32) for p in collect(parts)).astype(bf16)
            pres.append(pre)
            ins.append(here)
            outs.append(out)
            if tick + 1 < ticks:
                behind_next = shifted(out, 0, 0, 1)
        if tick >= stages:
            number = tick - stages
            if number == 0:
                grad = cotangent[:rows]
            elif number < MICRO:
                grad = jnp.where(stage == stages - 1, cotangent[number * rows:(number + 1) * rows], ahead)
            else:
                grad = ahead
            x = pick(ins, tick).astype(f32)
            scale = inverse_rms(x)
            pre = pick(pres, tick)
            gate_pre, up_pre = pre[:, :2 * ff], pre[:, 2 * ff:]
            sigma = jax.nn.sigmoid(gate_pre)
            weight = jnp.repeat(backward_pairs[number], ff, axis=1)
            gate_rate = weight * up_pre * sigma * (1.0 + gate_pre * (1.0 - sigma))
            up_rate = weight * gate_pre * sigma
            parts = backward_experts(spread(grad), gate_rate, up_rate, joint, down)
            normed_grad = sum(p.astype(f32) for p in collect(parts))
            weighted = gain * normed_grad
            grad_x = (
                grad.astype(f32)
                + scale * weighted
                - x * scale * scale * scale * jnp.mean(weighted * x, axis=-1, keepdims=True)
            ).astype(bf16)
            gain_sum = gain_sum + jnp.sum(normed_grad * x * scale, axis=0)
            grads.append(grad_x)
            if number + 1 < ticks:
                ahead = shifted(grad_x, 0, 0, -1)
        if tick + 1 < ticks:
            behind = behind_next
    gain_grad = lax.psum(gain_sum, ("dp", "expert"))
    stage_range = range(stages)
    segment_out = jnp.concatenate([choose([(s, outs[m + s]) for s in stage_range]) for m in range(MICRO)])
    segment_grad = jnp.concatenate(
        [choose([(s, grads[m + stages - 1 - s]) for s in stage_range]) for m in range(MICRO)]
    )
    return (segment_out[None], segment_grad[None], gain_grad[None])


def body(tokens, cotangent, owner_ids, *rest):
    owners = lax.axis_size("dp") * lax.axis_size("expert")
    routed_densely = owners <= 2 * owner_ids.shape[2] and lax.axis_size("expert") % 2 == 0
    plan = dense_body if routed_densely else slot_body
    return plan(tokens, cotangent, owner_ids, *rest)


def solution(mesh):
    in_specs = (
        P(("dp", "expert"), None),
        P(("dp", "expert"), None),
        P("pipe", ("dp", "expert"), None),
        P("pipe", ("dp", "expert"), None),
        P("pipe", None),
        P("pipe", ("dp", "expert"), None, None),
        P("pipe", ("dp", "expert"), None, None),
        P("pipe", ("dp", "expert"), None, None),
    )
    out_specs = (
        P("pipe", ("dp", "expert"), None),
        P("pipe", ("dp", "expert"), None),
        P("pipe", None),
    )
    return jax.shard_map(body, mesh=mesh, in_specs=in_specs, out_specs=out_specs, check_vma=False)
```

```python
import jax
import jax.numpy as jnp
from jax import lax
from jax.experimental import pallas as pl
from jax.experimental.pallas import tpu as pltpu
import functools
from jax.sharding import PartitionSpec as P

MICRO = 4
LIMIT = 12 * 1024 * 1024


epsilon = 1e-06


def from_behind(value, axis, steps):
    count = lax.axis_size(axis)
    leading, last = (max(0, -steps), min(count, count - steps))
    return lax.ppermute(value, axis, [(source, source + steps) for source in range(leading, last)])


def inverse_rms(values):
    return lax.rsqrt(jnp.mean(values * values, axis=-1, keepdims=True) + epsilon)


def contract_last(left, right):
    return lax.dot_general(
        left, right, (((1,), (1,)), ((), ())), preferred_element_type=jnp.float32
    )


def route_tables(ids_part, owners, capacity):
    owner_range = jnp.arange(owners, dtype=jnp.int32)
    onehot = (ids_part[:, :, None] == owner_range[None, None, :]).astype(jnp.int32)
    member = jnp.sum(onehot, axis=1)
    position = jnp.cumsum(member, axis=0) - member
    slot_range = jnp.arange(capacity, dtype=jnp.int32)
    placed = (position[:, :, None] == slot_range[None, None, :]) & (member[:, :, None] > 0)
    placing = jnp.transpose(placed, (1, 2, 0)).astype(jnp.bfloat16)
    return (onehot.astype(jnp.float32), placing)


def gate_slots(onehot, gates_part, placing, experts_here):
    gate_pairs = gates_part.astype(jnp.float32).reshape(gates_part.shape[0], -1, experts_here)
    chosen = jnp.einsum("rjo,rjc->roc", onehot, gate_pairs)
    return jnp.einsum("okr,roc->okc", placing.astype(jnp.float32), chosen).astype(jnp.bfloat16)


def send_rows(row_block, pair_block):
    got_rows, got_pairs = (
        lax.all_to_all(row_block, ("dp", "expert"), split_axis=0, concat_axis=0, tiled=True),
        lax.all_to_all(pair_block, ("dp", "expert"), split_axis=0, concat_axis=0, tiled=True),
    )
    return (got_rows, got_pairs)


def return_rows(row_block):
    return lax.all_to_all(row_block, ("dp", "expert"), split_axis=0, concat_axis=0, tiled=True)


def send_grads(row_block):
    return lax.all_to_all(row_block, ("dp", "expert"), split_axis=0, concat_axis=0, tiled=True)


def return_grads(row_block):
    return lax.all_to_all(row_block, ("dp", "expert"), split_axis=0, concat_axis=0, tiled=True)


def expert_forward(flat_rows, flat_pairs, joint_mats, down_mats):
    hidden_width = down_mats.shape[1]
    joint_pre = jnp.dot(flat_rows, joint_mats[0], preferred_element_type=jnp.float32)
    gate_pre = joint_pre[:, :hidden_width]
    up_pre = joint_pre[:, hidden_width:]
    hidden = (jax.nn.silu(gate_pre) * up_pre).astype(jnp.bfloat16)
    projected = jnp.dot(hidden, down_mats[0], preferred_element_type=jnp.float32)
    term = flat_pairs.astype(jnp.float32) * projected
    kept_both = [joint_pre]
    return (term.astype(jnp.bfloat16), jnp.stack(kept_both))


def expert_backward(grad_rows, flat_pairs, joint_keep, joint_mats, down_mats):
    hidden_width = down_mats.shape[1]
    q_vals = contract_last(grad_rows, down_mats[0])
    gate_pre = joint_keep[0][:, :hidden_width]
    up_pre = joint_keep[0][:, hidden_width:]
    sigma = jax.nn.sigmoid(gate_pre)
    weight = flat_pairs.astype(jnp.float32)
    d_gate = (q_vals * weight * up_pre * sigma * (1.0 + gate_pre * (1.0 - sigma))).astype(
        jnp.bfloat16
    )
    d_up = (q_vals * weight * gate_pre * sigma).astype(jnp.bfloat16)
    joint_grad = jnp.concatenate([d_gate, d_up], axis=1)
    term = contract_last(joint_grad, joint_mats[0])
    return term.astype(jnp.bfloat16)


def slot_body(tokens, cotangent, owner_ids, gate_weights, norm_gain, w_gate, w_up, w_down):
    segments = lax.axis_size("pipe")
    segment_index = lax.axis_index("pipe")
    owners = lax.axis_size("dp") * lax.axis_size("expert")
    tok_rows = tokens.shape[0]
    width = tokens.shape[1]
    micro_rows = tok_rows // MICRO
    route_count = owner_ids.shape[2]
    capacity = max(2, (5 * micro_rows * route_count + 4 * owners - 1) // (4 * owners))
    slot_count = owners * capacity
    gain_row = norm_gain[0]
    joint_mats = jnp.concatenate([w_gate[0], w_up[0]], axis=2)
    down_mats = w_down[0]
    layer_ids = owner_ids[0]
    layer_gates = gate_weights[0]
    experts_here = joint_mats.shape[0]
    joint_width = joint_mats.shape[2]

    def skip_forward(operands):
        return (
            jnp.zeros((slot_count, width), jnp.bfloat16),
            jnp.zeros((experts_here, slot_count, joint_width), jnp.float32),
        )

    def run_forward(operands):
        return expert_forward(operands[0], operands[1], joint_mats, down_mats)

    def skip_backward(operands):
        return jnp.zeros((slot_count, width), jnp.bfloat16)

    def run_backward(operands):
        return expert_backward(operands[0], operands[1], operands[2], joint_mats, down_mats)

    def timing(micro):
        is_valid = (micro >= 0) & (micro < MICRO)
        slot_pick = jnp.where(is_valid, micro, MICRO)
        start_row = jnp.clip(micro, 0, MICRO - 1) * micro_rows
        return (is_valid, slot_pick, start_row)

    layer_outs = jnp.zeros((MICRO + 1, micro_rows, width), jnp.bfloat16)
    layer_ins = jnp.zeros((MICRO + 1, micro_rows, width), jnp.bfloat16)
    kept_joint = jnp.zeros((MICRO + 1, experts_here, slot_count, joint_width), jnp.float32)
    kept_pairs = jnp.zeros((MICRO + 1, slot_count, experts_here), jnp.bfloat16)
    grad_outs = jnp.zeros((MICRO + 1, micro_rows, width), jnp.bfloat16)
    gain_sum = jnp.zeros((width,), jnp.float32)
    ticks = MICRO + segments - 1
    incoming = jnp.zeros((micro_rows, width), jnp.bfloat16)
    for tick_num in range(ticks):
        forward_is_valid, forward_slot_pick, forward_start_row = timing(tick_num - segment_index)
        forward_own_part = lax.dynamic_slice_in_dim(tokens, forward_start_row, micro_rows, 0)
        forward_layer_in = jnp.where(segment_index == 0, forward_own_part, incoming)
        forward_ids_part = lax.dynamic_slice_in_dim(layer_ids, forward_start_row, micro_rows, 0)
        gates_part = lax.dynamic_slice_in_dim(layer_gates, forward_start_row, micro_rows, 0)
        forward_x_float = forward_layer_in.astype(jnp.float32)
        forward_scale = inverse_rms(forward_x_float)
        normed = (forward_x_float * forward_scale * gain_row).astype(jnp.bfloat16)
        forward_onehot, forward_placing = route_tables(forward_ids_part, owners, capacity)
        row_block = jnp.einsum(
            "okr,rd->okd", forward_placing, normed, preferred_element_type=jnp.float32
        ).astype(jnp.bfloat16)
        pair_block = gate_slots(forward_onehot, gates_part, forward_placing, experts_here)
        f_valid, f_pick, layer_in, x_float, f_placing, row_block, pair_block = (
            forward_is_valid,
            forward_slot_pick,
            forward_layer_in,
            forward_x_float,
            forward_placing,
            row_block,
            pair_block,
        )
        got_rows, got_pairs = send_rows(row_block, pair_block)
        flat_rows = got_rows.reshape(slot_count, width)
        flat_pairs = got_pairs.reshape(slot_count, experts_here)
        result, joint_pre = lax.cond(f_valid, run_forward, skip_forward, (flat_rows, flat_pairs))
        returned = return_rows(result.reshape(owners, capacity, width))
        branch = jnp.einsum("okr,okd->rd", f_placing, returned, preferred_element_type=jnp.float32)
        layer_out = (x_float + branch).astype(jnp.bfloat16)
        layer_outs = lax.dynamic_update_index_in_dim(layer_outs, layer_out, f_pick, 0)
        layer_ins = lax.dynamic_update_index_in_dim(layer_ins, layer_in, f_pick, 0)
        kept_joint = lax.dynamic_update_index_in_dim(kept_joint, joint_pre, f_pick, 0)
        kept_pairs = lax.dynamic_update_index_in_dim(kept_pairs, flat_pairs, f_pick, 0)
        if tick_num + 1 < ticks:
            incoming = from_behind(layer_out, "pipe", 1)
    incoming = jnp.zeros((micro_rows, width), jnp.bfloat16)
    for tick_num in range(ticks):
        backward_is_valid, backward_slot_pick, backward_start_row = timing(
            tick_num - (segments - 1 - segment_index)
        )
        own_part = lax.dynamic_slice_in_dim(cotangent, backward_start_row, micro_rows, 0)
        backward_grad_in = jnp.where(segment_index == segments - 1, own_part, incoming)
        ids_part = lax.dynamic_slice_in_dim(layer_ids, backward_start_row, micro_rows, 0)
        backward_layer_in = lax.dynamic_index_in_dim(
            layer_ins, backward_slot_pick, 0, keepdims=False
        )
        backward_x_float = backward_layer_in.astype(jnp.float32)
        backward_scale = inverse_rms(backward_x_float)
        _, backward_placing = route_tables(ids_part, owners, capacity)
        grad_block = jnp.einsum(
            "okr,rd->okd", backward_placing, backward_grad_in, preferred_element_type=jnp.float32
        ).astype(jnp.bfloat16)
        b_valid, b_pick, grad_in, bx_float, b_scale, b_placing, grad_block = (
            backward_is_valid,
            backward_slot_pick,
            backward_grad_in,
            backward_x_float,
            backward_scale,
            backward_placing,
            grad_block,
        )
        got_grads = send_grads(grad_block).reshape(slot_count, width)
        joint_keep = lax.dynamic_index_in_dim(kept_joint, b_pick, 0, keepdims=False)
        pair_keep = lax.dynamic_index_in_dim(kept_pairs, b_pick, 0, keepdims=False)
        owner_grad = lax.cond(
            b_valid, run_backward, skip_backward, (got_grads, pair_keep, joint_keep)
        )
        returned = return_grads(owner_grad.reshape(owners, capacity, width))
        normed_grad = jnp.einsum(
            "okr,okd->rd", b_placing, returned, preferred_element_type=jnp.float32
        )
        weighted = gain_row * normed_grad
        grad_x = (
            grad_in.astype(jnp.float32)
            + b_scale * weighted
            - bx_float
            * b_scale
            * b_scale
            * b_scale
            * jnp.mean(weighted * bx_float, axis=-1, keepdims=True)
        )
        gain_term = jnp.where(b_valid, jnp.sum(normed_grad * bx_float * b_scale, axis=0), 0.0)
        grad_bf, gain_term = (grad_x.astype(jnp.bfloat16), gain_term)
        grad_outs = lax.dynamic_update_index_in_dim(grad_outs, grad_bf, b_pick, 0)
        gain_sum = gain_sum + gain_term
        if tick_num + 1 < ticks:
            incoming = from_behind(grad_bf, "pipe", -1)
    gain_grad = lax.psum(gain_sum, ("dp", "expert"))
    segment_out = layer_outs[:MICRO].reshape(1, tok_rows, width)
    segment_grad = grad_outs[:MICRO].reshape(1, tok_rows, width)
    return (segment_out, segment_grad, gain_grad.reshape(1, width))


def swap_cores(value):
    count = lax.axis_size("expert")
    return lax.ppermute(value, "expert", [(e, e ^ 1) for e in range(count)])


def device_number(dp, pipe, expert):
    return (dp * lax.axis_size("pipe") + pipe) * lax.axis_size("expert") + expert


def shifted(value, dp_step, chip_step, pipe_step):
    dps, pipes, experts = (lax.axis_size(name) for name in ("dp", "pipe", "expert"))
    pairs = []
    for dp in range(dps):
        for pipe in range(pipes):
            for expert in range(experts):
                target = device_number(
                    (dp + dp_step) % dps,
                    (pipe + pipe_step) % pipes,
                    (expert + 2 * chip_step) % experts,
                )
                pairs.append((device_number(dp, pipe, expert), target))
    return lax.ppermute(value, ("dp", "pipe", "expert"), pairs)


def chip_steps():
    dps, chips = lax.axis_size("dp"), lax.axis_size("expert") // 2
    steps = [(d, c) for d in range(dps) for c in range(chips)]
    return sorted(steps[1:], key=lambda step: -(step[0] + step[1]))


def spread(rows):
    return [rows] + [shifted(rows, d, c, 0) for d, c in chip_steps()]


def collect(blocks):
    dps, chips = lax.axis_size("dp"), lax.axis_size("expert") // 2
    back = [shifted(block, -d % dps, -c % chips, 0) for block, (d, c) in zip(blocks[1:], chip_steps())]
    return [blocks[0]] + back


VMEM = pl.BlockSpec(memory_space=pltpu.VMEM)
CHUNK = 256


def in_vmem(kernel, outs, scratch, flops, *operands):
    moved = sum(a.size * a.dtype.itemsize for a in [*outs, *operands])
    return pl.pallas_call(
        kernel,
        out_shape=outs,
        in_specs=[VMEM] * len(operands),
        out_specs=[VMEM] * len(outs),
        scratch_shapes=scratch,
        compiler_params=pltpu.CompilerParams(vmem_limit_bytes=LIMIT),
        cost_estimate=pl.CostEstimate(flops=flops, bytes_accessed=moved, transcendentals=0),
    )(*operands)


def transpose_kernel(axis, *refs):
    start = 0
    for ref in refs[:-1]:
        size = ref.shape[1 - axis]
        window = (slice(start, start + size), slice(None))
        refs[-1][window if axis == 0 else window[::-1]] = ref[...].T
        start += size


def transposed(axis, *parts):
    shape = [parts[0].shape[1], parts[0].shape[0]]
    shape[axis] = sum(part.shape[1 - axis] for part in parts)
    outs = [jax.ShapeDtypeStruct(tuple(shape), parts[0].dtype)]
    return in_vmem(functools.partial(transpose_kernel, axis), outs, [], 0, *parts)[0]


def forward_kernel(blocks, *refs):
    row_refs, refs = refs[:blocks], refs[blocks:]
    pair_ref, gain_ref, *weight_refs = refs[:6]
    pre_ref, flat_ref, own_ref, *part_refs, hidden = refs[6:]
    rows, width = row_refs[0].shape
    ff = weight_refs[2].shape[0]
    gain = gain_ref[...]
    for k, row_ref in enumerate(row_refs):
        x = row_ref[...].astype(jnp.float32)
        flat_ref[k * rows:(k + 1) * rows, :] = (x * inverse_rms(x) * gain).astype(jnp.bfloat16)
    for e in range(2):
        base = 2 * ff * e
        for start in range(0, 2 * ff, CHUNK):
            pre_ref[:, base + start:base + start + CHUNK] = jnp.dot(
                flat_ref[...], weight_refs[e][:, start:start + CHUNK], preferred_element_type=jnp.float32
            )
        gate_pre = pre_ref[:, base:base + ff]
        up_pre = pre_ref[:, base + ff:base + 2 * ff]
        hidden[:, e * ff:(e + 1) * ff] = (jax.nn.silu(gate_pre) * up_pre * pair_ref[:, e:e + 1]).astype(jnp.bfloat16)
    for start in range(0, width, CHUNK):
        columns = slice(start, start + CHUNK)
        partial = sum(
            jnp.dot(hidden[:, e * ff:(e + 1) * ff], weight_refs[2 + e][:, columns], preferred_element_type=jnp.float32)
            for e in range(2)
        )
        own_ref[:, columns] = row_refs[0][:, columns].astype(jnp.float32) + partial[:rows]
        for k, part_ref in enumerate(part_refs):
            part_ref[:, columns] = partial[(k + 1) * rows:(k + 2) * rows].astype(jnp.bfloat16)


def backward_kernel(blocks, *refs):
    row_refs, refs = refs[:blocks], refs[blocks:]
    gate_ref, up_ref, normed_ref, joint_ref, down_ref = refs[:5]
    gain_ref, own_ref, *part_refs, flat, q, hidden = refs[5:]
    rows, width = row_refs[0].shape
    both = down_ref.shape[1]
    ff = both // 2
    for k, row_ref in enumerate(row_refs):
        flat[k * rows:(k + 1) * rows, :] = row_ref[...]
    for start in range(0, both, CHUNK):
        columns = slice(start, start + CHUNK)
        q[:, columns] = jnp.dot(flat[...], down_ref[:, columns], preferred_element_type=jnp.float32)
    for e in range(2):
        columns = slice(e * ff, (e + 1) * ff)
        hidden[:, 2 * e * ff:(2 * e + 1) * ff] = (q[:, columns] * gate_ref[:, columns]).astype(jnp.bfloat16)
        hidden[:, (2 * e + 1) * ff:(2 * e + 2) * ff] = (q[:, columns] * up_ref[:, columns]).astype(jnp.bfloat16)
    for start in range(0, width, CHUNK):
        columns = slice(start, start + CHUNK)
        partial = jnp.dot(hidden[...], joint_ref[:, columns], preferred_element_type=jnp.float32)
        gain_ref[:, columns] = jnp.sum(partial * normed_ref[:, columns].astype(jnp.float32), axis=0, keepdims=True)
        own_ref[:, columns] = partial[:rows]
        for k, part_ref in enumerate(part_refs):
            part_ref[:, columns] = partial[(k + 1) * rows:(k + 2) * rows].astype(jnp.bfloat16)


def forward_experts(row_blocks, pair, gain, weights):
    blocks, (rows, width) = len(row_blocks), row_blocks[0].shape
    total, ff = blocks * rows, weights[2].shape[0]
    outs = [
        jax.ShapeDtypeStruct((total, 4 * ff), jnp.float32),
        jax.ShapeDtypeStruct((total, width), jnp.bfloat16),
        jax.ShapeDtypeStruct((rows, width), jnp.float32),
    ]
    outs += [jax.ShapeDtypeStruct((rows, width), jnp.bfloat16)] * (blocks - 1)
    scratch = [pltpu.VMEM((total, 2 * ff), jnp.bfloat16)]
    kernel = functools.partial(forward_kernel, blocks)
    flops = 12 * total * width * ff
    pre, normed, *parts = in_vmem(kernel, outs, scratch, flops, *row_blocks, pair, gain, *weights)
    return pre, normed, parts


def backward_experts(row_blocks, gate_rate, up_rate, normed, weights):
    blocks, (rows, width) = len(row_blocks), row_blocks[0].shape
    total, both = normed.shape[0], gate_rate.shape[1]
    outs = [jax.ShapeDtypeStruct((1, width), jnp.float32), jax.ShapeDtypeStruct((rows, width), jnp.float32)]
    outs += [jax.ShapeDtypeStruct((rows, width), jnp.bfloat16)] * (blocks - 1)
    scratch = [
        pltpu.VMEM((total, width), jnp.bfloat16),
        pltpu.VMEM((total, both), jnp.float32),
        pltpu.VMEM((total, 2 * both), jnp.bfloat16),
    ]
    kernel = functools.partial(backward_kernel, blocks)
    flops = 6 * total * width * both
    gained, *parts = in_vmem(kernel, outs, scratch, flops, *row_blocks, gate_rate, up_rate, normed, *weights)
    return gained, parts


def summed_over_owners(value):
    dps, chips = lax.axis_size("dp"), lax.axis_size("expert") // 2
    value = value + swap_cores(value)
    total = value
    for step in range(1, chips):
        total = total + shifted(value, 0, step, 0)
    value = total
    for step in range(1, dps):
        total = total + shifted(value, step, 0, 0)
    return total


def dense_body(tokens, cotangent, owner_ids, gate_weights, norm_gain, w_gate, w_up, w_down):
    f32, bf16 = jnp.float32, jnp.bfloat16
    stages = lax.axis_size("pipe")
    stage = lax.axis_index("pipe")
    owners = lax.axis_size("dp") * lax.axis_size("expert")
    me = lax.axis_index("dp") * lax.axis_size("expert") + lax.axis_index("expert")
    tok_rows, width = tokens.shape
    rows = tok_rows // MICRO
    ff = w_down.shape[2]
    gain = norm_gain[0][None, :]
    ticks = MICRO + stages - 1

    joint = jnp.concatenate([w_gate[0, 0], w_up[0, 0]], axis=1)
    down = w_down[0, 0]
    pair_joint, pair_down = swap_cores(joint), swap_cores(down)
    forward_weights = (joint, pair_joint, down, pair_down)
    backward_weights = (transposed(0, joint, pair_joint), transposed(1, down, pair_down))

    owner_range = jnp.arange(owners, dtype=jnp.int32)
    onehot = owner_ids[0][:, :, None] == owner_range
    table = jnp.sum(jnp.where(onehot, gate_weights[0].astype(f32)[:, :, None], 0.0), axis=1).astype(bf16)
    tables = jnp.stack(spread(table)).astype(f32)
    mine = jnp.sum(jnp.where(owner_range == me, tables, 0.0), axis=2)
    theirs = jnp.sum(jnp.where(owner_range == (me ^ 1), tables, 0.0), axis=2)
    pair = jnp.stack([mine, theirs], axis=-1)
    blocks = pair.shape[0]
    pair = pair.reshape(blocks, MICRO, rows, 2).transpose(1, 0, 2, 3).reshape(MICRO, blocks * rows, 2)
    padded = jnp.pad(pair, ((stages - 1, stages - 1), (0, 0), (0, 0)))
    forward_pairs = lax.dynamic_slice_in_dim(padded, stages - 1 - stage, ticks, 0)
    backward_pairs = lax.dynamic_slice_in_dim(padded, stage, ticks, 0)

    def choose(options):
        found = None
        for s, value in options:
            found = value if found is None else jnp.where(stage == s, value, found)
        return found

    def pick(saved, tick):
        first = tick - (2 * stages - 1)
        return choose([(s, saved[first + 2 * s]) for s in range(stages) if 0 <= first + 2 * s < min(ticks, tick)])

    pres, normeds, ins, outs, grads = [], [], [], [], []
    gain_sum = jnp.zeros((1, width), f32)
    behind = ahead = None
    for tick in range(MICRO + 2 * stages - 1):
        if tick < ticks:
            if tick == 0:
                here = tokens[:rows]
            elif tick < MICRO:
                here = jnp.where(stage == 0, tokens[tick * rows:(tick + 1) * rows], behind)
            else:
                here = behind
            pre, normed, parts = forward_experts(spread(here), forward_pairs[tick], gain, forward_weights)
            out = sum(p.astype(f32) for p in collect(parts)).astype(bf16)
            pres.append(pre)
            normeds.append(normed)
            ins.append(here)
            outs.append(out)
            if tick + 1 < ticks:
                behind_next = shifted(out, 0, 0, 1)
        if tick >= stages:
            number = tick - stages
            if number == 0:
                grad = cotangent[:rows]
            elif number < MICRO:
                grad = jnp.where(stage == stages - 1, cotangent[number * rows:(number + 1) * rows], ahead)
            else:
                grad = ahead
            x = pick(ins, tick).astype(f32)
            scale = inverse_rms(x)
            pre = pick(pres, tick)
            gate_pre = jnp.concatenate([pre[:, :ff], pre[:, 2 * ff:3 * ff]], axis=1)
            up_pre = jnp.concatenate([pre[:, ff:2 * ff], pre[:, 3 * ff:]], axis=1)
            sigma = jax.nn.sigmoid(gate_pre)
            weight = jnp.repeat(backward_pairs[number], ff, axis=1)
            gate_rate = weight * up_pre * sigma * (1.0 + gate_pre * (1.0 - sigma))
            up_rate = weight * gate_pre * sigma
            gained, parts = backward_experts(spread(grad), gate_rate, up_rate, pick(normeds, tick), backward_weights)
            normed_grad = sum(p.astype(f32) for p in collect(parts))
            weighted = gain * normed_grad
            grad_x = (
                grad.astype(f32)
                + scale * weighted
                - x * scale * scale * scale * jnp.mean(weighted * x, axis=-1, keepdims=True)
            ).astype(bf16)
            gain_sum = gain_sum + gained
            grads.append(grad_x)
            if number + 1 < ticks:
                ahead = shifted(grad_x, 0, 0, -1)
        if tick + 1 < ticks:
            behind = behind_next
    gain_grad = summed_over_owners(gain_sum) / gain
    stage_range = range(stages)
    segment_out = jnp.concatenate([choose([(s, outs[m + s]) for s in stage_range]) for m in range(MICRO)])
    segment_grad = jnp.concatenate(
        [choose([(s, grads[m + stages - 1 - s]) for s in stage_range]) for m in range(MICRO)]
    )
    return (segment_out[None], segment_grad[None], gain_grad)


def body(tokens, cotangent, owner_ids, *rest):
    owners = lax.axis_size("dp") * lax.axis_size("expert")
    routed_densely = owners <= 2 * owner_ids.shape[2] and lax.axis_size("expert") % 2 == 0
    plan = dense_body if routed_densely else slot_body
    return plan(tokens, cotangent, owner_ids, *rest)


def solution(mesh):
    in_specs = (
        P(("dp", "expert"), None),
        P(("dp", "expert"), None),
        P("pipe", ("dp", "expert"), None),
        P("pipe", ("dp", "expert"), None),
        P("pipe", None),
        P("pipe", ("dp", "expert"), None, None),
        P("pipe", ("dp", "expert"), None, None),
        P("pipe", ("dp", "expert"), None, None),
    )
    out_specs = (
        P("pipe", ("dp", "expert"), None),
        P("pipe", ("dp", "expert"), None),
        P("pipe", None),
    )
    return jax.shard_map(body, mesh=mesh, in_specs=in_specs, out_specs=out_specs, check_vma=False)
```

```python
import jax
import jax.numpy as jnp
from jax import lax
from jax.experimental import pallas as pl
from jax.experimental.pallas import tpu as pltpu
import functools
import math
from jax.sharding import PartitionSpec as P

MICRO = 4
LIMIT = 12 * 1024 * 1024


epsilon = 1e-06


def from_behind(value, axis, steps):
    count = lax.axis_size(axis)
    leading, last = (max(0, -steps), min(count, count - steps))
    return lax.ppermute(value, axis, [(source, source + steps) for source in range(leading, last)])


def inverse_rms(values):
    return lax.rsqrt(jnp.mean(values * values, axis=-1, keepdims=True) + epsilon)


def contract_last(left, right):
    return lax.dot_general(
        left, right, (((1,), (1,)), ((), ())), preferred_element_type=jnp.float32
    )


def route_tables(ids_part, owners, capacity):
    owner_range = jnp.arange(owners, dtype=jnp.int32)
    onehot = (ids_part[:, :, None] == owner_range[None, None, :]).astype(jnp.int32)
    member = jnp.sum(onehot, axis=1)
    position = jnp.cumsum(member, axis=0) - member
    slot_range = jnp.arange(capacity, dtype=jnp.int32)
    placed = (position[:, :, None] == slot_range[None, None, :]) & (member[:, :, None] > 0)
    placing = jnp.transpose(placed, (1, 2, 0)).astype(jnp.bfloat16)
    return (onehot.astype(jnp.float32), placing)


def gate_slots(onehot, gates_part, placing, experts_here):
    gate_pairs = gates_part.astype(jnp.float32).reshape(gates_part.shape[0], -1, experts_here)
    chosen = jnp.einsum("rjo,rjc->roc", onehot, gate_pairs)
    return jnp.einsum("okr,roc->okc", placing.astype(jnp.float32), chosen).astype(jnp.bfloat16)


def send_rows(row_block, pair_block):
    got_rows, got_pairs = (
        lax.all_to_all(row_block, ("dp", "expert"), split_axis=0, concat_axis=0, tiled=True),
        lax.all_to_all(pair_block, ("dp", "expert"), split_axis=0, concat_axis=0, tiled=True),
    )
    return (got_rows, got_pairs)


def return_rows(row_block):
    return lax.all_to_all(row_block, ("dp", "expert"), split_axis=0, concat_axis=0, tiled=True)


def send_grads(row_block):
    return lax.all_to_all(row_block, ("dp", "expert"), split_axis=0, concat_axis=0, tiled=True)


def return_grads(row_block):
    return lax.all_to_all(row_block, ("dp", "expert"), split_axis=0, concat_axis=0, tiled=True)


def expert_forward(flat_rows, flat_pairs, joint_mats, down_mats):
    hidden_width = down_mats.shape[1]
    joint_pre = jnp.dot(flat_rows, joint_mats[0], preferred_element_type=jnp.float32)
    gate_pre = joint_pre[:, :hidden_width]
    up_pre = joint_pre[:, hidden_width:]
    hidden = (jax.nn.silu(gate_pre) * up_pre).astype(jnp.bfloat16)
    projected = jnp.dot(hidden, down_mats[0], preferred_element_type=jnp.float32)
    term = flat_pairs.astype(jnp.float32) * projected
    kept_both = [joint_pre]
    return (term.astype(jnp.bfloat16), jnp.stack(kept_both))


def expert_backward(grad_rows, flat_pairs, joint_keep, joint_mats, down_mats):
    hidden_width = down_mats.shape[1]
    q_vals = contract_last(grad_rows, down_mats[0])
    gate_pre = joint_keep[0][:, :hidden_width]
    up_pre = joint_keep[0][:, hidden_width:]
    sigma = jax.nn.sigmoid(gate_pre)
    weight = flat_pairs.astype(jnp.float32)
    d_gate = (q_vals * weight * up_pre * sigma * (1.0 + gate_pre * (1.0 - sigma))).astype(
        jnp.bfloat16
    )
    d_up = (q_vals * weight * gate_pre * sigma).astype(jnp.bfloat16)
    joint_grad = jnp.concatenate([d_gate, d_up], axis=1)
    term = contract_last(joint_grad, joint_mats[0])
    return term.astype(jnp.bfloat16)


def slot_body(tokens, cotangent, owner_ids, gate_weights, norm_gain, w_gate, w_up, w_down):
    segments = lax.axis_size("pipe")
    segment_index = lax.axis_index("pipe")
    owners = lax.axis_size("dp") * lax.axis_size("expert")
    tok_rows = tokens.shape[0]
    width = tokens.shape[1]
    micro_rows = tok_rows // MICRO
    route_count = owner_ids.shape[2]
    capacity = max(2, (5 * micro_rows * route_count + 4 * owners - 1) // (4 * owners))
    slot_count = owners * capacity
    gain_row = norm_gain[0]
    joint_mats = jnp.concatenate([w_gate[0], w_up[0]], axis=2)
    down_mats = w_down[0]
    layer_ids = owner_ids[0]
    layer_gates = gate_weights[0]
    experts_here = joint_mats.shape[0]
    joint_width = joint_mats.shape[2]

    def skip_forward(operands):
        return (
            jnp.zeros((slot_count, width), jnp.bfloat16),
            jnp.zeros((experts_here, slot_count, joint_width), jnp.float32),
        )

    def run_forward(operands):
        return expert_forward(operands[0], operands[1], joint_mats, down_mats)

    def skip_backward(operands):
        return jnp.zeros((slot_count, width), jnp.bfloat16)

    def run_backward(operands):
        return expert_backward(operands[0], operands[1], operands[2], joint_mats, down_mats)

    def timing(micro):
        is_valid = (micro >= 0) & (micro < MICRO)
        slot_pick = jnp.where(is_valid, micro, MICRO)
        start_row = jnp.clip(micro, 0, MICRO - 1) * micro_rows
        return (is_valid, slot_pick, start_row)

    layer_outs = jnp.zeros((MICRO + 1, micro_rows, width), jnp.bfloat16)
    layer_ins = jnp.zeros((MICRO + 1, micro_rows, width), jnp.bfloat16)
    kept_joint = jnp.zeros((MICRO + 1, experts_here, slot_count, joint_width), jnp.float32)
    kept_pairs = jnp.zeros((MICRO + 1, slot_count, experts_here), jnp.bfloat16)
    grad_outs = jnp.zeros((MICRO + 1, micro_rows, width), jnp.bfloat16)
    gain_sum = jnp.zeros((width,), jnp.float32)
    ticks = MICRO + segments - 1
    incoming = jnp.zeros((micro_rows, width), jnp.bfloat16)
    for tick_num in range(ticks):
        forward_is_valid, forward_slot_pick, forward_start_row = timing(tick_num - segment_index)
        forward_own_part = lax.dynamic_slice_in_dim(tokens, forward_start_row, micro_rows, 0)
        forward_layer_in = jnp.where(segment_index == 0, forward_own_part, incoming)
        forward_ids_part = lax.dynamic_slice_in_dim(layer_ids, forward_start_row, micro_rows, 0)
        gates_part = lax.dynamic_slice_in_dim(layer_gates, forward_start_row, micro_rows, 0)
        forward_x_float = forward_layer_in.astype(jnp.float32)
        forward_scale = inverse_rms(forward_x_float)
        normed = (forward_x_float * forward_scale * gain_row).astype(jnp.bfloat16)
        forward_onehot, forward_placing = route_tables(forward_ids_part, owners, capacity)
        row_block = jnp.einsum(
            "okr,rd->okd", forward_placing, normed, preferred_element_type=jnp.float32
        ).astype(jnp.bfloat16)
        pair_block = gate_slots(forward_onehot, gates_part, forward_placing, experts_here)
        f_valid, f_pick, layer_in, x_float, f_placing, row_block, pair_block = (
            forward_is_valid,
            forward_slot_pick,
            forward_layer_in,
            forward_x_float,
            forward_placing,
            row_block,
            pair_block,
        )
        got_rows, got_pairs = send_rows(row_block, pair_block)
        flat_rows = got_rows.reshape(slot_count, width)
        flat_pairs = got_pairs.reshape(slot_count, experts_here)
        result, joint_pre = lax.cond(f_valid, run_forward, skip_forward, (flat_rows, flat_pairs))
        returned = return_rows(result.reshape(owners, capacity, width))
        branch = jnp.einsum("okr,okd->rd", f_placing, returned, preferred_element_type=jnp.float32)
        layer_out = (x_float + branch).astype(jnp.bfloat16)
        layer_outs = lax.dynamic_update_index_in_dim(layer_outs, layer_out, f_pick, 0)
        layer_ins = lax.dynamic_update_index_in_dim(layer_ins, layer_in, f_pick, 0)
        kept_joint = lax.dynamic_update_index_in_dim(kept_joint, joint_pre, f_pick, 0)
        kept_pairs = lax.dynamic_update_index_in_dim(kept_pairs, flat_pairs, f_pick, 0)
        if tick_num + 1 < ticks:
            incoming = from_behind(layer_out, "pipe", 1)
    incoming = jnp.zeros((micro_rows, width), jnp.bfloat16)
    for tick_num in range(ticks):
        backward_is_valid, backward_slot_pick, backward_start_row = timing(
            tick_num - (segments - 1 - segment_index)
        )
        own_part = lax.dynamic_slice_in_dim(cotangent, backward_start_row, micro_rows, 0)
        backward_grad_in = jnp.where(segment_index == segments - 1, own_part, incoming)
        ids_part = lax.dynamic_slice_in_dim(layer_ids, backward_start_row, micro_rows, 0)
        backward_layer_in = lax.dynamic_index_in_dim(
            layer_ins, backward_slot_pick, 0, keepdims=False
        )
        backward_x_float = backward_layer_in.astype(jnp.float32)
        backward_scale = inverse_rms(backward_x_float)
        _, backward_placing = route_tables(ids_part, owners, capacity)
        grad_block = jnp.einsum(
            "okr,rd->okd", backward_placing, backward_grad_in, preferred_element_type=jnp.float32
        ).astype(jnp.bfloat16)
        b_valid, b_pick, grad_in, bx_float, b_scale, b_placing, grad_block = (
            backward_is_valid,
            backward_slot_pick,
            backward_grad_in,
            backward_x_float,
            backward_scale,
            backward_placing,
            grad_block,
        )
        got_grads = send_grads(grad_block).reshape(slot_count, width)
        joint_keep = lax.dynamic_index_in_dim(kept_joint, b_pick, 0, keepdims=False)
        pair_keep = lax.dynamic_index_in_dim(kept_pairs, b_pick, 0, keepdims=False)
        owner_grad = lax.cond(
            b_valid, run_backward, skip_backward, (got_grads, pair_keep, joint_keep)
        )
        returned = return_grads(owner_grad.reshape(owners, capacity, width))
        normed_grad = jnp.einsum(
            "okr,okd->rd", b_placing, returned, preferred_element_type=jnp.float32
        )
        weighted = gain_row * normed_grad
        grad_x = (
            grad_in.astype(jnp.float32)
            + b_scale * weighted
            - bx_float
            * b_scale
            * b_scale
            * b_scale
            * jnp.mean(weighted * bx_float, axis=-1, keepdims=True)
        )
        gain_term = jnp.where(b_valid, jnp.sum(normed_grad * bx_float * b_scale, axis=0), 0.0)
        grad_bf, gain_term = (grad_x.astype(jnp.bfloat16), gain_term)
        grad_outs = lax.dynamic_update_index_in_dim(grad_outs, grad_bf, b_pick, 0)
        gain_sum = gain_sum + gain_term
        if tick_num + 1 < ticks:
            incoming = from_behind(grad_bf, "pipe", -1)
    gain_grad = lax.psum(gain_sum, ("dp", "expert"))
    segment_out = layer_outs[:MICRO].reshape(1, tok_rows, width)
    segment_grad = grad_outs[:MICRO].reshape(1, tok_rows, width)
    return (segment_out, segment_grad, gain_grad.reshape(1, width))


def swap_cores(value):
    count = lax.axis_size("expert")
    return lax.ppermute(value, "expert", [(e, e ^ 1) for e in range(count)])


def device_number(dp, pipe, expert):
    return (dp * lax.axis_size("pipe") + pipe) * lax.axis_size("expert") + expert


def shifted(value, dp_step, chip_step, pipe_step):
    dps, pipes, experts = (lax.axis_size(name) for name in ("dp", "pipe", "expert"))
    pairs = []
    for dp in range(dps):
        for pipe in range(pipes):
            for expert in range(experts):
                target = device_number(
                    (dp + dp_step) % dps,
                    (pipe + pipe_step) % pipes,
                    (expert + 2 * chip_step) % experts,
                )
                pairs.append((device_number(dp, pipe, expert), target))
    return lax.ppermute(value, ("dp", "pipe", "expert"), pairs)


def chip_steps():
    dps, chips = lax.axis_size("dp"), lax.axis_size("expert") // 2
    steps = [(d, c) for d in range(dps) for c in range(chips)]
    return sorted(steps[1:], key=lambda step: -(step[0] + step[1]))


def spread(rows):
    return [rows] + [shifted(rows, d, c, 0) for d, c in chip_steps()]


def collect(blocks):
    dps, chips = lax.axis_size("dp"), lax.axis_size("expert") // 2
    back = [shifted(block, -d % dps, -c % chips, 0) for block, (d, c) in zip(blocks[1:], chip_steps())]
    return [blocks[0]] + back


VMEM = pl.BlockSpec(memory_space=pltpu.VMEM)
CHUNK = 256


def in_vmem(kernel, outs, scratch, flops, *operands, specs=None):
    moved = sum(math.prod(a.shape) * a.dtype.itemsize for a in [*outs, *operands])
    return pl.pallas_call(
        kernel,
        out_shape=outs,
        in_specs=specs or [VMEM] * len(operands),
        out_specs=[VMEM] * len(outs),
        scratch_shapes=scratch,
        compiler_params=pltpu.CompilerParams(vmem_limit_bytes=LIMIT),
        cost_estimate=pl.CostEstimate(flops=flops, bytes_accessed=moved, transcendentals=0),
    )(*operands)


def load_kernel(gate_ref, up_ref, down_in, joint_ref, down_ref, sems):
    ff = gate_ref.shape[1]
    copies = [
        pltpu.make_async_copy(gate_ref, joint_ref.at[:, :ff], sems.at[0]),
        pltpu.make_async_copy(up_ref, joint_ref.at[:, ff:], sems.at[1]),
        pltpu.make_async_copy(down_in, down_ref, sems.at[2]),
    ]
    for copy in copies:
        copy.start()
    for copy in copies:
        copy.wait()


def loaded(gate, up, down):
    outs = [pltpu.VMEM((gate.shape[0], 2 * gate.shape[1]), gate.dtype), pltpu.VMEM(down.shape, down.dtype)]
    specs = [pl.BlockSpec(memory_space=pl.ANY)] * 3
    return in_vmem(load_kernel, outs, [pltpu.SemaphoreType.DMA((3,))], 0, gate, up, down, specs=specs)


def stage_kernel(out_ref):
    out_ref[...] = jnp.full(out_ref.shape, lax.axis_index("pipe"), jnp.int32)


def turn_kernel(in_ref, out_ref):
    out_ref[...] = in_ref[...].T


def turned(part):
    outs = [pltpu.VMEM(part.shape[::-1], part.dtype)]
    return in_vmem(turn_kernel, outs, [], 0, part)[0]


def owner_number():
    return lax.axis_index("dp") * lax.axis_size("expert") + lax.axis_index("expert")


def forward_kernel(blocks, tick, *refs):
    row_refs, table_refs, refs = refs[:blocks], refs[blocks:2 * blocks], refs[2 * blocks:]
    gain_ref, *weight_refs = refs[:5]
    rate_ref, flat_ref, own_ref, *part_refs, pre, hidden = refs[5:]
    rows, width = row_refs[0].shape
    ff = weight_refs[2].shape[0]
    gain = gain_ref[...]
    for k, row_ref in enumerate(row_refs):
        x = row_ref[...].astype(jnp.float32)
        flat_ref[k * rows:(k + 1) * rows, :] = (x * inverse_rms(x) * gain).astype(jnp.bfloat16)
    micro = tick - lax.axis_index("pipe")
    is_valid = (micro >= 0) & (micro < MICRO)
    first = pl.multiple_of(jnp.clip(micro, 0, MICRO - 1) * rows, rows)
    routed = jnp.concatenate([ref[pl.ds(first, rows), :] for ref in table_refs], axis=0).astype(jnp.float32)
    number = lax.broadcasted_iota(jnp.int32, routed.shape, 1)
    me = owner_number()
    for e, owner in enumerate((me, me ^ 1)):
        weight = jnp.sum(jnp.where((number == owner) & is_valid, routed, 0.0), axis=1, keepdims=True)
        for start in range(0, 2 * ff, CHUNK):
            pre[:, start:start + CHUNK] = jnp.dot(
                flat_ref[...], weight_refs[e][:, start:start + CHUNK], preferred_element_type=jnp.float32
            )
        gate_pre, up_pre = pre[:, :ff], pre[:, ff:]
        sigma = jax.nn.sigmoid(gate_pre)
        up_rate = weight * gate_pre * sigma
        hidden[:, e * ff:(e + 1) * ff] = (up_rate * up_pre).astype(jnp.bfloat16)
        rate_ref[:, 2 * e * ff:(2 * e + 1) * ff] = weight * up_pre * sigma * (1.0 + gate_pre * (1.0 - sigma))
        rate_ref[:, (2 * e + 1) * ff:(2 * e + 2) * ff] = up_rate
    for start in range(0, width, CHUNK):
        columns = slice(start, start + CHUNK)
        partial = sum(
            jnp.dot(hidden[:, e * ff:(e + 1) * ff], weight_refs[2 + e][:, columns], preferred_element_type=jnp.float32)
            for e in range(2)
        )
        own_ref[:, columns] = row_refs[0][:, columns].astype(jnp.float32) + partial[:rows]
        for k, part_ref in enumerate(part_refs):
            part_ref[:, columns] = partial[(k + 1) * rows:(k + 2) * rows].astype(jnp.bfloat16)


def backward_kernel(blocks, tick, picks, saves, *refs):
    row_refs, refs = refs[:blocks], refs[blocks:]
    rate_refs, normed_refs, refs = refs[:saves], refs[saves:2 * saves], refs[2 * saves:]
    weight_refs, (gain_ref, own_ref, *part_refs, flat, rate, normed, hidden, sems) = refs[:4], refs[4:]
    rows, width = row_refs[0].shape
    ff = weight_refs[2].shape[1]
    stage = lax.axis_index("pipe")

    def copies(at):
        return (
            pltpu.make_async_copy(rate_refs[at], rate, sems.at[0]),
            pltpu.make_async_copy(normed_refs[at], normed, sems.at[1]),
        )

    for at in range(saves):
        holders = [s for s, picked in enumerate(picks) if picked == at]

        @pl.when(functools.reduce(jnp.logical_or, [stage == s for s in holders]))
        def _():
            for copy in copies(at):
                copy.start()

    for k, row_ref in enumerate(row_refs):
        flat[k * rows:(k + 1) * rows, :] = row_ref[...]
    micro = tick - (2 * len(picks) - 1) + stage
    kept = jnp.where((micro >= 0) & (micro < MICRO), 1.0, 0.0)
    for e in range(2):
        q = jnp.dot(flat[...], weight_refs[2 + e][...], preferred_element_type=jnp.float32) * kept
        if e == 0:
            for copy in copies(0):
                copy.wait()
        for half in range(2):
            columns = slice((2 * e + half) * ff, (2 * e + half + 1) * ff)
            hidden[:, columns] = (q * rate[:, columns]).astype(jnp.bfloat16)
    for start in range(0, width, CHUNK):
        columns = slice(start, start + CHUNK)
        partial = sum(
            jnp.dot(
                hidden[:, 2 * e * ff:(2 * e + 2) * ff], weight_refs[e][:, columns], preferred_element_type=jnp.float32
            )
            for e in range(2)
        )
        gain_ref[:, columns] = jnp.sum(partial * normed[:, columns].astype(jnp.float32), axis=0, keepdims=True)
        own_ref[:, columns] = partial[:rows]
        for k, part_ref in enumerate(part_refs):
            part_ref[:, columns] = partial[(k + 1) * rows:(k + 2) * rows].astype(jnp.bfloat16)


def forward_experts(tick, row_blocks, tables, gain, weights):
    blocks, (rows, width) = len(row_blocks), row_blocks[0].shape
    total, ff = blocks * rows, weights[2].shape[0]
    outs = [
        jax.ShapeDtypeStruct((total, 4 * ff), jnp.float32),
        jax.ShapeDtypeStruct((total, width), jnp.bfloat16),
        jax.ShapeDtypeStruct((rows, width), jnp.float32),
    ]
    outs += [jax.ShapeDtypeStruct((rows, width), jnp.bfloat16)] * (blocks - 1)
    scratch = [pltpu.VMEM((total, 2 * ff), jnp.float32), pltpu.VMEM((total, 2 * ff), jnp.bfloat16)]
    kernel = functools.partial(forward_kernel, blocks, tick)
    flops = 12 * total * width * ff
    rate, normed, *parts = in_vmem(kernel, outs, scratch, flops, *row_blocks, *tables, gain, *weights)
    return rate, normed, parts


def backward_experts(tick, picks, row_blocks, rates, normeds, weights):
    blocks, (rows, width) = len(row_blocks), row_blocks[0].shape
    total, wide = rates[0].shape
    outs = [jax.ShapeDtypeStruct((1, width), jnp.float32), jax.ShapeDtypeStruct((rows, width), jnp.float32)]
    outs += [jax.ShapeDtypeStruct((rows, width), jnp.bfloat16)] * (blocks - 1)
    scratch = [
        pltpu.VMEM((total, width), jnp.bfloat16),
        pltpu.VMEM((total, wide), jnp.float32),
        pltpu.VMEM((total, width), jnp.bfloat16),
        pltpu.VMEM((total, wide), jnp.bfloat16),
        pltpu.SemaphoreType.DMA((2,)),
    ]
    used = sorted(set(picks))
    kernel = functools.partial(backward_kernel, blocks, tick, [used.index(at) for at in picks], len(used))
    anywhere = pl.BlockSpec(memory_space=pl.ANY)
    specs = [VMEM] * blocks + [anywhere] * (2 * len(used)) + [VMEM] * 4
    saved = [rates[at] for at in used] + [normeds[at] for at in used]
    flops = 3 * total * width * wide
    gained, *parts = in_vmem(kernel, outs, scratch, flops, *row_blocks, *saved, *weights, specs=specs)
    return gained, parts


def summed_over_owners(value):
    dps, chips = lax.axis_size("dp"), lax.axis_size("expert") // 2
    value = value + swap_cores(value)
    total = value
    for step in range(1, chips):
        total = total + shifted(value, 0, step, 0)
    value = total
    for step in range(1, dps):
        total = total + shifted(value, step, 0, 0)
    return total


def dense_body(tokens, cotangent, owner_ids, gate_weights, norm_gain, w_gate, w_up, w_down):
    f32, bf16 = jnp.float32, jnp.bfloat16
    stages = lax.axis_size("pipe")
    owners = lax.axis_size("dp") * lax.axis_size("expert")
    tok_rows, width = tokens.shape
    rows = tok_rows // MICRO
    gain = norm_gain[0][None, :]
    ticks = MICRO + stages - 1
    stage = in_vmem(stage_kernel, [jax.ShapeDtypeStruct((1, width), jnp.int32)], [], 0)[0]

    own = [w[0, 0] for w in (w_gate, w_up, w_down)]
    theirs = [swap_cores(w) for w in own]
    joint, down = loaded(*own)
    pair_joint, pair_down = loaded(*theirs)
    forward_weights = (joint, pair_joint, down, pair_down)
    backward_weights = []
    for number, part in enumerate(forward_weights):
        backward_weights.append(turned(part))

    onehot = owner_ids[0][:, :, None] == jnp.arange(owners, dtype=jnp.int32)
    table = jnp.sum(jnp.where(onehot, gate_weights[0].astype(f32)[:, :, None], 0.0), axis=1).astype(bf16)
    tables = spread(table)

    def choose(values):
        found = values[0]
        for s, value in enumerate(values):
            if value is not found:
                found = jnp.where(stage == s, value, found)
        return found

    rates, normeds, ins, outs, grads = [], [], [], [], []
    gain_sum = jnp.zeros((1, width), f32)
    behind = ahead = None
    for tick in range(MICRO + 2 * stages - 1):
        if tick < ticks:
            if tick == 0:
                here = tokens[:rows]
            elif tick < MICRO:
                here = jnp.where(stage == 0, tokens[tick * rows:(tick + 1) * rows], behind)
            else:
                here = behind
            here_blocks = spread(here)
            rate, normed, parts = forward_experts(tick, here_blocks, tables, gain, forward_weights)
            parts = collect(parts)
            out = sum(p.astype(f32) for p in parts).astype(bf16)
            rates.append(rate)
            normeds.append(normed)
            ins.append(here)
            outs.append(out)
            if tick + 1 < ticks:
                behind_next = shifted(out, 0, 0, 1)
        if tick >= stages:
            number = tick - stages
            latest = min(ticks, tick) - 1
            picks = [min(max(tick - (2 * stages - 1) + 2 * s, 0), latest) for s in range(stages)]
            if number == 0:
                grad = cotangent[:rows]
            elif number < MICRO:
                grad = jnp.where(stage == stages - 1, cotangent[number * rows:(number + 1) * rows], ahead)
            else:
                grad = ahead
            grad_blocks = spread(grad)
            gained, parts = backward_experts(tick, picks, grad_blocks, rates, normeds, backward_weights)
            parts = collect(parts)
            normed_grad = sum(p.astype(f32) for p in parts)
            x = choose([ins[at] for at in picks]).astype(f32)
            scale = inverse_rms(x)
            weighted = gain * normed_grad
            grad_x = (
                grad.astype(f32)
                + scale * weighted
                - x * scale * scale * scale * jnp.mean(weighted * x, axis=-1, keepdims=True)
            ).astype(bf16)
            gain_sum = gain_sum + gained
            grads.append(grad_x)
            if number + 1 < ticks:
                ahead = shifted(grad_x, 0, 0, -1)
        if tick + 1 < ticks:
            behind = behind_next
    gain_grad = summed_over_owners(gain_sum) / gain
    segment_out = jnp.concatenate([choose([outs[m + s] for s in range(stages)]) for m in range(MICRO)])
    segment_grad = jnp.concatenate(
        [choose([grads[m + stages - 1 - s] for s in range(stages)]) for m in range(MICRO)]
    )
    return (segment_out[None], segment_grad[None], gain_grad)


def body(tokens, cotangent, owner_ids, *rest):
    owners = lax.axis_size("dp") * lax.axis_size("expert")
    routed_densely = owners <= 2 * owner_ids.shape[2] and lax.axis_size("expert") % 2 == 0
    plan = dense_body if routed_densely else slot_body
    return plan(tokens, cotangent, owner_ids, *rest)


def solution(mesh):
    in_specs = (
        P(("dp", "expert"), None),
        P(("dp", "expert"), None),
        P("pipe", ("dp", "expert"), None),
        P("pipe", ("dp", "expert"), None),
        P("pipe", None),
        P("pipe", ("dp", "expert"), None, None),
        P("pipe", ("dp", "expert"), None, None),
        P("pipe", ("dp", "expert"), None, None),
    )
    out_specs = (
        P("pipe", ("dp", "expert"), None),
        P("pipe", ("dp", "expert"), None),
        P("pipe", None),
    )
    return jax.shard_map(body, mesh=mesh, in_specs=in_specs, out_specs=out_specs, check_vma=False)
```

```python
import jax
import jax.numpy as jnp
from jax import lax
from jax.experimental import pallas as pl
from jax.experimental.pallas import tpu as pltpu
import functools
import math
from jax.sharding import PartitionSpec as P

MICRO = 4
LIMIT = 12 * 1024 * 1024


epsilon = 1e-06


def from_behind(value, axis, steps):
    count = lax.axis_size(axis)
    leading, last = (max(0, -steps), min(count, count - steps))
    return lax.ppermute(value, axis, [(source, source + steps) for source in range(leading, last)])


def inverse_rms(values):
    return lax.rsqrt(jnp.mean(values * values, axis=-1, keepdims=True) + epsilon)


def contract_last(left, right):
    return lax.dot_general(
        left, right, (((1,), (1,)), ((), ())), preferred_element_type=jnp.float32
    )


def route_tables(ids_part, owners, capacity):
    owner_range = jnp.arange(owners, dtype=jnp.int32)
    onehot = (ids_part[:, :, None] == owner_range[None, None, :]).astype(jnp.int32)
    member = jnp.sum(onehot, axis=1)
    position = jnp.cumsum(member, axis=0) - member
    slot_range = jnp.arange(capacity, dtype=jnp.int32)
    placed = (position[:, :, None] == slot_range[None, None, :]) & (member[:, :, None] > 0)
    placing = jnp.transpose(placed, (1, 2, 0)).astype(jnp.bfloat16)
    return (onehot.astype(jnp.float32), placing)


def gate_slots(onehot, gates_part, placing, experts_here):
    gate_pairs = gates_part.astype(jnp.float32).reshape(gates_part.shape[0], -1, experts_here)
    chosen = jnp.einsum("rjo,rjc->roc", onehot, gate_pairs)
    return jnp.einsum("okr,roc->okc", placing.astype(jnp.float32), chosen).astype(jnp.bfloat16)


def send_rows(row_block, pair_block):
    got_rows, got_pairs = (
        lax.all_to_all(row_block, ("dp", "expert"), split_axis=0, concat_axis=0, tiled=True),
        lax.all_to_all(pair_block, ("dp", "expert"), split_axis=0, concat_axis=0, tiled=True),
    )
    return (got_rows, got_pairs)


def return_rows(row_block):
    return lax.all_to_all(row_block, ("dp", "expert"), split_axis=0, concat_axis=0, tiled=True)


def send_grads(row_block):
    return lax.all_to_all(row_block, ("dp", "expert"), split_axis=0, concat_axis=0, tiled=True)


def return_grads(row_block):
    return lax.all_to_all(row_block, ("dp", "expert"), split_axis=0, concat_axis=0, tiled=True)


def expert_forward(flat_rows, flat_pairs, joint_mats, down_mats):
    hidden_width = down_mats.shape[1]
    joint_pre = jnp.dot(flat_rows, joint_mats[0], preferred_element_type=jnp.float32)
    gate_pre = joint_pre[:, :hidden_width]
    up_pre = joint_pre[:, hidden_width:]
    hidden = (jax.nn.silu(gate_pre) * up_pre).astype(jnp.bfloat16)
    projected = jnp.dot(hidden, down_mats[0], preferred_element_type=jnp.float32)
    term = flat_pairs.astype(jnp.float32) * projected
    kept_both = [joint_pre]
    return (term.astype(jnp.bfloat16), jnp.stack(kept_both))


def expert_backward(grad_rows, flat_pairs, joint_keep, joint_mats, down_mats):
    hidden_width = down_mats.shape[1]
    q_vals = contract_last(grad_rows, down_mats[0])
    gate_pre = joint_keep[0][:, :hidden_width]
    up_pre = joint_keep[0][:, hidden_width:]
    sigma = jax.nn.sigmoid(gate_pre)
    weight = flat_pairs.astype(jnp.float32)
    d_gate = (q_vals * weight * up_pre * sigma * (1.0 + gate_pre * (1.0 - sigma))).astype(
        jnp.bfloat16
    )
    d_up = (q_vals * weight * gate_pre * sigma).astype(jnp.bfloat16)
    joint_grad = jnp.concatenate([d_gate, d_up], axis=1)
    term = contract_last(joint_grad, joint_mats[0])
    return term.astype(jnp.bfloat16)


def slot_body(tokens, cotangent, owner_ids, gate_weights, norm_gain, w_gate, w_up, w_down):
    segments = lax.axis_size("pipe")
    segment_index = lax.axis_index("pipe")
    owners = lax.axis_size("dp") * lax.axis_size("expert")
    tok_rows = tokens.shape[0]
    width = tokens.shape[1]
    micro_rows = tok_rows // MICRO
    route_count = owner_ids.shape[2]
    capacity = max(2, (5 * micro_rows * route_count + 4 * owners - 1) // (4 * owners))
    slot_count = owners * capacity
    gain_row = norm_gain[0]
    joint_mats = jnp.concatenate([w_gate[0], w_up[0]], axis=2)
    down_mats = w_down[0]
    layer_ids = owner_ids[0]
    layer_gates = gate_weights[0]
    experts_here = joint_mats.shape[0]
    joint_width = joint_mats.shape[2]

    def skip_forward(operands):
        return (
            jnp.zeros((slot_count, width), jnp.bfloat16),
            jnp.zeros((experts_here, slot_count, joint_width), jnp.float32),
        )

    def run_forward(operands):
        return expert_forward(operands[0], operands[1], joint_mats, down_mats)

    def skip_backward(operands):
        return jnp.zeros((slot_count, width), jnp.bfloat16)

    def run_backward(operands):
        return expert_backward(operands[0], operands[1], operands[2], joint_mats, down_mats)

    def timing(micro):
        is_valid = (micro >= 0) & (micro < MICRO)
        slot_pick = jnp.where(is_valid, micro, MICRO)
        start_row = jnp.clip(micro, 0, MICRO - 1) * micro_rows
        return (is_valid, slot_pick, start_row)

    layer_outs = jnp.zeros((MICRO + 1, micro_rows, width), jnp.bfloat16)
    layer_ins = jnp.zeros((MICRO + 1, micro_rows, width), jnp.bfloat16)
    kept_joint = jnp.zeros((MICRO + 1, experts_here, slot_count, joint_width), jnp.float32)
    kept_pairs = jnp.zeros((MICRO + 1, slot_count, experts_here), jnp.bfloat16)
    grad_outs = jnp.zeros((MICRO + 1, micro_rows, width), jnp.bfloat16)
    gain_sum = jnp.zeros((width,), jnp.float32)
    ticks = MICRO + segments - 1
    incoming = jnp.zeros((micro_rows, width), jnp.bfloat16)
    for tick_num in range(ticks):
        forward_is_valid, forward_slot_pick, forward_start_row = timing(tick_num - segment_index)
        forward_own_part = lax.dynamic_slice_in_dim(tokens, forward_start_row, micro_rows, 0)
        forward_layer_in = jnp.where(segment_index == 0, forward_own_part, incoming)
        forward_ids_part = lax.dynamic_slice_in_dim(layer_ids, forward_start_row, micro_rows, 0)
        gates_part = lax.dynamic_slice_in_dim(layer_gates, forward_start_row, micro_rows, 0)
        forward_x_float = forward_layer_in.astype(jnp.float32)
        forward_scale = inverse_rms(forward_x_float)
        normed = (forward_x_float * forward_scale * gain_row).astype(jnp.bfloat16)
        forward_onehot, forward_placing = route_tables(forward_ids_part, owners, capacity)
        row_block = jnp.einsum(
            "okr,rd->okd", forward_placing, normed, preferred_element_type=jnp.float32
        ).astype(jnp.bfloat16)
        pair_block = gate_slots(forward_onehot, gates_part, forward_placing, experts_here)
        f_valid, f_pick, layer_in, x_float, f_placing, row_block, pair_block = (
            forward_is_valid,
            forward_slot_pick,
            forward_layer_in,
            forward_x_float,
            forward_placing,
            row_block,
            pair_block,
        )
        got_rows, got_pairs = send_rows(row_block, pair_block)
        flat_rows = got_rows.reshape(slot_count, width)
        flat_pairs = got_pairs.reshape(slot_count, experts_here)
        result, joint_pre = lax.cond(f_valid, run_forward, skip_forward, (flat_rows, flat_pairs))
        returned = return_rows(result.reshape(owners, capacity, width))
        branch = jnp.einsum("okr,okd->rd", f_placing, returned, preferred_element_type=jnp.float32)
        layer_out = (x_float + branch).astype(jnp.bfloat16)
        layer_outs = lax.dynamic_update_index_in_dim(layer_outs, layer_out, f_pick, 0)
        layer_ins = lax.dynamic_update_index_in_dim(layer_ins, layer_in, f_pick, 0)
        kept_joint = lax.dynamic_update_index_in_dim(kept_joint, joint_pre, f_pick, 0)
        kept_pairs = lax.dynamic_update_index_in_dim(kept_pairs, flat_pairs, f_pick, 0)
        if tick_num + 1 < ticks:
            incoming = from_behind(layer_out, "pipe", 1)
    incoming = jnp.zeros((micro_rows, width), jnp.bfloat16)
    for tick_num in range(ticks):
        backward_is_valid, backward_slot_pick, backward_start_row = timing(
            tick_num - (segments - 1 - segment_index)
        )
        own_part = lax.dynamic_slice_in_dim(cotangent, backward_start_row, micro_rows, 0)
        backward_grad_in = jnp.where(segment_index == segments - 1, own_part, incoming)
        ids_part = lax.dynamic_slice_in_dim(layer_ids, backward_start_row, micro_rows, 0)
        backward_layer_in = lax.dynamic_index_in_dim(
            layer_ins, backward_slot_pick, 0, keepdims=False
        )
        backward_x_float = backward_layer_in.astype(jnp.float32)
        backward_scale = inverse_rms(backward_x_float)
        _, backward_placing = route_tables(ids_part, owners, capacity)
        grad_block = jnp.einsum(
            "okr,rd->okd", backward_placing, backward_grad_in, preferred_element_type=jnp.float32
        ).astype(jnp.bfloat16)
        b_valid, b_pick, grad_in, bx_float, b_scale, b_placing, grad_block = (
            backward_is_valid,
            backward_slot_pick,
            backward_grad_in,
            backward_x_float,
            backward_scale,
            backward_placing,
            grad_block,
        )
        got_grads = send_grads(grad_block).reshape(slot_count, width)
        joint_keep = lax.dynamic_index_in_dim(kept_joint, b_pick, 0, keepdims=False)
        pair_keep = lax.dynamic_index_in_dim(kept_pairs, b_pick, 0, keepdims=False)
        owner_grad = lax.cond(
            b_valid, run_backward, skip_backward, (got_grads, pair_keep, joint_keep)
        )
        returned = return_grads(owner_grad.reshape(owners, capacity, width))
        normed_grad = jnp.einsum(
            "okr,okd->rd", b_placing, returned, preferred_element_type=jnp.float32
        )
        weighted = gain_row * normed_grad
        grad_x = (
            grad_in.astype(jnp.float32)
            + b_scale * weighted
            - bx_float
            * b_scale
            * b_scale
            * b_scale
            * jnp.mean(weighted * bx_float, axis=-1, keepdims=True)
        )
        gain_term = jnp.where(b_valid, jnp.sum(normed_grad * bx_float * b_scale, axis=0), 0.0)
        grad_bf, gain_term = (grad_x.astype(jnp.bfloat16), gain_term)
        grad_outs = lax.dynamic_update_index_in_dim(grad_outs, grad_bf, b_pick, 0)
        gain_sum = gain_sum + gain_term
        if tick_num + 1 < ticks:
            incoming = from_behind(grad_bf, "pipe", -1)
    gain_grad = lax.psum(gain_sum, ("dp", "expert"))
    segment_out = layer_outs[:MICRO].reshape(1, tok_rows, width)
    segment_grad = grad_outs[:MICRO].reshape(1, tok_rows, width)
    return (segment_out, segment_grad, gain_grad.reshape(1, width))


def swap_cores(value):
    count = lax.axis_size("expert")
    return lax.ppermute(value, "expert", [(e, e ^ 1) for e in range(count)])


def device_number(dp, pipe, expert):
    return (dp * lax.axis_size("pipe") + pipe) * lax.axis_size("expert") + expert


def shifted(value, dp_step, chip_step, pipe_step):
    dps, pipes, experts = (lax.axis_size(name) for name in ("dp", "pipe", "expert"))
    pairs = []
    for dp in range(dps):
        for pipe in range(pipes):
            for expert in range(experts):
                target = device_number(
                    (dp + dp_step) % dps,
                    (pipe + pipe_step) % pipes,
                    (expert + 2 * chip_step) % experts,
                )
                pairs.append((device_number(dp, pipe, expert), target))
    return lax.ppermute(value, ("dp", "pipe", "expert"), pairs)


def chip_steps():
    dps, chips = lax.axis_size("dp"), lax.axis_size("expert") // 2
    steps = [(d, c) for d in range(dps) for c in range(chips)]
    return sorted(steps[1:], key=lambda step: -(step[0] + step[1]))


def spread(rows):
    return [rows] + [shifted(rows, d, c, 0) for d, c in chip_steps()]


def collect(blocks):
    dps, chips = lax.axis_size("dp"), lax.axis_size("expert") // 2
    back = [shifted(block, -d % dps, -c % chips, 0) for block, (d, c) in zip(blocks[1:], chip_steps())]
    return [blocks[0]] + back


VMEM = pl.BlockSpec(memory_space=pltpu.VMEM)
CHUNK = 256
HALVES = 2


def in_vmem(kernel, outs, scratch, flops, *operands, specs=None):
    moved = sum(math.prod(a.shape) * a.dtype.itemsize for a in [*outs, *operands])
    return pl.pallas_call(
        kernel,
        out_shape=outs,
        in_specs=specs or [VMEM] * len(operands),
        out_specs=[VMEM] * len(outs),
        scratch_shapes=scratch,
        compiler_params=pltpu.CompilerParams(vmem_limit_bytes=LIMIT),
        cost_estimate=pl.CostEstimate(flops=flops, bytes_accessed=moved, transcendentals=0),
    )(*operands)


def load_kernel(*refs):
    own, pair, outs, sems = refs[:3], refs[3:6], refs[6:10], refs[10]
    ff = own[0].shape[1]
    copies = []
    for e, (gate_ref, up_ref, down_ref) in enumerate((own, pair)):
        copies += [
            pltpu.make_async_copy(gate_ref, outs[e].at[:, :ff], sems.at[3 * e]),
            pltpu.make_async_copy(up_ref, outs[e].at[:, ff:], sems.at[3 * e + 1]),
            pltpu.make_async_copy(down_ref, outs[2 + e], sems.at[3 * e + 2]),
        ]
    for copy in copies:
        copy.start()
    for copy in copies:
        copy.wait()


def loaded(own, pair):
    gate, _, down = own
    joint, down = pltpu.VMEM((gate.shape[0], 2 * gate.shape[1]), gate.dtype), pltpu.VMEM(down.shape, down.dtype)
    specs = [pl.BlockSpec(memory_space=pltpu.HBM)] * 6
    scratch = [pltpu.SemaphoreType.DMA((6,))]
    return in_vmem(load_kernel, [joint, joint, down, down], scratch, 0, *own, *pair, specs=specs)


def stage_kernel(out_ref):
    out_ref[...] = jnp.full(out_ref.shape, lax.axis_index("pipe"), jnp.int32)


def turn_kernel(in_ref, out_ref):
    size = math.gcd(in_ref.shape[0], CHUNK)

    @pl.loop(0, in_ref.shape[0] // size)
    def _(at):
        window = pl.ds(pl.multiple_of(at * size, size), size)
        out_ref[:, window] = in_ref[window, :].T


def turned(part):
    outs = [pltpu.VMEM(part.shape[::-1], part.dtype)]
    return in_vmem(turn_kernel, outs, [], 0, part)[0]


def in_chunks(width):
    half = width // HALVES

    def run(work):
        @pl.loop(0, HALVES)
        def _(at):
            for start in range(0, half, CHUNK):
                work(pl.ds(pl.multiple_of(at * half + start, CHUNK), CHUNK))

    return run


def owner_number():
    return lax.axis_index("dp") * lax.axis_size("expert") + lax.axis_index("expert")


def forward_kernel(blocks, tick, *refs):
    row_refs, table_refs, refs = refs[:blocks], refs[blocks:2 * blocks], refs[2 * blocks:]
    gain_ref, *weight_refs = refs[:5]
    rate_ref, flat_ref, own_ref, *part_refs, pre, hidden = refs[5:]
    rows, width = row_refs[0].shape
    ff = weight_refs[2].shape[0]
    gain = gain_ref[...]
    for k, row_ref in enumerate(row_refs):
        x = row_ref[...].astype(jnp.float32)
        flat_ref[k * rows:(k + 1) * rows, :] = (x * inverse_rms(x) * gain).astype(jnp.bfloat16)
    micro = tick - lax.axis_index("pipe")
    is_valid = (micro >= 0) & (micro < MICRO)
    first = pl.multiple_of(jnp.clip(micro, 0, MICRO - 1) * rows, rows)
    routed = jnp.concatenate([ref[pl.ds(first, rows), :] for ref in table_refs], axis=0).astype(jnp.float32)
    number = lax.broadcasted_iota(jnp.int32, routed.shape, 1)
    me = owner_number()
    for e, owner in enumerate((me, me ^ 1)):
        weight = jnp.sum(jnp.where((number == owner) & is_valid, routed, 0.0), axis=1, keepdims=True)
        for start in range(0, 2 * ff, CHUNK):
            pre[:, start:start + CHUNK] = jnp.dot(
                flat_ref[...], weight_refs[e][:, start:start + CHUNK], preferred_element_type=jnp.float32
            )
        gate_pre, up_pre = pre[:, :ff], pre[:, ff:]
        sigma = jax.nn.sigmoid(gate_pre)
        up_rate = weight * gate_pre * sigma
        hidden[:, e * ff:(e + 1) * ff] = (up_rate * up_pre).astype(jnp.bfloat16)
        rate_ref[:, 2 * e * ff:(2 * e + 1) * ff] = weight * up_pre * sigma * (1.0 + gate_pre * (1.0 - sigma))
        rate_ref[:, (2 * e + 1) * ff:(2 * e + 2) * ff] = up_rate

    @in_chunks(width)
    def _(columns):
        partial = sum(
            jnp.dot(hidden[:, e * ff:(e + 1) * ff], weight_refs[2 + e][:, columns], preferred_element_type=jnp.float32)
            for e in range(2)
        )
        own_ref[:, columns] = row_refs[0][:, columns].astype(jnp.float32) + partial[:rows]
        for k, part_ref in enumerate(part_refs):
            part_ref[:, columns] = partial[(k + 1) * rows:(k + 2) * rows].astype(jnp.bfloat16)


def backward_kernel(blocks, first, picks, saves, *refs):
    row_refs, refs = refs[:blocks], refs[blocks:]
    rate_refs, normed_refs, refs = refs[:saves], refs[saves:2 * saves], refs[2 * saves:]
    weight_refs, (gain_ref, own_ref, *part_refs, flat, rate, normed, hidden, sems) = refs[:4], refs[4:]
    rows, width = row_refs[0].shape
    ff = weight_refs[2].shape[1]
    stage = lax.axis_index("pipe")

    def copies(at):
        return (
            pltpu.make_async_copy(rate_refs[at], rate, sems.at[0]),
            pltpu.make_async_copy(normed_refs[at], normed, sems.at[1]),
        )

    for at in range(saves):
        holders = [s for s, picked in enumerate(picks) if picked == at]

        @pl.when(functools.reduce(jnp.logical_or, [stage == s for s in holders]))
        def _():
            for copy in copies(at):
                copy.start()

    for k, row_ref in enumerate(row_refs):
        flat[k * rows:(k + 1) * rows, :] = row_ref[...]
    micro = first + stage
    kept = jnp.where((micro >= 0) & (micro < MICRO), 1.0, 0.0)
    for e in range(2):
        q = jnp.dot(flat[...], weight_refs[2 + e][...], preferred_element_type=jnp.float32) * kept
        if e == 0:
            for copy in copies(0):
                copy.wait()
        for half in range(2):
            columns = slice((2 * e + half) * ff, (2 * e + half + 1) * ff)
            hidden[:, columns] = (q * rate[:, columns]).astype(jnp.bfloat16)

    @in_chunks(width)
    def _(columns):
        partial = sum(
            jnp.dot(
                hidden[:, 2 * e * ff:(2 * e + 2) * ff], weight_refs[e][:, columns], preferred_element_type=jnp.float32
            )
            for e in range(2)
        )
        gain_ref[:, columns] = jnp.sum(partial * normed[:, columns].astype(jnp.float32), axis=0, keepdims=True)
        own_ref[:, columns] = partial[:rows]
        for k, part_ref in enumerate(part_refs):
            part_ref[:, columns] = partial[(k + 1) * rows:(k + 2) * rows].astype(jnp.bfloat16)


def forward_experts(tick, row_blocks, tables, gain, weights):
    blocks, (rows, width) = len(row_blocks), row_blocks[0].shape
    total, ff = blocks * rows, weights[2].shape[0]
    outs = [
        jax.ShapeDtypeStruct((total, 4 * ff), jnp.float32),
        jax.ShapeDtypeStruct((total, width), jnp.bfloat16),
        jax.ShapeDtypeStruct((rows, width), jnp.float32),
    ]
    outs += [jax.ShapeDtypeStruct((rows, width), jnp.bfloat16)] * (blocks - 1)
    scratch = [pltpu.VMEM((total, 2 * ff), jnp.float32), pltpu.VMEM((total, 2 * ff), jnp.bfloat16)]
    kernel = functools.partial(forward_kernel, blocks, tick)
    flops = 12 * total * width * ff
    rate, normed, *parts = in_vmem(kernel, outs, scratch, flops, *row_blocks, *tables, gain, *weights)
    return rate, normed, parts


def backward_experts(first, picks, row_blocks, rates, normeds, weights):
    blocks, (rows, width) = len(row_blocks), row_blocks[0].shape
    total, wide = rates[0].shape
    outs = [jax.ShapeDtypeStruct((1, width), jnp.float32), jax.ShapeDtypeStruct((rows, width), jnp.float32)]
    outs += [jax.ShapeDtypeStruct((rows, width), jnp.bfloat16)] * (blocks - 1)
    scratch = [
        pltpu.VMEM((total, width), jnp.bfloat16),
        pltpu.VMEM((total, wide), jnp.float32),
        pltpu.VMEM((total, width), jnp.bfloat16),
        pltpu.VMEM((total, wide), jnp.bfloat16),
        pltpu.SemaphoreType.DMA((2,)),
    ]
    used = sorted(set(picks))
    kernel = functools.partial(backward_kernel, blocks, first, [used.index(at) for at in picks], len(used))
    anywhere = pl.BlockSpec(memory_space=pl.ANY)
    specs = [VMEM] * blocks + [anywhere] * (2 * len(used)) + [VMEM] * 4
    saved = [rates[at] for at in used] + [normeds[at] for at in used]
    flops = 3 * total * width * wide
    gained, *parts = in_vmem(kernel, outs, scratch, flops, *row_blocks, *saved, *weights, specs=specs)
    return gained, parts


def summed_over_owners(value):
    dps, chips = lax.axis_size("dp"), lax.axis_size("expert") // 2
    value = value + swap_cores(value)
    total = value
    for step in range(1, chips):
        total = total + shifted(value, 0, step, 0)
    value = total
    for step in range(1, dps):
        total = total + shifted(value, step, 0, 0)
    return total


def dense_body(tokens, cotangent, owner_ids, gate_weights, norm_gain, w_gate, w_up, w_down):
    f32, bf16 = jnp.float32, jnp.bfloat16
    stages = lax.axis_size("pipe")
    owners = lax.axis_size("dp") * lax.axis_size("expert")
    tok_rows, width = tokens.shape
    rows = tok_rows // MICRO
    gain = norm_gain[0][None, :]
    ticks = MICRO + stages - 1
    stage = in_vmem(stage_kernel, [jax.ShapeDtypeStruct((1, width), jnp.int32)], [], 0)[0]

    own = [pltpu.with_memory_space_constraint(w[0, 0], pltpu.HBM) for w in (w_gate, w_up, w_down)]
    theirs = [swap_cores(w) for w in own]
    theirs = [pltpu.with_memory_space_constraint(w, pltpu.HBM) for w in theirs]
    forward_weights = loaded(own, theirs)
    backward_weights = []
    for number, part in enumerate(forward_weights):
        backward_weights.append(turned(part))

    onehot = owner_ids[0][:, :, None] == jnp.arange(owners, dtype=jnp.int32)
    table = jnp.sum(jnp.where(onehot, gate_weights[0].astype(f32)[:, :, None], 0.0), axis=1).astype(bf16)
    tables = spread(table)

    def choose(values):
        found = values[0]
        for s, value in enumerate(values):
            if value is not found:
                found = jnp.where(stage == s, value, found)
        return found

    rates, normeds, ins, outs, grads = [], [], [], [], []
    gain_sum = jnp.zeros((1, width), f32)
    behind = ahead = None
    last = ticks + stages - 2
    for tick in range(last + 1):
        if tick < ticks:
            if tick == 0:
                here = tokens[:rows]
            elif tick < MICRO:
                here = jnp.where(stage == 0, tokens[tick * rows:(tick + 1) * rows], behind)
            else:
                here = behind
            here_blocks = spread(here)
            rate, normed, parts = forward_experts(tick, here_blocks, tables, gain, forward_weights)
            parts = collect(parts)
            out = lax.optimization_barrier(sum(p.astype(f32) for p in parts).astype(bf16))
            rates.append(rate)
            normeds.append(normed)
            ins.append(here)
            outs.append(out)
            if tick + 1 < ticks:
                behind = shifted(out, 0, 0, 1)
        number = tick - (stages - 1)
        if number >= 0:
            first = number - (stages - 1)
            picks = [min(max(first + 2 * s, 0), min(ticks - 1, tick)) for s in range(stages)]
            if number == 0:
                grad = cotangent[:rows]
            elif number < MICRO:
                grad = jnp.where(stage == stages - 1, cotangent[number * rows:(number + 1) * rows], ahead)
            else:
                grad = ahead
            grad_blocks = spread(grad)
            gained, parts = backward_experts(first, picks, grad_blocks, rates, normeds, backward_weights)
            parts = collect(parts)
            normed_grad = sum(p.astype(f32) for p in parts)
            x = choose([ins[at] for at in picks]).astype(f32)
            scale = inverse_rms(x)
            weighted = gain * normed_grad
            grad_x = (
                grad.astype(f32)
                + scale * weighted
                - x * scale * scale * scale * jnp.mean(weighted * x, axis=-1, keepdims=True)
            ).astype(bf16)
            gain_sum = gain_sum + gained
            if tick < last:
                grad_x = lax.optimization_barrier(grad_x)
            grads.append(grad_x)
            if tick < last:
                ahead = shifted(grad_x, 0, 0, -1)
    gain_grad = summed_over_owners(gain_sum) / gain
    segment_out = jnp.concatenate([choose([outs[m + s] for s in range(stages)]) for m in range(MICRO)])
    segment_grad = jnp.concatenate(
        [choose([grads[m + stages - 1 - s] for s in range(stages)]) for m in range(MICRO)]
    )
    return (segment_out[None], segment_grad[None], gain_grad)


def body(tokens, cotangent, owner_ids, *rest):
    owners = lax.axis_size("dp") * lax.axis_size("expert")
    routed_densely = owners <= 2 * owner_ids.shape[2] and lax.axis_size("expert") % 2 == 0
    plan = dense_body if routed_densely else slot_body
    return plan(tokens, cotangent, owner_ids, *rest)


def solution(mesh):
    in_specs = (
        P(("dp", "expert"), None),
        P(("dp", "expert"), None),
        P("pipe", ("dp", "expert"), None),
        P("pipe", ("dp", "expert"), None),
        P("pipe", None),
        P("pipe", ("dp", "expert"), None, None),
        P("pipe", ("dp", "expert"), None, None),
        P("pipe", ("dp", "expert"), None, None),
    )
    out_specs = (
        P("pipe", ("dp", "expert"), None),
        P("pipe", ("dp", "expert"), None),
        P("pipe", None),
    )
    return jax.shard_map(body, mesh=mesh, in_specs=in_specs, out_specs=out_specs, check_vma=False)
```

```python
import jax
import jax.numpy as jnp
from jax import lax
from jax.experimental import pallas as pl
from jax.experimental.pallas import tpu as pltpu
import functools
import math
from jax.sharding import PartitionSpec as P

MICRO = 4
LIMIT = 12 * 1024 * 1024


epsilon = 1e-06


def from_behind(value, axis, steps):
    count = lax.axis_size(axis)
    leading, last = (max(0, -steps), min(count, count - steps))
    return lax.ppermute(value, axis, [(source, source + steps) for source in range(leading, last)])


def inverse_rms(values):
    return lax.rsqrt(jnp.mean(values * values, axis=-1, keepdims=True) + epsilon)


def contract_last(left, right):
    return lax.dot_general(
        left, right, (((1,), (1,)), ((), ())), preferred_element_type=jnp.float32
    )


def route_tables(ids_part, owners, capacity):
    owner_range = jnp.arange(owners, dtype=jnp.int32)
    onehot = (ids_part[:, :, None] == owner_range[None, None, :]).astype(jnp.int32)
    member = jnp.sum(onehot, axis=1)
    position = jnp.cumsum(member, axis=0) - member
    slot_range = jnp.arange(capacity, dtype=jnp.int32)
    placed = (position[:, :, None] == slot_range[None, None, :]) & (member[:, :, None] > 0)
    placing = jnp.transpose(placed, (1, 2, 0)).astype(jnp.bfloat16)
    return (onehot.astype(jnp.float32), placing)


def gate_slots(onehot, gates_part, placing, experts_here):
    gate_pairs = gates_part.astype(jnp.float32).reshape(gates_part.shape[0], -1, experts_here)
    chosen = jnp.einsum("rjo,rjc->roc", onehot, gate_pairs)
    return jnp.einsum("okr,roc->okc", placing.astype(jnp.float32), chosen).astype(jnp.bfloat16)


def send_rows(row_block, pair_block):
    got_rows, got_pairs = (
        lax.all_to_all(row_block, ("dp", "expert"), split_axis=0, concat_axis=0, tiled=True),
        lax.all_to_all(pair_block, ("dp", "expert"), split_axis=0, concat_axis=0, tiled=True),
    )
    return (got_rows, got_pairs)


def return_rows(row_block):
    return lax.all_to_all(row_block, ("dp", "expert"), split_axis=0, concat_axis=0, tiled=True)


def send_grads(row_block):
    return lax.all_to_all(row_block, ("dp", "expert"), split_axis=0, concat_axis=0, tiled=True)


def return_grads(row_block):
    return lax.all_to_all(row_block, ("dp", "expert"), split_axis=0, concat_axis=0, tiled=True)


def expert_forward(flat_rows, flat_pairs, joint_mats, down_mats):
    hidden_width = down_mats.shape[1]
    joint_pre = jnp.dot(flat_rows, joint_mats[0], preferred_element_type=jnp.float32)
    gate_pre = joint_pre[:, :hidden_width]
    up_pre = joint_pre[:, hidden_width:]
    hidden = (jax.nn.silu(gate_pre) * up_pre).astype(jnp.bfloat16)
    projected = jnp.dot(hidden, down_mats[0], preferred_element_type=jnp.float32)
    term = flat_pairs.astype(jnp.float32) * projected
    kept_both = [joint_pre]
    return (term.astype(jnp.bfloat16), jnp.stack(kept_both))


def expert_backward(grad_rows, flat_pairs, joint_keep, joint_mats, down_mats):
    hidden_width = down_mats.shape[1]
    q_vals = contract_last(grad_rows, down_mats[0])
    gate_pre = joint_keep[0][:, :hidden_width]
    up_pre = joint_keep[0][:, hidden_width:]
    sigma = jax.nn.sigmoid(gate_pre)
    weight = flat_pairs.astype(jnp.float32)
    d_gate = (q_vals * weight * up_pre * sigma * (1.0 + gate_pre * (1.0 - sigma))).astype(
        jnp.bfloat16
    )
    d_up = (q_vals * weight * gate_pre * sigma).astype(jnp.bfloat16)
    joint_grad = jnp.concatenate([d_gate, d_up], axis=1)
    term = contract_last(joint_grad, joint_mats[0])
    return term.astype(jnp.bfloat16)


def slot_body(tokens, cotangent, owner_ids, gate_weights, norm_gain, w_gate, w_up, w_down):
    segments = lax.axis_size("pipe")
    segment_index = lax.axis_index("pipe")
    owners = lax.axis_size("dp") * lax.axis_size("expert")
    tok_rows = tokens.shape[0]
    width = tokens.shape[1]
    micro_rows = tok_rows // MICRO
    route_count = owner_ids.shape[2]
    capacity = max(2, (5 * micro_rows * route_count + 4 * owners - 1) // (4 * owners))
    slot_count = owners * capacity
    gain_row = norm_gain[0]
    joint_mats = jnp.concatenate([w_gate[0], w_up[0]], axis=2)
    down_mats = w_down[0]
    layer_ids = owner_ids[0]
    layer_gates = gate_weights[0]
    experts_here = joint_mats.shape[0]
    joint_width = joint_mats.shape[2]

    def skip_forward(operands):
        return (
            jnp.zeros((slot_count, width), jnp.bfloat16),
            jnp.zeros((experts_here, slot_count, joint_width), jnp.float32),
        )

    def run_forward(operands):
        return expert_forward(operands[0], operands[1], joint_mats, down_mats)

    def skip_backward(operands):
        return jnp.zeros((slot_count, width), jnp.bfloat16)

    def run_backward(operands):
        return expert_backward(operands[0], operands[1], operands[2], joint_mats, down_mats)

    def timing(micro):
        is_valid = (micro >= 0) & (micro < MICRO)
        slot_pick = jnp.where(is_valid, micro, MICRO)
        start_row = jnp.clip(micro, 0, MICRO - 1) * micro_rows
        return (is_valid, slot_pick, start_row)

    layer_outs = jnp.zeros((MICRO + 1, micro_rows, width), jnp.bfloat16)
    layer_ins = jnp.zeros((MICRO + 1, micro_rows, width), jnp.bfloat16)
    kept_joint = jnp.zeros((MICRO + 1, experts_here, slot_count, joint_width), jnp.float32)
    kept_pairs = jnp.zeros((MICRO + 1, slot_count, experts_here), jnp.bfloat16)
    grad_outs = jnp.zeros((MICRO + 1, micro_rows, width), jnp.bfloat16)
    gain_sum = jnp.zeros((width,), jnp.float32)
    ticks = MICRO + segments - 1
    incoming = jnp.zeros((micro_rows, width), jnp.bfloat16)
    for tick_num in range(ticks):
        forward_is_valid, forward_slot_pick, forward_start_row = timing(tick_num - segment_index)
        forward_own_part = lax.dynamic_slice_in_dim(tokens, forward_start_row, micro_rows, 0)
        forward_layer_in = jnp.where(segment_index == 0, forward_own_part, incoming)
        forward_ids_part = lax.dynamic_slice_in_dim(layer_ids, forward_start_row, micro_rows, 0)
        gates_part = lax.dynamic_slice_in_dim(layer_gates, forward_start_row, micro_rows, 0)
        forward_x_float = forward_layer_in.astype(jnp.float32)
        forward_scale = inverse_rms(forward_x_float)
        normed = (forward_x_float * forward_scale * gain_row).astype(jnp.bfloat16)
        forward_onehot, forward_placing = route_tables(forward_ids_part, owners, capacity)
        row_block = jnp.einsum(
            "okr,rd->okd", forward_placing, normed, preferred_element_type=jnp.float32
        ).astype(jnp.bfloat16)
        pair_block = gate_slots(forward_onehot, gates_part, forward_placing, experts_here)
        f_valid, f_pick, layer_in, x_float, f_placing, row_block, pair_block = (
            forward_is_valid,
            forward_slot_pick,
            forward_layer_in,
            forward_x_float,
            forward_placing,
            row_block,
            pair_block,
        )
        got_rows, got_pairs = send_rows(row_block, pair_block)
        flat_rows = got_rows.reshape(slot_count, width)
        flat_pairs = got_pairs.reshape(slot_count, experts_here)
        result, joint_pre = lax.cond(f_valid, run_forward, skip_forward, (flat_rows, flat_pairs))
        returned = return_rows(result.reshape(owners, capacity, width))
        branch = jnp.einsum("okr,okd->rd", f_placing, returned, preferred_element_type=jnp.float32)
        layer_out = (x_float + branch).astype(jnp.bfloat16)
        layer_outs = lax.dynamic_update_index_in_dim(layer_outs, layer_out, f_pick, 0)
        layer_ins = lax.dynamic_update_index_in_dim(layer_ins, layer_in, f_pick, 0)
        kept_joint = lax.dynamic_update_index_in_dim(kept_joint, joint_pre, f_pick, 0)
        kept_pairs = lax.dynamic_update_index_in_dim(kept_pairs, flat_pairs, f_pick, 0)
        if tick_num + 1 < ticks:
            incoming = from_behind(layer_out, "pipe", 1)
    incoming = jnp.zeros((micro_rows, width), jnp.bfloat16)
    for tick_num in range(ticks):
        backward_is_valid, backward_slot_pick, backward_start_row = timing(
            tick_num - (segments - 1 - segment_index)
        )
        own_part = lax.dynamic_slice_in_dim(cotangent, backward_start_row, micro_rows, 0)
        backward_grad_in = jnp.where(segment_index == segments - 1, own_part, incoming)
        ids_part = lax.dynamic_slice_in_dim(layer_ids, backward_start_row, micro_rows, 0)
        backward_layer_in = lax.dynamic_index_in_dim(
            layer_ins, backward_slot_pick, 0, keepdims=False
        )
        backward_x_float = backward_layer_in.astype(jnp.float32)
        backward_scale = inverse_rms(backward_x_float)
        _, backward_placing = route_tables(ids_part, owners, capacity)
        grad_block = jnp.einsum(
            "okr,rd->okd", backward_placing, backward_grad_in, preferred_element_type=jnp.float32
        ).astype(jnp.bfloat16)
        b_valid, b_pick, grad_in, bx_float, b_scale, b_placing, grad_block = (
            backward_is_valid,
            backward_slot_pick,
            backward_grad_in,
            backward_x_float,
            backward_scale,
            backward_placing,
            grad_block,
        )
        got_grads = send_grads(grad_block).reshape(slot_count, width)
        joint_keep = lax.dynamic_index_in_dim(kept_joint, b_pick, 0, keepdims=False)
        pair_keep = lax.dynamic_index_in_dim(kept_pairs, b_pick, 0, keepdims=False)
        owner_grad = lax.cond(
            b_valid, run_backward, skip_backward, (got_grads, pair_keep, joint_keep)
        )
        returned = return_grads(owner_grad.reshape(owners, capacity, width))
        normed_grad = jnp.einsum(
            "okr,okd->rd", b_placing, returned, preferred_element_type=jnp.float32
        )
        weighted = gain_row * normed_grad
        grad_x = (
            grad_in.astype(jnp.float32)
            + b_scale * weighted
            - bx_float
            * b_scale
            * b_scale
            * b_scale
            * jnp.mean(weighted * bx_float, axis=-1, keepdims=True)
        )
        gain_term = jnp.where(b_valid, jnp.sum(normed_grad * bx_float * b_scale, axis=0), 0.0)
        grad_bf, gain_term = (grad_x.astype(jnp.bfloat16), gain_term)
        grad_outs = lax.dynamic_update_index_in_dim(grad_outs, grad_bf, b_pick, 0)
        gain_sum = gain_sum + gain_term
        if tick_num + 1 < ticks:
            incoming = from_behind(grad_bf, "pipe", -1)
    gain_grad = lax.psum(gain_sum, ("dp", "expert"))
    segment_out = layer_outs[:MICRO].reshape(1, tok_rows, width)
    segment_grad = grad_outs[:MICRO].reshape(1, tok_rows, width)
    return (segment_out, segment_grad, gain_grad.reshape(1, width))


def swap_cores(value):
    count = lax.axis_size("expert")
    return lax.ppermute(value, "expert", [(e, e ^ 1) for e in range(count)])


def device_number(dp, pipe, expert):
    return (dp * lax.axis_size("pipe") + pipe) * lax.axis_size("expert") + expert


def shifted(value, dp_step, chip_step, pipe_step):
    dps, pipes, experts = (lax.axis_size(name) for name in ("dp", "pipe", "expert"))
    pairs = []
    for dp in range(dps):
        for pipe in range(pipes):
            for expert in range(experts):
                target = device_number(
                    (dp + dp_step) % dps,
                    (pipe + pipe_step) % pipes,
                    (expert + 2 * chip_step) % experts,
                )
                pairs.append((device_number(dp, pipe, expert), target))
    return lax.ppermute(value, ("dp", "pipe", "expert"), pairs)


def chip_steps():
    dps, chips = lax.axis_size("dp"), lax.axis_size("expert") // 2
    steps = [(d, c) for d in range(dps) for c in range(chips)]
    return sorted(steps[1:], key=lambda step: -(step[0] + step[1]))


def spread(rows):
    return [rows] + [shifted(rows, d, c, 0) for d, c in chip_steps()]


def collect(blocks):
    dps, chips = lax.axis_size("dp"), lax.axis_size("expert") // 2
    back = [shifted(block, -d % dps, -c % chips, 0) for block, (d, c) in zip(blocks[1:], chip_steps())]
    return [blocks[0]] + back


VMEM = pl.BlockSpec(memory_space=pltpu.VMEM)
CHUNK = 256
HALVES = 2


def in_vmem(kernel, outs, scratch, flops, *operands, specs=None):
    moved = sum(math.prod(a.shape) * a.dtype.itemsize for a in [*outs, *operands])
    return pl.pallas_call(
        kernel,
        out_shape=outs,
        in_specs=specs or [VMEM] * len(operands),
        out_specs=[VMEM] * len(outs),
        scratch_shapes=scratch,
        compiler_params=pltpu.CompilerParams(vmem_limit_bytes=LIMIT),
        cost_estimate=pl.CostEstimate(flops=flops, bytes_accessed=moved, transcendentals=0),
    )(*operands)


def load_kernel(*refs):
    own, pair, outs, sems = refs[:3], refs[3:6], refs[6:10], refs[10]
    ff = own[0].shape[1]
    copies = []
    for e, (gate_ref, up_ref, down_ref) in enumerate((own, pair)):
        copies += [
            pltpu.make_async_copy(gate_ref, outs[e].at[:, :ff], sems.at[3 * e]),
            pltpu.make_async_copy(up_ref, outs[e].at[:, ff:], sems.at[3 * e + 1]),
            pltpu.make_async_copy(down_ref, outs[2 + e], sems.at[3 * e + 2]),
        ]
    for copy in copies:
        copy.start()
    for copy in copies:
        copy.wait()


def loaded(own, pair):
    gate, _, down = own
    joint, down = pltpu.VMEM((gate.shape[0], 2 * gate.shape[1]), gate.dtype), pltpu.VMEM(down.shape, down.dtype)
    specs = [pl.BlockSpec(memory_space=pltpu.HBM)] * 6
    scratch = [pltpu.SemaphoreType.DMA((6,))]
    return in_vmem(load_kernel, [joint, joint, down, down], scratch, 0, *own, *pair, specs=specs)


def stage_kernel(out_ref):
    out_ref[...] = jnp.full(out_ref.shape, lax.axis_index("pipe"), jnp.int32)


def turn_kernel(in_ref, out_ref):
    size = math.gcd(in_ref.shape[0], CHUNK)

    @pl.loop(0, in_ref.shape[0] // size)
    def _(at):
        window = pl.ds(pl.multiple_of(at * size, size), size)
        out_ref[:, window] = in_ref[window, :].T


def turned(part):
    outs = [pltpu.VMEM(part.shape[::-1], part.dtype)]
    return in_vmem(turn_kernel, outs, [], 0, part)[0]


def in_chunks(width):
    half = width // HALVES

    def run(work):
        @pl.loop(0, HALVES)
        def _(at):
            for start in range(0, half, CHUNK):
                work(pl.ds(pl.multiple_of(at * half + start, CHUNK), CHUNK))

    return run


def owner_number():
    return lax.axis_index("dp") * lax.axis_size("expert") + lax.axis_index("expert")


def forward_kernel(blocks, tick, *refs):
    row_refs, table_refs, refs = refs[:blocks], refs[blocks:2 * blocks], refs[2 * blocks:]
    gain_ref, *weight_refs = refs[:5]
    rate_ref, flat_ref, own_ref, *part_refs, pre, hidden = refs[5:]
    rows, width = row_refs[0].shape
    ff = weight_refs[2].shape[0]
    gain = gain_ref[...]
    for k, row_ref in enumerate(row_refs):
        x = row_ref[...].astype(jnp.float32)
        flat_ref[k * rows:(k + 1) * rows, :] = (x * inverse_rms(x) * gain).astype(jnp.bfloat16)
    micro = tick - lax.axis_index("pipe")
    is_valid = (micro >= 0) & (micro < MICRO)
    first = pl.multiple_of(jnp.clip(micro, 0, MICRO - 1) * rows, rows)
    routed = jnp.concatenate([ref[pl.ds(first, rows), :] for ref in table_refs], axis=0).astype(jnp.float32)
    number = lax.broadcasted_iota(jnp.int32, routed.shape, 1)
    me = owner_number()
    for e, owner in enumerate((me, me ^ 1)):
        weight = jnp.sum(jnp.where((number == owner) & is_valid, routed, 0.0), axis=1, keepdims=True)
        for start in range(0, 2 * ff, CHUNK):
            pre[:, start:start + CHUNK] = jnp.dot(
                flat_ref[...], weight_refs[e][:, start:start + CHUNK], preferred_element_type=jnp.float32
            )
        gate_pre, up_pre = pre[:, :ff], pre[:, ff:]
        sigma = jax.nn.sigmoid(gate_pre)
        up_rate = weight * gate_pre * sigma
        hidden[:, e * ff:(e + 1) * ff] = (up_rate * up_pre).astype(jnp.bfloat16)
        rate_ref[:, 2 * e * ff:(2 * e + 1) * ff] = weight * up_pre * sigma * (1.0 + gate_pre * (1.0 - sigma))
        rate_ref[:, (2 * e + 1) * ff:(2 * e + 2) * ff] = up_rate

    @in_chunks(width)
    def _(columns):
        partial = sum(
            jnp.dot(hidden[:, e * ff:(e + 1) * ff], weight_refs[2 + e][:, columns], preferred_element_type=jnp.float32)
            for e in range(2)
        )
        own_ref[:, columns] = row_refs[0][:, columns].astype(jnp.float32) + partial[:rows]
        for k, part_ref in enumerate(part_refs):
            part_ref[:, columns] = partial[(k + 1) * rows:(k + 2) * rows].astype(jnp.bfloat16)


def backward_kernel(blocks, first, picks, saves, *refs):
    row_refs, refs = refs[:blocks], refs[blocks:]
    rate_refs, normed_refs, refs = refs[:saves], refs[saves:2 * saves], refs[2 * saves:]
    weight_refs, (gain_ref, own_ref, *part_refs, flat, rate, normed, hidden, sems) = refs[:4], refs[4:]
    rows, width = row_refs[0].shape
    ff = weight_refs[2].shape[1]
    stage = lax.axis_index("pipe")

    def copies(at):
        return (
            pltpu.make_async_copy(rate_refs[at], rate, sems.at[0]),
            pltpu.make_async_copy(normed_refs[at], normed, sems.at[1]),
        )

    for at in range(saves):
        holders = [s for s, picked in enumerate(picks) if picked == at]

        @pl.when(functools.reduce(jnp.logical_or, [stage == s for s in holders]))
        def _():
            for copy in copies(at):
                copy.start()

    for k, row_ref in enumerate(row_refs):
        flat[k * rows:(k + 1) * rows, :] = row_ref[...]
    micro = first + stage
    kept = jnp.where((micro >= 0) & (micro < MICRO), 1.0, 0.0)
    for e in range(2):
        q = jnp.dot(flat[...], weight_refs[2 + e][...], preferred_element_type=jnp.float32) * kept
        if e == 0:
            for copy in copies(0):
                copy.wait()
        for half in range(2):
            columns = slice((2 * e + half) * ff, (2 * e + half + 1) * ff)
            hidden[:, columns] = (q * rate[:, columns]).astype(jnp.bfloat16)

    @in_chunks(width)
    def _(columns):
        partial = sum(
            jnp.dot(
                hidden[:, 2 * e * ff:(2 * e + 2) * ff], weight_refs[e][:, columns], preferred_element_type=jnp.float32
            )
            for e in range(2)
        )
        gain_ref[:, columns] = jnp.sum(partial * normed[:, columns].astype(jnp.float32), axis=0, keepdims=True)
        own_ref[:, columns] = partial[:rows]
        for k, part_ref in enumerate(part_refs):
            part_ref[:, columns] = partial[(k + 1) * rows:(k + 2) * rows].astype(jnp.bfloat16)


def forward_experts(tick, row_blocks, tables, gain, weights):
    blocks, (rows, width) = len(row_blocks), row_blocks[0].shape
    total, ff = blocks * rows, weights[2].shape[0]
    outs = [
        jax.ShapeDtypeStruct((total, 4 * ff), jnp.float32),
        jax.ShapeDtypeStruct((total, width), jnp.bfloat16),
        jax.ShapeDtypeStruct((rows, width), jnp.float32),
    ]
    outs += [jax.ShapeDtypeStruct((rows, width), jnp.bfloat16)] * (blocks - 1)
    scratch = [pltpu.VMEM((total, 2 * ff), jnp.float32), pltpu.VMEM((total, 2 * ff), jnp.bfloat16)]
    kernel = functools.partial(forward_kernel, blocks, tick)
    flops = 12 * total * width * ff
    rate, normed, *parts = in_vmem(kernel, outs, scratch, flops, *row_blocks, *tables, gain, *weights)
    return rate, normed, parts


def backward_experts(first, picks, row_blocks, rates, normeds, weights):
    blocks, (rows, width) = len(row_blocks), row_blocks[0].shape
    total, wide = rates[0].shape
    outs = [jax.ShapeDtypeStruct((1, width), jnp.float32), jax.ShapeDtypeStruct((rows, width), jnp.float32)]
    outs += [jax.ShapeDtypeStruct((rows, width), jnp.bfloat16)] * (blocks - 1)
    scratch = [
        pltpu.VMEM((total, width), jnp.bfloat16),
        pltpu.VMEM((total, wide), jnp.float32),
        pltpu.VMEM((total, width), jnp.bfloat16),
        pltpu.VMEM((total, wide), jnp.bfloat16),
        pltpu.SemaphoreType.DMA((2,)),
    ]
    used = sorted(set(picks))
    kernel = functools.partial(backward_kernel, blocks, first, [used.index(at) for at in picks], len(used))
    anywhere = pl.BlockSpec(memory_space=pl.ANY)
    specs = [VMEM] * blocks + [anywhere] * (2 * len(used)) + [VMEM] * 4
    saved = [rates[at] for at in used] + [normeds[at] for at in used]
    flops = 3 * total * width * wide
    gained, *parts = in_vmem(kernel, outs, scratch, flops, *row_blocks, *saved, *weights, specs=specs)
    return gained, parts


def summed_over_owners(value):
    value = value + swap_cores(value)
    return sum(spread(value))


def dense_body(tokens, cotangent, owner_ids, gate_weights, norm_gain, w_gate, w_up, w_down):
    f32, bf16 = jnp.float32, jnp.bfloat16
    stages = lax.axis_size("pipe")
    owners = lax.axis_size("dp") * lax.axis_size("expert")
    tok_rows, width = tokens.shape
    rows = tok_rows // MICRO
    gain = norm_gain[0][None, :]
    ticks = MICRO + stages - 1
    stage = in_vmem(stage_kernel, [jax.ShapeDtypeStruct((1, width), jnp.int32)], [], 0)[0]

    own = [pltpu.with_memory_space_constraint(w[0, 0], pltpu.HBM) for w in (w_gate, w_up, w_down)]
    theirs = [swap_cores(w) for w in own]
    theirs = [pltpu.with_memory_space_constraint(w, pltpu.HBM) for w in theirs]
    forward_weights = loaded(own, theirs)
    backward_weights = []
    for number, part in enumerate(forward_weights):
        backward_weights.append(turned(part))

    onehot = owner_ids[0][:, :, None] == jnp.arange(owners, dtype=jnp.int32)
    table = jnp.sum(jnp.where(onehot, gate_weights[0].astype(f32)[:, :, None], 0.0), axis=1).astype(bf16)
    tables = spread(table)

    def choose(values):
        found = values[0]
        for s, value in enumerate(values):
            if value is not found:
                found = jnp.where(stage == s, value, found)
        return found

    rates, normeds, ins, outs, grads = [], [], [], [], []
    gain_sum = jnp.zeros((1, width), f32)
    behind = ahead = None
    last = ticks + stages - 2
    for tick in range(last + 1):
        if tick < ticks:
            if tick == 0:
                here = tokens[:rows]
            elif tick < MICRO:
                here = jnp.where(stage == 0, tokens[tick * rows:(tick + 1) * rows], behind)
            else:
                here = behind
            here_blocks = spread(here)
            rate, normed, parts = forward_experts(tick, here_blocks, tables, gain, forward_weights)
            rates.append(rate)
            normeds.append(normed)
            ins.append(here)
            if tick + 1 < ticks:
                parts = collect(parts)
                outs.append(lax.optimization_barrier(sum(p.astype(f32) for p in parts).astype(bf16)))
                behind = shifted(outs[-1], 0, 0, 1)
        number = tick - (stages - 1)
        if number >= 0:
            first = number - (stages - 1)
            picks = [min(max(first + 2 * s, 0), min(ticks - 1, tick)) for s in range(stages)]
            if number == 0:
                grad = cotangent[:rows]
            elif number < MICRO:
                grad = jnp.where(stage == stages - 1, cotangent[number * rows:(number + 1) * rows], ahead)
            else:
                grad = ahead
            grad_blocks = spread(grad)
            gained, sums = backward_experts(first, picks, grad_blocks, rates, normeds, backward_weights)
            sums = collect(sums)
            normed_grad = sum(p.astype(f32) for p in sums)
            x = choose([ins[at] for at in picks]).astype(f32)
            scale = inverse_rms(x)
            weighted = gain * normed_grad
            grad_x = (
                grad.astype(f32)
                + scale * weighted
                - x * scale * scale * scale * jnp.mean(weighted * x, axis=-1, keepdims=True)
            ).astype(bf16)
            gain_sum = gain_sum + gained
            if tick < last:
                grad_x = lax.optimization_barrier(grad_x)
            grads.append(grad_x)
            if tick < last:
                ahead = shifted(grad_x, 0, 0, -1)
            if tick + 1 == ticks:
                parts = collect(lax.optimization_barrier((parts, grad_x))[0])
                outs.append(sum(p.astype(f32) for p in parts).astype(bf16))
    gain_grad = summed_over_owners(gain_sum) / gain
    segment_out = jnp.concatenate([choose([outs[m + s] for s in range(stages)]) for m in range(MICRO)])
    segment_grad = jnp.concatenate(
        [choose([grads[m + stages - 1 - s] for s in range(stages)]) for m in range(MICRO)]
    )
    return (segment_out[None], segment_grad[None], gain_grad)


def body(tokens, cotangent, owner_ids, *rest):
    owners = lax.axis_size("dp") * lax.axis_size("expert")
    routed_densely = owners <= 2 * owner_ids.shape[2] and lax.axis_size("expert") % 2 == 0
    plan = dense_body if routed_densely else slot_body
    return plan(tokens, cotangent, owner_ids, *rest)


def solution(mesh):
    in_specs = (
        P(("dp", "expert"), None),
        P(("dp", "expert"), None),
        P("pipe", ("dp", "expert"), None),
        P("pipe", ("dp", "expert"), None),
        P("pipe", None),
        P("pipe", ("dp", "expert"), None, None),
        P("pipe", ("dp", "expert"), None, None),
        P("pipe", ("dp", "expert"), None, None),
    )
    out_specs = (
        P("pipe", ("dp", "expert"), None),
        P("pipe", ("dp", "expert"), None),
        P("pipe", None),
    )
    return jax.shard_map(body, mesh=mesh, in_specs=in_specs, out_specs=out_specs, check_vma=False)
```

```python
import jax
import jax.numpy as jnp
from jax import lax
from jax.experimental import pallas as pl
from jax.experimental.pallas import tpu as pltpu
import functools
import math
from jax.sharding import PartitionSpec as P

MICRO = 4
LIMIT = 12 * 1024 * 1024


epsilon = 1e-06


def from_behind(value, axis, steps):
    count = lax.axis_size(axis)
    leading, last = (max(0, -steps), min(count, count - steps))
    return lax.ppermute(value, axis, [(source, source + steps) for source in range(leading, last)])


def inverse_rms(values):
    return lax.rsqrt(jnp.mean(values * values, axis=-1, keepdims=True) + epsilon)


def contract_last(left, right):
    return lax.dot_general(
        left, right, (((1,), (1,)), ((), ())), preferred_element_type=jnp.float32
    )


def route_tables(ids_part, owners, capacity):
    owner_range = jnp.arange(owners, dtype=jnp.int32)
    onehot = (ids_part[:, :, None] == owner_range[None, None, :]).astype(jnp.int32)
    member = jnp.sum(onehot, axis=1)
    position = jnp.cumsum(member, axis=0) - member
    slot_range = jnp.arange(capacity, dtype=jnp.int32)
    placed = (position[:, :, None] == slot_range[None, None, :]) & (member[:, :, None] > 0)
    placing = jnp.transpose(placed, (1, 2, 0)).astype(jnp.bfloat16)
    return (onehot.astype(jnp.float32), placing)


def gate_slots(onehot, gates_part, placing, experts_here):
    gate_pairs = gates_part.astype(jnp.float32).reshape(gates_part.shape[0], -1, experts_here)
    chosen = jnp.einsum("rjo,rjc->roc", onehot, gate_pairs)
    return jnp.einsum("okr,roc->okc", placing.astype(jnp.float32), chosen).astype(jnp.bfloat16)


def send_rows(row_block, pair_block):
    got_rows, got_pairs = (
        lax.all_to_all(row_block, ("dp", "expert"), split_axis=0, concat_axis=0, tiled=True),
        lax.all_to_all(pair_block, ("dp", "expert"), split_axis=0, concat_axis=0, tiled=True),
    )
    return (got_rows, got_pairs)


def return_rows(row_block):
    return lax.all_to_all(row_block, ("dp", "expert"), split_axis=0, concat_axis=0, tiled=True)


def send_grads(row_block):
    return lax.all_to_all(row_block, ("dp", "expert"), split_axis=0, concat_axis=0, tiled=True)


def return_grads(row_block):
    return lax.all_to_all(row_block, ("dp", "expert"), split_axis=0, concat_axis=0, tiled=True)


def expert_forward(flat_rows, flat_pairs, joint_mats, down_mats):
    hidden_width = down_mats.shape[1]
    joint_pre = jnp.dot(flat_rows, joint_mats[0], preferred_element_type=jnp.float32)
    gate_pre = joint_pre[:, :hidden_width]
    up_pre = joint_pre[:, hidden_width:]
    hidden = (jax.nn.silu(gate_pre) * up_pre).astype(jnp.bfloat16)
    projected = jnp.dot(hidden, down_mats[0], preferred_element_type=jnp.float32)
    term = flat_pairs.astype(jnp.float32) * projected
    kept_both = [joint_pre]
    return (term.astype(jnp.bfloat16), jnp.stack(kept_both))


def expert_backward(grad_rows, flat_pairs, joint_keep, joint_mats, down_mats):
    hidden_width = down_mats.shape[1]
    q_vals = contract_last(grad_rows, down_mats[0])
    gate_pre = joint_keep[0][:, :hidden_width]
    up_pre = joint_keep[0][:, hidden_width:]
    sigma = jax.nn.sigmoid(gate_pre)
    weight = flat_pairs.astype(jnp.float32)
    d_gate = (q_vals * weight * up_pre * sigma * (1.0 + gate_pre * (1.0 - sigma))).astype(
        jnp.bfloat16
    )
    d_up = (q_vals * weight * gate_pre * sigma).astype(jnp.bfloat16)
    joint_grad = jnp.concatenate([d_gate, d_up], axis=1)
    term = contract_last(joint_grad, joint_mats[0])
    return term.astype(jnp.bfloat16)


def slot_body(tokens, cotangent, owner_ids, gate_weights, norm_gain, w_gate, w_up, w_down):
    segments = lax.axis_size("pipe")
    segment_index = lax.axis_index("pipe")
    owners = lax.axis_size("dp") * lax.axis_size("expert")
    tok_rows = tokens.shape[0]
    width = tokens.shape[1]
    micro_rows = tok_rows // MICRO
    route_count = owner_ids.shape[2]
    capacity = max(2, (5 * micro_rows * route_count + 4 * owners - 1) // (4 * owners))
    slot_count = owners * capacity
    gain_row = norm_gain[0]
    joint_mats = jnp.concatenate([w_gate[0], w_up[0]], axis=2)
    down_mats = w_down[0]
    layer_ids = owner_ids[0]
    layer_gates = gate_weights[0]
    experts_here = joint_mats.shape[0]
    joint_width = joint_mats.shape[2]

    def skip_forward(operands):
        return (
            jnp.zeros((slot_count, width), jnp.bfloat16),
            jnp.zeros((experts_here, slot_count, joint_width), jnp.float32),
        )

    def run_forward(operands):
        return expert_forward(operands[0], operands[1], joint_mats, down_mats)

    def skip_backward(operands):
        return jnp.zeros((slot_count, width), jnp.bfloat16)

    def run_backward(operands):
        return expert_backward(operands[0], operands[1], operands[2], joint_mats, down_mats)

    def timing(micro):
        is_valid = (micro >= 0) & (micro < MICRO)
        slot_pick = jnp.where(is_valid, micro, MICRO)
        start_row = jnp.clip(micro, 0, MICRO - 1) * micro_rows
        return (is_valid, slot_pick, start_row)

    layer_outs = jnp.zeros((MICRO + 1, micro_rows, width), jnp.bfloat16)
    layer_ins = jnp.zeros((MICRO + 1, micro_rows, width), jnp.bfloat16)
    kept_joint = jnp.zeros((MICRO + 1, experts_here, slot_count, joint_width), jnp.float32)
    kept_pairs = jnp.zeros((MICRO + 1, slot_count, experts_here), jnp.bfloat16)
    grad_outs = jnp.zeros((MICRO + 1, micro_rows, width), jnp.bfloat16)
    gain_sum = jnp.zeros((width,), jnp.float32)
    ticks = MICRO + segments - 1
    incoming = jnp.zeros((micro_rows, width), jnp.bfloat16)
    for tick_num in range(ticks):
        forward_is_valid, forward_slot_pick, forward_start_row = timing(tick_num - segment_index)
        forward_own_part = lax.dynamic_slice_in_dim(tokens, forward_start_row, micro_rows, 0)
        forward_layer_in = jnp.where(segment_index == 0, forward_own_part, incoming)
        forward_ids_part = lax.dynamic_slice_in_dim(layer_ids, forward_start_row, micro_rows, 0)
        gates_part = lax.dynamic_slice_in_dim(layer_gates, forward_start_row, micro_rows, 0)
        forward_x_float = forward_layer_in.astype(jnp.float32)
        forward_scale = inverse_rms(forward_x_float)
        normed = (forward_x_float * forward_scale * gain_row).astype(jnp.bfloat16)
        forward_onehot, forward_placing = route_tables(forward_ids_part, owners, capacity)
        row_block = jnp.einsum(
            "okr,rd->okd", forward_placing, normed, preferred_element_type=jnp.float32
        ).astype(jnp.bfloat16)
        pair_block = gate_slots(forward_onehot, gates_part, forward_placing, experts_here)
        f_valid, f_pick, layer_in, x_float, f_placing, row_block, pair_block = (
            forward_is_valid,
            forward_slot_pick,
            forward_layer_in,
            forward_x_float,
            forward_placing,
            row_block,
            pair_block,
        )
        got_rows, got_pairs = send_rows(row_block, pair_block)
        flat_rows = got_rows.reshape(slot_count, width)
        flat_pairs = got_pairs.reshape(slot_count, experts_here)
        result, joint_pre = lax.cond(f_valid, run_forward, skip_forward, (flat_rows, flat_pairs))
        returned = return_rows(result.reshape(owners, capacity, width))
        branch = jnp.einsum("okr,okd->rd", f_placing, returned, preferred_element_type=jnp.float32)
        layer_out = (x_float + branch).astype(jnp.bfloat16)
        layer_outs = lax.dynamic_update_index_in_dim(layer_outs, layer_out, f_pick, 0)
        layer_ins = lax.dynamic_update_index_in_dim(layer_ins, layer_in, f_pick, 0)
        kept_joint = lax.dynamic_update_index_in_dim(kept_joint, joint_pre, f_pick, 0)
        kept_pairs = lax.dynamic_update_index_in_dim(kept_pairs, flat_pairs, f_pick, 0)
        if tick_num + 1 < ticks:
            incoming = from_behind(layer_out, "pipe", 1)
    incoming = jnp.zeros((micro_rows, width), jnp.bfloat16)
    for tick_num in range(ticks):
        backward_is_valid, backward_slot_pick, backward_start_row = timing(
            tick_num - (segments - 1 - segment_index)
        )
        own_part = lax.dynamic_slice_in_dim(cotangent, backward_start_row, micro_rows, 0)
        backward_grad_in = jnp.where(segment_index == segments - 1, own_part, incoming)
        ids_part = lax.dynamic_slice_in_dim(layer_ids, backward_start_row, micro_rows, 0)
        backward_layer_in = lax.dynamic_index_in_dim(
            layer_ins, backward_slot_pick, 0, keepdims=False
        )
        backward_x_float = backward_layer_in.astype(jnp.float32)
        backward_scale = inverse_rms(backward_x_float)
        _, backward_placing = route_tables(ids_part, owners, capacity)
        grad_block = jnp.einsum(
            "okr,rd->okd", backward_placing, backward_grad_in, preferred_element_type=jnp.float32
        ).astype(jnp.bfloat16)
        b_valid, b_pick, grad_in, bx_float, b_scale, b_placing, grad_block = (
            backward_is_valid,
            backward_slot_pick,
            backward_grad_in,
            backward_x_float,
            backward_scale,
            backward_placing,
            grad_block,
        )
        got_grads = send_grads(grad_block).reshape(slot_count, width)
        joint_keep = lax.dynamic_index_in_dim(kept_joint, b_pick, 0, keepdims=False)
        pair_keep = lax.dynamic_index_in_dim(kept_pairs, b_pick, 0, keepdims=False)
        owner_grad = lax.cond(
            b_valid, run_backward, skip_backward, (got_grads, pair_keep, joint_keep)
        )
        returned = return_grads(owner_grad.reshape(owners, capacity, width))
        normed_grad = jnp.einsum(
            "okr,okd->rd", b_placing, returned, preferred_element_type=jnp.float32
        )
        weighted = gain_row * normed_grad
        grad_x = (
            grad_in.astype(jnp.float32)
            + b_scale * weighted
            - bx_float
            * b_scale
            * b_scale
            * b_scale
            * jnp.mean(weighted * bx_float, axis=-1, keepdims=True)
        )
        gain_term = jnp.where(b_valid, jnp.sum(normed_grad * bx_float * b_scale, axis=0), 0.0)
        grad_bf, gain_term = (grad_x.astype(jnp.bfloat16), gain_term)
        grad_outs = lax.dynamic_update_index_in_dim(grad_outs, grad_bf, b_pick, 0)
        gain_sum = gain_sum + gain_term
        if tick_num + 1 < ticks:
            incoming = from_behind(grad_bf, "pipe", -1)
    gain_grad = lax.psum(gain_sum, ("dp", "expert"))
    segment_out = layer_outs[:MICRO].reshape(1, tok_rows, width)
    segment_grad = grad_outs[:MICRO].reshape(1, tok_rows, width)
    return (segment_out, segment_grad, gain_grad.reshape(1, width))


def swap_cores(value):
    count = lax.axis_size("expert")
    return lax.ppermute(value, "expert", [(e, e ^ 1) for e in range(count)])


def shifted(value, dp_step, chip_step):
    dps, experts = (lax.axis_size(name) for name in ("dp", "expert"))
    pairs = []
    for dp in range(dps):
        for expert in range(experts):
            target = (dp + dp_step) % dps * experts + (expert + 2 * chip_step) % experts
            pairs.append((dp * experts + expert, target))
    return lax.ppermute(value, ("dp", "expert"), pairs)


def hopped(value, step):
    stages = lax.axis_size("pipe")
    return lax.ppermute(value, "pipe", [(s, (s + step) % stages) for s in range(stages)])


def chip_steps():
    dps, chips = lax.axis_size("dp"), lax.axis_size("expert") // 2
    steps = [(d, c) for d in range(dps) for c in range(chips)]
    return sorted(steps[1:], key=lambda step: -(step[0] + step[1]))


def spread(rows):
    return [rows] + [shifted(rows, d, c) for d, c in chip_steps()]


def returned(blocks, which):
    dps, chips = lax.axis_size("dp"), lax.axis_size("expert") // 2
    dp, chip = chip_steps()[which - 1]
    return shifted(blocks[which], -dp % dps, -chip % chips)


def collect(blocks):
    return [blocks[0]] + [returned(blocks, which) for which in range(1, len(blocks))]


VMEM = pl.BlockSpec(memory_space=pltpu.VMEM)
CHUNK = 256
LANES = 128
HALVES = 2


def in_vmem(kernel, outs, scratch, flops, *operands, specs=None):
    moved = sum(math.prod(a.shape) * a.dtype.itemsize for a in [*outs, *operands])
    return pl.pallas_call(
        kernel,
        out_shape=outs,
        in_specs=specs or [VMEM] * len(operands),
        out_specs=[VMEM] * len(outs),
        scratch_shapes=scratch,
        compiler_params=pltpu.CompilerParams(vmem_limit_bytes=LIMIT),
        cost_estimate=pl.CostEstimate(flops=flops, bytes_accessed=moved, transcendentals=0),
    )(*operands)


def load_kernel(*refs):
    own, pair, outs, sems = refs[:3], refs[3:6], refs[6:10], refs[10]
    ff = own[0].shape[1]
    copies = []
    for e, (gate_ref, up_ref, down_ref) in enumerate((own, pair)):
        copies += [
            pltpu.make_async_copy(gate_ref, outs[e].at[:, :ff], sems.at[3 * e]),
            pltpu.make_async_copy(up_ref, outs[e].at[:, ff:], sems.at[3 * e + 1]),
            pltpu.make_async_copy(down_ref, outs[2 + e], sems.at[3 * e + 2]),
        ]
    for copy in copies:
        copy.start()
    for copy in copies:
        copy.wait()


def loaded(own, pair):
    gate, _, down = own
    joint, down = pltpu.VMEM((gate.shape[0], 2 * gate.shape[1]), gate.dtype), pltpu.VMEM(down.shape, down.dtype)
    specs = [pl.BlockSpec(memory_space=pltpu.HBM)] * 3 + [pl.BlockSpec(memory_space=pl.ANY)] * 3
    scratch = [pltpu.SemaphoreType.DMA((6,))]
    return in_vmem(load_kernel, [joint, joint, down, down], scratch, 0, *own, *pair, specs=specs)


def stage_kernel(out_ref):
    out_ref[...] = jnp.full(out_ref.shape, lax.axis_index("pipe"), jnp.int32)


def first_rows_kernel(token_ref, id_ref, gate_ref, out_ref, copied, sem):
    rows, width = copied.shape
    copy = pltpu.make_async_copy(token_ref.at[pl.ds(0, rows), :], copied, sem)
    copy.start()
    owners = lax.axis_size("dp") * lax.axis_size("expert")
    column = lax.broadcasted_iota(jnp.int32, (rows, out_ref.shape[1] - width), 1)
    table = jnp.zeros(column.shape, jnp.float32)
    for micro in range(MICRO):
        window = slice(micro * rows, (micro + 1) * rows)
        gates = gate_ref[window, :].astype(jnp.float32)
        for slot in range(id_ref.shape[1]):
            place = micro * owners + id_ref[window, slot:slot + 1]
            table = table + jnp.where(column == place, gates[:, slot:slot + 1], 0.0)
    out_ref[:, width:] = table.astype(jnp.bfloat16)
    copy.wait()
    out_ref[:, :width] = copied[...]


def first_rows(tokens, ids, gates):
    rows, width = tokens.shape[0] // MICRO, tokens.shape[1]
    owners = lax.axis_size("dp") * lax.axis_size("expert")
    extra = -(-MICRO * owners // LANES) * LANES
    outs = [jax.ShapeDtypeStruct((rows, width + extra), tokens.dtype)]
    scratch = [pltpu.VMEM((rows, width), tokens.dtype), pltpu.SemaphoreType.DMA]
    specs = [pl.BlockSpec(memory_space=pl.ANY), VMEM, VMEM]
    return in_vmem(first_rows_kernel, outs, scratch, 0, tokens, ids, gates, specs=specs)[0]


def turn_kernel(in_ref, out_ref):
    size = math.gcd(in_ref.shape[0], CHUNK)

    @pl.loop(0, in_ref.shape[0] // size)
    def _(at):
        window = pl.ds(pl.multiple_of(at * size, size), size)
        out_ref[:, window] = in_ref[window, :].T


def turned(part):
    outs = [pltpu.VMEM(part.shape[::-1], part.dtype)]
    return in_vmem(turn_kernel, outs, [], 0, part)[0]


def in_chunks(width):
    half = width // HALVES

    def run(work):
        @pl.loop(0, HALVES)
        def _(at):
            for start in range(0, half, CHUNK):
                work(pl.ds(pl.multiple_of(at * half + start, CHUNK), CHUNK))

    return run


def owner_number():
    return lax.axis_index("dp") * lax.axis_size("expert") + lax.axis_index("expert")


def forward_kernel(blocks, tick, *refs):
    row_refs, table_refs, refs = refs[:blocks], refs[blocks:2 * blocks], refs[2 * blocks:]
    gain_ref, *weight_refs = refs[:5]
    rate_ref, flat_ref, own_ref, *part_refs, pre, hidden = refs[5:]
    rows, width = own_ref.shape
    ff = weight_refs[2].shape[0]
    gain = gain_ref[...]
    for k, row_ref in enumerate(row_refs):
        x = row_ref[:, :width].astype(jnp.float32)
        flat_ref[k * rows:(k + 1) * rows, :] = (x * inverse_rms(x) * gain).astype(jnp.bfloat16)
    micro = tick - lax.axis_index("pipe")
    is_valid = (micro >= 0) & (micro < MICRO)
    routed = jnp.concatenate([ref[:, width:] for ref in table_refs], axis=0).astype(jnp.float32)
    column = lax.broadcasted_iota(jnp.int32, routed.shape, 1)
    me, owners = owner_number(), lax.axis_size("dp") * lax.axis_size("expert")
    for e, owner in enumerate((me, me ^ 1)):
        is_routed = (column == micro * owners + owner) & is_valid
        weight = jnp.sum(jnp.where(is_routed, routed, 0.0), axis=1, keepdims=True)
        for start in range(0, 2 * ff, CHUNK):
            pre[:, start:start + CHUNK] = jnp.dot(
                flat_ref[...], weight_refs[e][:, start:start + CHUNK], preferred_element_type=jnp.float32
            )
        gate_pre, up_pre = pre[:, :ff], pre[:, ff:]
        sigma = jax.nn.sigmoid(gate_pre)
        up_rate = weight * gate_pre * sigma
        hidden[:, e * ff:(e + 1) * ff] = (up_rate * up_pre).astype(jnp.bfloat16)
        rate_ref[:, 2 * e * ff:(2 * e + 1) * ff] = weight * up_pre * sigma * (1.0 + gate_pre * (1.0 - sigma))
        rate_ref[:, (2 * e + 1) * ff:(2 * e + 2) * ff] = up_rate

    @in_chunks(width)
    def _(columns):
        partial = sum(
            jnp.dot(hidden[:, e * ff:(e + 1) * ff], weight_refs[2 + e][:, columns], preferred_element_type=jnp.float32)
            for e in range(2)
        )
        own_ref[:, columns] = row_refs[0][:, columns].astype(jnp.float32) + partial[:rows]
        for k, part_ref in enumerate(part_refs):
            part_ref[:, columns] = partial[(k + 1) * rows:(k + 2) * rows].astype(jnp.bfloat16)


def backward_kernel(blocks, first, picks, saves, *refs):
    row_refs, refs = refs[:blocks], refs[blocks:]
    rate_refs, normed_refs, refs = refs[:saves], refs[saves:2 * saves], refs[2 * saves:]
    weight_refs, (gain_ref, own_ref, *part_refs, flat, rate, normed, hidden, sems) = refs[:4], refs[4:]
    rows, width = row_refs[0].shape
    ff = weight_refs[2].shape[1]
    stage = lax.axis_index("pipe")

    def copies(at):
        return (
            pltpu.make_async_copy(rate_refs[at], rate, sems.at[0]),
            pltpu.make_async_copy(normed_refs[at], normed, sems.at[1]),
        )

    for at in range(saves):
        holders = [s for s, picked in enumerate(picks) if picked == at]

        @pl.when(functools.reduce(jnp.logical_or, [stage == s for s in holders]))
        def _():
            for copy in copies(at):
                copy.start()

    for k, row_ref in enumerate(row_refs):
        flat[k * rows:(k + 1) * rows, :] = row_ref[...]
    micro = first + stage
    kept = jnp.where((micro >= 0) & (micro < MICRO), 1.0, 0.0)
    for e in range(2):
        q = jnp.dot(flat[...], weight_refs[2 + e][...], preferred_element_type=jnp.float32) * kept
        if e == 0:
            for copy in copies(0):
                copy.wait()
        for half in range(2):
            columns = slice((2 * e + half) * ff, (2 * e + half + 1) * ff)
            hidden[:, columns] = (q * rate[:, columns]).astype(jnp.bfloat16)

    @in_chunks(width)
    def _(columns):
        partial = sum(
            jnp.dot(
                hidden[:, 2 * e * ff:(2 * e + 2) * ff], weight_refs[e][:, columns], preferred_element_type=jnp.float32
            )
            for e in range(2)
        )
        gain_ref[:, columns] = jnp.sum(partial * normed[:, columns].astype(jnp.float32), axis=0, keepdims=True)
        own_ref[:, columns] = partial[:rows]
        for k, part_ref in enumerate(part_refs):
            part_ref[:, columns] = partial[(k + 1) * rows:(k + 2) * rows].astype(jnp.bfloat16)


def forward_experts(tick, row_blocks, tables, gain, weights):
    blocks, rows, width = len(row_blocks), row_blocks[0].shape[0], gain.shape[1]
    total, ff = blocks * rows, weights[2].shape[0]
    outs = [
        jax.ShapeDtypeStruct((total, 4 * ff), jnp.float32),
        jax.ShapeDtypeStruct((total, width), jnp.bfloat16),
        jax.ShapeDtypeStruct((rows, width), jnp.float32),
    ]
    outs += [jax.ShapeDtypeStruct((rows, width), jnp.bfloat16)] * (blocks - 1)
    scratch = [pltpu.VMEM((total, 2 * ff), jnp.float32), pltpu.VMEM((total, 2 * ff), jnp.bfloat16)]
    kernel = functools.partial(forward_kernel, blocks, tick)
    flops = 12 * total * width * ff
    rate, normed, *parts = in_vmem(kernel, outs, scratch, flops, *row_blocks, *tables, gain, *weights)
    return rate, normed, parts


def backward_experts(first, picks, row_blocks, rates, normeds, weights):
    blocks, (rows, width) = len(row_blocks), row_blocks[0].shape
    total, wide = rates[0].shape
    outs = [jax.ShapeDtypeStruct((1, width), jnp.float32), jax.ShapeDtypeStruct((rows, width), jnp.float32)]
    outs += [jax.ShapeDtypeStruct((rows, width), jnp.bfloat16)] * (blocks - 1)
    scratch = [
        pltpu.VMEM((total, width), jnp.bfloat16),
        pltpu.VMEM((total, wide), jnp.float32),
        pltpu.VMEM((total, width), jnp.bfloat16),
        pltpu.VMEM((total, wide), jnp.bfloat16),
        pltpu.SemaphoreType.DMA((2,)),
    ]
    used = sorted(set(picks))
    kernel = functools.partial(backward_kernel, blocks, first, [used.index(at) for at in picks], len(used))
    anywhere = pl.BlockSpec(memory_space=pl.ANY)
    specs = [VMEM] * blocks + [anywhere] * (2 * len(used)) + [VMEM] * 4
    saved = [rates[at] for at in used] + [normeds[at] for at in used]
    flops = 3 * total * width * wide
    gained, *parts = in_vmem(kernel, outs, scratch, flops, *row_blocks, *saved, *weights, specs=specs)
    return gained, parts


def summed_over_owners(value):
    value = value + swap_cores(value)
    return sum(spread(value))


def dense_body(tokens, cotangent, owner_ids, gate_weights, norm_gain, w_gate, w_up, w_down):
    f32, bf16 = jnp.float32, jnp.bfloat16
    stages = lax.axis_size("pipe")
    tok_rows, width = tokens.shape
    rows = tok_rows // MICRO
    gain = norm_gain[0][None, :]
    ticks = MICRO + stages - 1
    stage = in_vmem(stage_kernel, [jax.ShapeDtypeStruct((1, width), jnp.int32)], [], 0)[0]

    own = [pltpu.with_memory_space_constraint(w[0, 0], pltpu.HBM) for w in (w_gate, w_up, w_down)]
    theirs = [swap_cores(w) for w in own]
    forward_weights = loaded(own, theirs)
    backward_weights = []
    for number, part in enumerate(forward_weights):
        backward_weights.append(turned(part))

    def choose(values):
        found = values[0]
        for s, value in enumerate(values):
            if value is not found:
                found = jnp.where(stage == s, value, found)
        return found

    rates, normeds, ins, outs, grads = [], [], [], [], []
    gain_sum = jnp.zeros((1, width), f32)
    behind = ahead = None
    last = ticks + stages - 2
    for tick in range(last + 1):
        if tick < ticks:
            if tick == 0:
                here = first_rows(tokens, owner_ids[0], gate_weights[0])
            elif tick < MICRO:
                here = jnp.where(stage == 0, tokens[tick * rows:(tick + 1) * rows], behind)
            else:
                here = behind
            here_blocks = spread(here)
            if tick == 0:
                tables = here_blocks
            rate, normed, parts = forward_experts(tick, here_blocks, tables, gain, forward_weights)
            rates.append(rate)
            normeds.append(normed)
            ins.append(here[:, :width])
            if tick + 1 < ticks:
                parts = collect(parts)
                outs.append(lax.optimization_barrier(sum(p.astype(f32) for p in parts).astype(bf16)))
                behind = hopped(outs[-1], 1)
        number = tick - (stages - 1)
        if number >= 0:
            first = number - (stages - 1)
            picks = [min(max(first + 2 * s, 0), min(ticks - 1, tick)) for s in range(stages)]
            if number == 0:
                grad = cotangent[:rows]
            elif number < MICRO:
                grad = jnp.where(stage == stages - 1, cotangent[number * rows:(number + 1) * rows], ahead)
            else:
                grad = ahead
            grad_blocks = spread(grad)
            gained, sums = backward_experts(first, picks, grad_blocks, rates, normeds, backward_weights)
            sums = collect(sums)
            normed_grad = sum(p.astype(f32) for p in sums)
            x = choose([ins[at] for at in picks]).astype(f32)
            scale = inverse_rms(x)
            weighted = gain * normed_grad
            grad_x = (
                grad.astype(f32)
                + scale * weighted
                - x * scale * scale * scale * jnp.mean(weighted * x, axis=-1, keepdims=True)
            ).astype(bf16)
            gain_sum = gain_sum + gained
            if tick < last:
                grad_x = lax.optimization_barrier(grad_x)
            grads.append(grad_x)
            if tick < last:
                ahead = hopped(grad_x, -1)
            if tick + 1 == ticks:
                waiting, kept = parts, parts[:1]
            while tick + 1 >= ticks and len(kept) < len(waiting) and (tick - ticks + 2 >= len(kept) or tick + 1 == last):
                kept.append(returned(lax.optimization_barrier((waiting, grad_x))[0], len(kept)))
    outs.append(sum(part.astype(f32) for part in kept).astype(bf16))
    gain_grad = summed_over_owners(gain_sum) / gain
    segment_out = jnp.concatenate([choose([outs[m + s] for s in range(stages)]) for m in range(MICRO)])
    segment_grad = jnp.concatenate(
        [choose([grads[m + stages - 1 - s] for s in range(stages)]) for m in range(MICRO)]
    )
    return (segment_out[None], segment_grad[None], gain_grad)


def body(tokens, cotangent, owner_ids, *rest):
    owners = lax.axis_size("dp") * lax.axis_size("expert")
    routed_densely = owners <= 2 * owner_ids.shape[2] and lax.axis_size("expert") % 2 == 0
    plan = dense_body if routed_densely else slot_body
    return plan(tokens, cotangent, owner_ids, *rest)


def solution(mesh):
    in_specs = (
        P(("dp", "expert"), None),
        P(("dp", "expert"), None),
        P("pipe", ("dp", "expert"), None),
        P("pipe", ("dp", "expert"), None),
        P("pipe", None),
        P("pipe", ("dp", "expert"), None, None),
        P("pipe", ("dp", "expert"), None, None),
        P("pipe", ("dp", "expert"), None, None),
    )
    out_specs = (
        P("pipe", ("dp", "expert"), None),
        P("pipe", ("dp", "expert"), None),
        P("pipe", None),
    )
    return jax.shard_map(body, mesh=mesh, in_specs=in_specs, out_specs=out_specs, check_vma=False)
```

```python
import jax
import jax.numpy as jnp
from jax import lax
from jax.experimental import pallas as pl
from jax.experimental.pallas import tpu as pltpu
import functools
import math
from jax.sharding import PartitionSpec as P

MICRO = 4
LIMIT = 12 * 1024 * 1024


epsilon = 1e-06


def from_behind(value, axis, steps):
    count = lax.axis_size(axis)
    leading, last = (max(0, -steps), min(count, count - steps))
    return lax.ppermute(value, axis, [(source, source + steps) for source in range(leading, last)])


def inverse_rms(values):
    return lax.rsqrt(jnp.mean(values * values, axis=-1, keepdims=True) + epsilon)


def contract_last(left, right):
    return lax.dot_general(
        left, right, (((1,), (1,)), ((), ())), preferred_element_type=jnp.float32
    )


def route_tables(ids_part, owners, capacity):
    owner_range = jnp.arange(owners, dtype=jnp.int32)
    onehot = (ids_part[:, :, None] == owner_range[None, None, :]).astype(jnp.int32)
    member = jnp.sum(onehot, axis=1)
    position = jnp.cumsum(member, axis=0) - member
    slot_range = jnp.arange(capacity, dtype=jnp.int32)
    placed = (position[:, :, None] == slot_range[None, None, :]) & (member[:, :, None] > 0)
    placing = jnp.transpose(placed, (1, 2, 0)).astype(jnp.bfloat16)
    return (onehot.astype(jnp.float32), placing)


def gate_slots(onehot, gates_part, placing, experts_here):
    gate_pairs = gates_part.astype(jnp.float32).reshape(gates_part.shape[0], -1, experts_here)
    chosen = jnp.einsum("rjo,rjc->roc", onehot, gate_pairs)
    return jnp.einsum("okr,roc->okc", placing.astype(jnp.float32), chosen).astype(jnp.bfloat16)


def send_rows(row_block, pair_block):
    got_rows, got_pairs = (
        lax.all_to_all(row_block, ("dp", "expert"), split_axis=0, concat_axis=0, tiled=True),
        lax.all_to_all(pair_block, ("dp", "expert"), split_axis=0, concat_axis=0, tiled=True),
    )
    return (got_rows, got_pairs)


def return_rows(row_block):
    return lax.all_to_all(row_block, ("dp", "expert"), split_axis=0, concat_axis=0, tiled=True)


def send_grads(row_block):
    return lax.all_to_all(row_block, ("dp", "expert"), split_axis=0, concat_axis=0, tiled=True)


def return_grads(row_block):
    return lax.all_to_all(row_block, ("dp", "expert"), split_axis=0, concat_axis=0, tiled=True)


def expert_forward(flat_rows, flat_pairs, joint_mats, down_mats):
    hidden_width = down_mats.shape[1]
    joint_pre = jnp.dot(flat_rows, joint_mats[0], preferred_element_type=jnp.float32)
    gate_pre = joint_pre[:, :hidden_width]
    up_pre = joint_pre[:, hidden_width:]
    hidden = (jax.nn.silu(gate_pre) * up_pre).astype(jnp.bfloat16)
    projected = jnp.dot(hidden, down_mats[0], preferred_element_type=jnp.float32)
    term = flat_pairs.astype(jnp.float32) * projected
    kept_both = [joint_pre]
    return (term.astype(jnp.bfloat16), jnp.stack(kept_both))


def expert_backward(grad_rows, flat_pairs, joint_keep, joint_mats, down_mats):
    hidden_width = down_mats.shape[1]
    q_vals = contract_last(grad_rows, down_mats[0])
    gate_pre = joint_keep[0][:, :hidden_width]
    up_pre = joint_keep[0][:, hidden_width:]
    sigma = jax.nn.sigmoid(gate_pre)
    weight = flat_pairs.astype(jnp.float32)
    d_gate = (q_vals * weight * up_pre * sigma * (1.0 + gate_pre * (1.0 - sigma))).astype(
        jnp.bfloat16
    )
    d_up = (q_vals * weight * gate_pre * sigma).astype(jnp.bfloat16)
    joint_grad = jnp.concatenate([d_gate, d_up], axis=1)
    term = contract_last(joint_grad, joint_mats[0])
    return term.astype(jnp.bfloat16)


def slot_body(tokens, cotangent, owner_ids, gate_weights, norm_gain, w_gate, w_up, w_down):
    segments = lax.axis_size("pipe")
    segment_index = lax.axis_index("pipe")
    owners = lax.axis_size("dp") * lax.axis_size("expert")
    tok_rows = tokens.shape[0]
    width = tokens.shape[1]
    micro_rows = tok_rows // MICRO
    route_count = owner_ids.shape[2]
    capacity = max(2, (5 * micro_rows * route_count + 4 * owners - 1) // (4 * owners))
    slot_count = owners * capacity
    gain_row = norm_gain[0]
    joint_mats = jnp.concatenate([w_gate[0], w_up[0]], axis=2)
    down_mats = w_down[0]
    layer_ids = owner_ids[0]
    layer_gates = gate_weights[0]
    experts_here = joint_mats.shape[0]
    joint_width = joint_mats.shape[2]

    def skip_forward(operands):
        return (
            jnp.zeros((slot_count, width), jnp.bfloat16),
            jnp.zeros((experts_here, slot_count, joint_width), jnp.float32),
        )

    def run_forward(operands):
        return expert_forward(operands[0], operands[1], joint_mats, down_mats)

    def skip_backward(operands):
        return jnp.zeros((slot_count, width), jnp.bfloat16)

    def run_backward(operands):
        return expert_backward(operands[0], operands[1], operands[2], joint_mats, down_mats)

    def timing(micro):
        is_valid = (micro >= 0) & (micro < MICRO)
        slot_pick = jnp.where(is_valid, micro, MICRO)
        start_row = jnp.clip(micro, 0, MICRO - 1) * micro_rows
        return (is_valid, slot_pick, start_row)

    layer_outs = jnp.zeros((MICRO + 1, micro_rows, width), jnp.bfloat16)
    layer_ins = jnp.zeros((MICRO + 1, micro_rows, width), jnp.bfloat16)
    kept_joint = jnp.zeros((MICRO + 1, experts_here, slot_count, joint_width), jnp.float32)
    kept_pairs = jnp.zeros((MICRO + 1, slot_count, experts_here), jnp.bfloat16)
    grad_outs = jnp.zeros((MICRO + 1, micro_rows, width), jnp.bfloat16)
    gain_sum = jnp.zeros((width,), jnp.float32)
    ticks = MICRO + segments - 1
    incoming = jnp.zeros((micro_rows, width), jnp.bfloat16)
    for tick_num in range(ticks):
        forward_is_valid, forward_slot_pick, forward_start_row = timing(tick_num - segment_index)
        forward_own_part = lax.dynamic_slice_in_dim(tokens, forward_start_row, micro_rows, 0)
        forward_layer_in = jnp.where(segment_index == 0, forward_own_part, incoming)
        forward_ids_part = lax.dynamic_slice_in_dim(layer_ids, forward_start_row, micro_rows, 0)
        gates_part = lax.dynamic_slice_in_dim(layer_gates, forward_start_row, micro_rows, 0)
        forward_x_float = forward_layer_in.astype(jnp.float32)
        forward_scale = inverse_rms(forward_x_float)
        normed = (forward_x_float * forward_scale * gain_row).astype(jnp.bfloat16)
        forward_onehot, forward_placing = route_tables(forward_ids_part, owners, capacity)
        row_block = jnp.einsum(
            "okr,rd->okd", forward_placing, normed, preferred_element_type=jnp.float32
        ).astype(jnp.bfloat16)
        pair_block = gate_slots(forward_onehot, gates_part, forward_placing, experts_here)
        f_valid, f_pick, layer_in, x_float, f_placing, row_block, pair_block = (
            forward_is_valid,
            forward_slot_pick,
            forward_layer_in,
            forward_x_float,
            forward_placing,
            row_block,
            pair_block,
        )
        got_rows, got_pairs = send_rows(row_block, pair_block)
        flat_rows = got_rows.reshape(slot_count, width)
        flat_pairs = got_pairs.reshape(slot_count, experts_here)
        result, joint_pre = lax.cond(f_valid, run_forward, skip_forward, (flat_rows, flat_pairs))
        returned = return_rows(result.reshape(owners, capacity, width))
        branch = jnp.einsum("okr,okd->rd", f_placing, returned, preferred_element_type=jnp.float32)
        layer_out = (x_float + branch).astype(jnp.bfloat16)
        layer_outs = lax.dynamic_update_index_in_dim(layer_outs, layer_out, f_pick, 0)
        layer_ins = lax.dynamic_update_index_in_dim(layer_ins, layer_in, f_pick, 0)
        kept_joint = lax.dynamic_update_index_in_dim(kept_joint, joint_pre, f_pick, 0)
        kept_pairs = lax.dynamic_update_index_in_dim(kept_pairs, flat_pairs, f_pick, 0)
        if tick_num + 1 < ticks:
            incoming = from_behind(layer_out, "pipe", 1)
    incoming = jnp.zeros((micro_rows, width), jnp.bfloat16)
    for tick_num in range(ticks):
        backward_is_valid, backward_slot_pick, backward_start_row = timing(
            tick_num - (segments - 1 - segment_index)
        )
        own_part = lax.dynamic_slice_in_dim(cotangent, backward_start_row, micro_rows, 0)
        backward_grad_in = jnp.where(segment_index == segments - 1, own_part, incoming)
        ids_part = lax.dynamic_slice_in_dim(layer_ids, backward_start_row, micro_rows, 0)
        backward_layer_in = lax.dynamic_index_in_dim(
            layer_ins, backward_slot_pick, 0, keepdims=False
        )
        backward_x_float = backward_layer_in.astype(jnp.float32)
        backward_scale = inverse_rms(backward_x_float)
        _, backward_placing = route_tables(ids_part, owners, capacity)
        grad_block = jnp.einsum(
            "okr,rd->okd", backward_placing, backward_grad_in, preferred_element_type=jnp.float32
        ).astype(jnp.bfloat16)
        b_valid, b_pick, grad_in, bx_float, b_scale, b_placing, grad_block = (
            backward_is_valid,
            backward_slot_pick,
            backward_grad_in,
            backward_x_float,
            backward_scale,
            backward_placing,
            grad_block,
        )
        got_grads = send_grads(grad_block).reshape(slot_count, width)
        joint_keep = lax.dynamic_index_in_dim(kept_joint, b_pick, 0, keepdims=False)
        pair_keep = lax.dynamic_index_in_dim(kept_pairs, b_pick, 0, keepdims=False)
        owner_grad = lax.cond(
            b_valid, run_backward, skip_backward, (got_grads, pair_keep, joint_keep)
        )
        returned = return_grads(owner_grad.reshape(owners, capacity, width))
        normed_grad = jnp.einsum(
            "okr,okd->rd", b_placing, returned, preferred_element_type=jnp.float32
        )
        weighted = gain_row * normed_grad
        grad_x = (
            grad_in.astype(jnp.float32)
            + b_scale * weighted
            - bx_float
            * b_scale
            * b_scale
            * b_scale
            * jnp.mean(weighted * bx_float, axis=-1, keepdims=True)
        )
        gain_term = jnp.where(b_valid, jnp.sum(normed_grad * bx_float * b_scale, axis=0), 0.0)
        grad_bf, gain_term = (grad_x.astype(jnp.bfloat16), gain_term)
        grad_outs = lax.dynamic_update_index_in_dim(grad_outs, grad_bf, b_pick, 0)
        gain_sum = gain_sum + gain_term
        if tick_num + 1 < ticks:
            incoming = from_behind(grad_bf, "pipe", -1)
    gain_grad = lax.psum(gain_sum, ("dp", "expert"))
    segment_out = layer_outs[:MICRO].reshape(1, tok_rows, width)
    segment_grad = grad_outs[:MICRO].reshape(1, tok_rows, width)
    return (segment_out, segment_grad, gain_grad.reshape(1, width))


def swap_cores(value):
    count = lax.axis_size("expert")
    return lax.ppermute(value, "expert", [(e, e ^ 1) for e in range(count)])


def shifted(value, dp_step, chip_step):
    dps, experts = (lax.axis_size(name) for name in ("dp", "expert"))
    pairs = []
    for dp in range(dps):
        for expert in range(experts):
            target = (dp + dp_step) % dps * experts + (expert + 2 * chip_step) % experts
            pairs.append((dp * experts + expert, target))
    return lax.ppermute(value, ("dp", "expert"), pairs)


def hopped(value, step):
    stages = lax.axis_size("pipe")
    return lax.ppermute(value, "pipe", [(s, (s + step) % stages) for s in range(stages)])


def chip_steps():
    dps, chips = lax.axis_size("dp"), lax.axis_size("expert") // 2
    steps = [(d, c) for d in range(dps) for c in range(chips)]
    return sorted(steps[1:], key=lambda step: -(step[0] + step[1]))


def spread(rows):
    return [rows] + [shifted(rows, d, c) for d, c in chip_steps()]


def returned(blocks, which):
    dps, chips = lax.axis_size("dp"), lax.axis_size("expert") // 2
    dp, chip = chip_steps()[which - 1]
    return shifted(blocks[which], -dp % dps, -chip % chips)


def collect(blocks):
    return [blocks[0]] + [returned(blocks, which) for which in range(1, len(blocks))]


VMEM = pl.BlockSpec(memory_space=pltpu.VMEM)
CHUNK = 256
LANES = 128
HALVES = 2


def in_vmem(kernel, outs, scratch, flops, *operands, specs=None):
    moved = sum(math.prod(a.shape) * a.dtype.itemsize for a in [*outs, *operands])
    return pl.pallas_call(
        kernel,
        out_shape=outs,
        in_specs=specs or [VMEM] * len(operands),
        out_specs=[VMEM] * len(outs),
        scratch_shapes=scratch,
        compiler_params=pltpu.CompilerParams(vmem_limit_bytes=LIMIT),
        cost_estimate=pl.CostEstimate(flops=flops, bytes_accessed=moved, transcendentals=0),
    )(*operands)


def load_kernel(gate_ref, up_ref, down_ref, joint_out, down_out, sems):
    ff = gate_ref.shape[1]
    copies = [
        pltpu.make_async_copy(gate_ref, joint_out.at[:, :ff], sems.at[0]),
        pltpu.make_async_copy(up_ref, joint_out.at[:, ff:], sems.at[1]),
        pltpu.make_async_copy(down_ref, down_out, sems.at[2]),
    ]
    for copy in copies:
        copy.start()
    for copy in copies:
        copy.wait()


def loaded(gate, up, down):
    outs = [pltpu.VMEM((gate.shape[0], 2 * gate.shape[1]), gate.dtype), pltpu.VMEM(down.shape, down.dtype)]
    specs = [pl.BlockSpec(memory_space=pl.ANY)] * 3
    return in_vmem(load_kernel, outs, [pltpu.SemaphoreType.DMA((3,))], 0, gate, up, down, specs=specs)


def stage_kernel(out_ref):
    out_ref[...] = jnp.full(out_ref.shape, lax.axis_index("pipe"), jnp.int32)


def first_rows_kernel(token_ref, id_hbm, gate_hbm, out_ref, copied, id_ref, gate_ref, sems):
    rows, width = copied.shape
    copy = pltpu.make_async_copy(token_ref.at[pl.ds(0, rows), :], copied, sems.at[0])
    id_copy = pltpu.make_async_copy(id_hbm, id_ref, sems.at[1])
    gate_copy = pltpu.make_async_copy(gate_hbm, gate_ref, sems.at[2])
    for each in (id_copy, gate_copy, copy):
        each.start()
    owners = lax.axis_size("dp") * lax.axis_size("expert")
    column = lax.broadcasted_iota(jnp.int32, (rows, out_ref.shape[1] - width), 1)
    table = jnp.zeros(column.shape, jnp.float32)
    id_copy.wait()
    gate_copy.wait()
    ids, gates = id_ref[...].T, gate_ref[...].astype(jnp.float32).T
    for micro in range(MICRO):
        window = slice(micro * rows, (micro + 1) * rows)
        for slot in range(ids.shape[1]):
            place = micro * owners + ids[window, slot:slot + 1]
            table = table + jnp.where(column == place, gates[window, slot:slot + 1], 0.0)
    out_ref[:, width:] = table.astype(jnp.bfloat16)
    copy.wait()
    out_ref[:, :width] = copied[...]


def first_rows(tokens, ids, gates):
    rows, width = tokens.shape[0] // MICRO, tokens.shape[1]
    owners = lax.axis_size("dp") * lax.axis_size("expert")
    extra = -(-MICRO * owners // LANES) * LANES
    outs = [jax.ShapeDtypeStruct((rows, width + extra), tokens.dtype)]
    scratch = [pltpu.VMEM((rows, width), tokens.dtype), pltpu.VMEM(ids.shape, ids.dtype)]
    scratch += [pltpu.VMEM(gates.shape, gates.dtype), pltpu.SemaphoreType.DMA((3,))]
    specs = [pl.BlockSpec(memory_space=pl.ANY)] * 3
    tokens, ids, gates = (pltpu.with_memory_space_constraint(value, pltpu.HBM) for value in (tokens, ids, gates))
    return in_vmem(first_rows_kernel, outs, scratch, 0, tokens, ids, gates, specs=specs)[0]


def turn_kernel(in_ref, out_ref):
    size = math.gcd(in_ref.shape[0], CHUNK)

    @pl.loop(0, in_ref.shape[0] // size)
    def _(at):
        window = pl.ds(pl.multiple_of(at * size, size), size)
        out_ref[:, window] = in_ref[window, :].T


def turned(part):
    outs = [pltpu.VMEM(part.shape[::-1], part.dtype)]
    return in_vmem(turn_kernel, outs, [], 0, part)[0]


def in_chunks(width):
    half = width // HALVES

    def run(work):
        @pl.loop(0, HALVES)
        def _(at):
            for start in range(0, half, CHUNK):
                work(pl.ds(pl.multiple_of(at * half + start, CHUNK), CHUNK))

    return run


def owner_number():
    return lax.axis_index("dp") * lax.axis_size("expert") + lax.axis_index("expert")


def forward_kernel(blocks, tick, *refs):
    row_refs, table_refs, refs = refs[:blocks], refs[blocks:2 * blocks], refs[2 * blocks:]
    gain_ref, *weight_refs = refs[:5]
    rate_ref, flat_ref, own_ref, *part_refs, pre, hidden = refs[5:]
    rows, width = own_ref.shape
    ff = weight_refs[2].shape[0]
    gain = gain_ref[...]
    for k, row_ref in enumerate(row_refs):
        x = row_ref[:, :width].astype(jnp.float32)
        flat_ref[k * rows:(k + 1) * rows, :] = (x * inverse_rms(x) * gain).astype(jnp.bfloat16)
    micro = tick - lax.axis_index("pipe")
    is_valid = (micro >= 0) & (micro < MICRO)
    routed = jnp.concatenate([ref[:, width:] for ref in table_refs], axis=0).astype(jnp.float32)
    column = lax.broadcasted_iota(jnp.int32, routed.shape, 1)
    me, owners = owner_number(), lax.axis_size("dp") * lax.axis_size("expert")
    for e, owner in enumerate((me, me ^ 1)):
        is_routed = (column == micro * owners + owner) & is_valid
        weight = jnp.sum(jnp.where(is_routed, routed, 0.0), axis=1, keepdims=True)
        for start in range(0, 2 * ff, CHUNK):
            pre[:, start:start + CHUNK] = jnp.dot(
                flat_ref[...], weight_refs[e][:, start:start + CHUNK], preferred_element_type=jnp.float32
            )
        gate_pre, up_pre = pre[:, :ff], pre[:, ff:]
        sigma = jax.nn.sigmoid(gate_pre)
        up_rate = weight * gate_pre * sigma
        hidden[:, e * ff:(e + 1) * ff] = (up_rate * up_pre).astype(jnp.bfloat16)
        rate_ref[:, 2 * e * ff:(2 * e + 1) * ff] = weight * up_pre * sigma * (1.0 + gate_pre * (1.0 - sigma))
        rate_ref[:, (2 * e + 1) * ff:(2 * e + 2) * ff] = up_rate

    @in_chunks(width)
    def _(columns):
        partial = sum(
            jnp.dot(hidden[:, e * ff:(e + 1) * ff], weight_refs[2 + e][:, columns], preferred_element_type=jnp.float32)
            for e in range(2)
        )
        own_ref[:, columns] = row_refs[0][:, columns].astype(jnp.float32) + partial[:rows]
        for k, part_ref in enumerate(part_refs):
            part_ref[:, columns] = partial[(k + 1) * rows:(k + 2) * rows].astype(jnp.bfloat16)


def backward_kernel(blocks, first, picks, saves, *refs):
    row_refs, refs = refs[:blocks], refs[blocks:]
    rate_refs, normed_refs, refs = refs[:saves], refs[saves:2 * saves], refs[2 * saves:]
    weight_refs, (gain_ref, own_ref, *part_refs, flat, rate, normed, hidden, sems) = refs[:4], refs[4:]
    rows, width = row_refs[0].shape
    ff = weight_refs[2].shape[1]
    stage = lax.axis_index("pipe")

    def copies(at):
        return (
            pltpu.make_async_copy(rate_refs[at], rate, sems.at[0]),
            pltpu.make_async_copy(normed_refs[at], normed, sems.at[1]),
        )

    for at in range(saves):
        holders = [s for s, picked in enumerate(picks) if picked == at]

        @pl.when(functools.reduce(jnp.logical_or, [stage == s for s in holders]))
        def _():
            for copy in copies(at):
                copy.start()

    for k, row_ref in enumerate(row_refs):
        flat[k * rows:(k + 1) * rows, :] = row_ref[...]
    micro = first + stage
    kept = jnp.where((micro >= 0) & (micro < MICRO), 1.0, 0.0)
    for e in range(2):
        q = jnp.dot(flat[...], weight_refs[2 + e][...], preferred_element_type=jnp.float32) * kept
        if e == 0:
            for copy in copies(0):
                copy.wait()
        for half in range(2):
            columns = slice((2 * e + half) * ff, (2 * e + half + 1) * ff)
            hidden[:, columns] = (q * rate[:, columns]).astype(jnp.bfloat16)

    @in_chunks(width)
    def _(columns):
        partial = sum(
            jnp.dot(
                hidden[:, 2 * e * ff:(2 * e + 2) * ff], weight_refs[e][:, columns], preferred_element_type=jnp.float32
            )
            for e in range(2)
        )
        gain_ref[:, columns] = jnp.sum(partial * normed[:, columns].astype(jnp.float32), axis=0, keepdims=True)
        own_ref[:, columns] = partial[:rows]
        for k, part_ref in enumerate(part_refs):
            part_ref[:, columns] = partial[(k + 1) * rows:(k + 2) * rows].astype(jnp.bfloat16)


def forward_experts(tick, row_blocks, tables, gain, weights):
    blocks, rows, width = len(row_blocks), row_blocks[0].shape[0], gain.shape[1]
    total, ff = blocks * rows, weights[2].shape[0]
    outs = [
        jax.ShapeDtypeStruct((total, 4 * ff), jnp.float32),
        jax.ShapeDtypeStruct((total, width), jnp.bfloat16),
        jax.ShapeDtypeStruct((rows, width), jnp.float32),
    ]
    outs += [jax.ShapeDtypeStruct((rows, width), jnp.bfloat16)] * (blocks - 1)
    scratch = [pltpu.VMEM((total, 2 * ff), jnp.float32), pltpu.VMEM((total, 2 * ff), jnp.bfloat16)]
    kernel = functools.partial(forward_kernel, blocks, tick)
    flops = 12 * total * width * ff
    rate, normed, *parts = in_vmem(kernel, outs, scratch, flops, *row_blocks, *tables, gain, *weights)
    return rate, normed, parts


def backward_experts(first, picks, row_blocks, rates, normeds, weights):
    blocks, (rows, width) = len(row_blocks), row_blocks[0].shape
    total, wide = rates[0].shape
    outs = [jax.ShapeDtypeStruct((1, width), jnp.float32), jax.ShapeDtypeStruct((rows, width), jnp.float32)]
    outs += [jax.ShapeDtypeStruct((rows, width), jnp.bfloat16)] * (blocks - 1)
    scratch = [
        pltpu.VMEM((total, width), jnp.bfloat16),
        pltpu.VMEM((total, wide), jnp.float32),
        pltpu.VMEM((total, width), jnp.bfloat16),
        pltpu.VMEM((total, wide), jnp.bfloat16),
        pltpu.SemaphoreType.DMA((2,)),
    ]
    used = sorted(set(picks))
    kernel = functools.partial(backward_kernel, blocks, first, [used.index(at) for at in picks], len(used))
    anywhere = pl.BlockSpec(memory_space=pl.ANY)
    specs = [VMEM] * blocks + [anywhere] * (2 * len(used)) + [VMEM] * 4
    saved = [rates[at] for at in used] + [normeds[at] for at in used]
    flops = 3 * total * width * wide
    gained, *parts = in_vmem(kernel, outs, scratch, flops, *row_blocks, *saved, *weights, specs=specs)
    return gained, parts


def summed_over_owners(value):
    value = value + swap_cores(value)
    return sum(spread(value))


def dense_body(tokens, cotangent, owner_ids, gate_weights, norm_gain, w_gate, w_up, w_down):
    f32, bf16 = jnp.float32, jnp.bfloat16
    stages = lax.axis_size("pipe")
    tok_rows, width = tokens.shape
    rows = tok_rows // MICRO
    gain = norm_gain[0][None, :]
    ticks = MICRO + stages - 1
    stage = in_vmem(stage_kernel, [jax.ShapeDtypeStruct((1, width), jnp.int32)], [], 0)[0]

    own = [pltpu.with_memory_space_constraint(w[0, 0], pltpu.HBM) for w in (w_gate, w_up, w_down)]
    theirs = [swap_cores(w) for w in own]
    joint, down = loaded(*own)
    pair_joint, pair_down = loaded(*[pltpu.with_memory_space_constraint(w, pltpu.VMEM) for w in theirs])
    forward_weights = (joint, pair_joint, down, pair_down)
    backward_weights = []
    for number, part in enumerate(forward_weights):
        backward_weights.append(turned(part))

    def choose(values):
        found = values[0]
        for s, value in enumerate(values):
            if value is not found:
                found = jnp.where(stage == s, value, found)
        return found

    rates, normeds, ins, outs, grads = [], [], [], [], []
    gain_sum = jnp.zeros((1, width), f32)
    behind = ahead = None
    last = ticks + stages - 2
    for tick in range(last + 1):
        if tick == stages - 1:
            grad_blocks = spread(lax.optimization_barrier((cotangent[:rows], *outs[-1:]))[0])
        if tick < ticks:
            if tick == 0:
                here = first_rows(tokens, owner_ids[0].T, gate_weights[0].T)
            elif tick < MICRO:
                here = jnp.where(stage == 0, tokens[tick * rows:(tick + 1) * rows], behind)
            else:
                here = behind
            here_blocks = spread(here)
            if tick == 0:
                tables = here_blocks
            rate, normed, parts = forward_experts(tick, here_blocks, tables, gain, forward_weights)
            rates.append(rate)
            normeds.append(normed)
            ins.append(here[:, :width])
            if tick + 1 < ticks:
                parts = collect(parts)
                outs.append(lax.optimization_barrier(sum(p.astype(f32) for p in parts).astype(bf16)))
                behind = hopped(outs[-1], 1)
        number = tick - (stages - 1)
        if number >= 0:
            first = number - (stages - 1)
            picks = [min(max(first + 2 * s, 0), min(ticks - 1, tick)) for s in range(stages)]
            if number == 0:
                grad = cotangent[:rows]
            elif number < MICRO:
                grad = jnp.where(stage == stages - 1, cotangent[number * rows:(number + 1) * rows], ahead)
            else:
                grad = ahead
            if number:
                grad_blocks = spread(grad)
            gained, sums = backward_experts(first, picks, grad_blocks, rates, normeds, backward_weights)
            sums = collect(sums)
            normed_grad = sum(p.astype(f32) for p in sums)
            x = choose([ins[at] for at in picks]).astype(f32)
            scale = inverse_rms(x)
            weighted = gain * normed_grad
            grad_x = (
                grad.astype(f32)
                + scale * weighted
                - x * scale * scale * scale * jnp.mean(weighted * x, axis=-1, keepdims=True)
            ).astype(bf16)
            gain_sum = gain_sum + gained
            if tick < last:
                grad_x = lax.optimization_barrier(grad_x)
            grads.append(grad_x)
            if tick < last:
                ahead = hopped(grad_x, -1)
            if tick + 1 == ticks:
                waiting, kept = parts, parts[:1]
            while tick + 1 >= ticks and len(kept) < len(waiting) and (tick - ticks + 2 >= len(kept) or tick + 1 == last):
                kept.append(returned(lax.optimization_barrier((waiting, grad_x))[0], len(kept)))
    outs.append(sum(part.astype(f32) for part in kept).astype(bf16))
    gain_grad = summed_over_owners(gain_sum) / gain
    segment_out = jnp.concatenate([choose([outs[m + s] for s in range(stages)]) for m in range(MICRO)])
    segment_grad = jnp.concatenate(
        [choose([grads[m + stages - 1 - s] for s in range(stages)]) for m in range(MICRO)]
    )
    return (segment_out[None], segment_grad[None], gain_grad)


def body(tokens, cotangent, owner_ids, *rest):
    owners = lax.axis_size("dp") * lax.axis_size("expert")
    routed_densely = owners <= 2 * owner_ids.shape[2] and lax.axis_size("expert") % 2 == 0
    plan = dense_body if routed_densely else slot_body
    return plan(tokens, cotangent, owner_ids, *rest)


def solution(mesh):
    in_specs = (
        P(("dp", "expert"), None),
        P(("dp", "expert"), None),
        P("pipe", ("dp", "expert"), None),
        P("pipe", ("dp", "expert"), None),
        P("pipe", None),
        P("pipe", ("dp", "expert"), None, None),
        P("pipe", ("dp", "expert"), None, None),
        P("pipe", ("dp", "expert"), None, None),
    )
    out_specs = (
        P("pipe", ("dp", "expert"), None),
        P("pipe", ("dp", "expert"), None),
        P("pipe", None),
    )
    return jax.shard_map(body, mesh=mesh, in_specs=in_specs, out_specs=out_specs, check_vma=False)
```

```python
import jax
import jax.numpy as jnp
from jax import lax
from jax.experimental import pallas as pl
from jax.experimental.pallas import tpu as pltpu
import functools
import math
from jax.sharding import PartitionSpec as P

MICRO = 4
LIMIT = 12 * 1024 * 1024
DP, PIPE, EXPERT = "dp", "pipe", "expert"


epsilon = 1e-06


def from_behind(value, axis, steps):
    count = lax.axis_size(axis)
    leading, last = (max(0, -steps), min(count, count - steps))
    return lax.ppermute(value, axis, [(source, source + steps) for source in range(leading, last)])


def inverse_rms(values):
    return lax.rsqrt(jnp.mean(values * values, axis=-1, keepdims=True) + epsilon)


def contract_last(left, right):
    return lax.dot_general(
        left, right, (((1,), (1,)), ((), ())), preferred_element_type=jnp.float32
    )


def route_tables(ids_part, owners, capacity):
    owner_range = jnp.arange(owners, dtype=jnp.int32)
    onehot = (ids_part[:, :, None] == owner_range[None, None, :]).astype(jnp.int32)
    member = jnp.sum(onehot, axis=1)
    position = jnp.cumsum(member, axis=0) - member
    slot_range = jnp.arange(capacity, dtype=jnp.int32)
    placed = (position[:, :, None] == slot_range[None, None, :]) & (member[:, :, None] > 0)
    placing = jnp.transpose(placed, (1, 2, 0)).astype(jnp.bfloat16)
    return (onehot.astype(jnp.float32), placing)


def gate_slots(onehot, gates_part, placing, experts_here):
    gate_pairs = gates_part.astype(jnp.float32).reshape(gates_part.shape[0], -1, experts_here)
    chosen = jnp.einsum("rjo,rjc->roc", onehot, gate_pairs)
    return jnp.einsum("okr,roc->okc", placing.astype(jnp.float32), chosen).astype(jnp.bfloat16)


def send_rows(row_block, pair_block):
    got_rows, got_pairs = (
        lax.all_to_all(row_block, (DP, EXPERT), split_axis=0, concat_axis=0, tiled=True),
        lax.all_to_all(pair_block, (DP, EXPERT), split_axis=0, concat_axis=0, tiled=True),
    )
    return (got_rows, got_pairs)


def return_rows(row_block):
    return lax.all_to_all(row_block, (DP, EXPERT), split_axis=0, concat_axis=0, tiled=True)


def send_grads(row_block):
    return lax.all_to_all(row_block, (DP, EXPERT), split_axis=0, concat_axis=0, tiled=True)


def return_grads(row_block):
    return lax.all_to_all(row_block, (DP, EXPERT), split_axis=0, concat_axis=0, tiled=True)


def expert_forward(flat_rows, flat_pairs, joint_mats, down_mats):
    hidden_width = down_mats.shape[1]
    joint_pre = jnp.dot(flat_rows, joint_mats[0], preferred_element_type=jnp.float32)
    gate_pre = joint_pre[:, :hidden_width]
    up_pre = joint_pre[:, hidden_width:]
    hidden = (jax.nn.silu(gate_pre) * up_pre).astype(jnp.bfloat16)
    projected = jnp.dot(hidden, down_mats[0], preferred_element_type=jnp.float32)
    term = flat_pairs.astype(jnp.float32) * projected
    kept_both = [joint_pre]
    return (term.astype(jnp.bfloat16), jnp.stack(kept_both))


def expert_backward(grad_rows, flat_pairs, joint_keep, joint_mats, down_mats):
    hidden_width = down_mats.shape[1]
    q_vals = contract_last(grad_rows, down_mats[0])
    gate_pre = joint_keep[0][:, :hidden_width]
    up_pre = joint_keep[0][:, hidden_width:]
    sigma = jax.nn.sigmoid(gate_pre)
    weight = flat_pairs.astype(jnp.float32)
    d_gate = (q_vals * weight * up_pre * sigma * (1.0 + gate_pre * (1.0 - sigma))).astype(
        jnp.bfloat16
    )
    d_up = (q_vals * weight * gate_pre * sigma).astype(jnp.bfloat16)
    joint_grad = jnp.concatenate([d_gate, d_up], axis=1)
    term = contract_last(joint_grad, joint_mats[0])
    return term.astype(jnp.bfloat16)


def slot_body(tokens, cotangent, owner_ids, gate_weights, norm_gain, w_gate, w_up, w_down):
    segments = lax.axis_size(PIPE)
    segment_index = lax.axis_index(PIPE)
    owners = lax.axis_size(DP) * lax.axis_size(EXPERT)
    tok_rows = tokens.shape[0]
    width = tokens.shape[1]
    micro_rows = tok_rows // MICRO
    route_count = owner_ids.shape[2]
    capacity = max(2, (5 * micro_rows * route_count + 4 * owners - 1) // (4 * owners))
    slot_count = owners * capacity
    gain_row = norm_gain[0]
    joint_mats = jnp.concatenate([w_gate[0], w_up[0]], axis=2)
    down_mats = w_down[0]
    layer_ids = owner_ids[0]
    layer_gates = gate_weights[0]
    experts_here = joint_mats.shape[0]
    joint_width = joint_mats.shape[2]

    def skip_forward(operands):
        return (
            jnp.zeros((slot_count, width), jnp.bfloat16),
            jnp.zeros((experts_here, slot_count, joint_width), jnp.float32),
        )

    def run_forward(operands):
        return expert_forward(operands[0], operands[1], joint_mats, down_mats)

    def skip_backward(operands):
        return jnp.zeros((slot_count, width), jnp.bfloat16)

    def run_backward(operands):
        return expert_backward(operands[0], operands[1], operands[2], joint_mats, down_mats)

    def timing(micro):
        is_valid = (micro >= 0) & (micro < MICRO)
        slot_pick = jnp.where(is_valid, micro, MICRO)
        start_row = jnp.clip(micro, 0, MICRO - 1) * micro_rows
        return (is_valid, slot_pick, start_row)

    layer_outs = jnp.zeros((MICRO + 1, micro_rows, width), jnp.bfloat16)
    layer_ins = jnp.zeros((MICRO + 1, micro_rows, width), jnp.bfloat16)
    kept_joint = jnp.zeros((MICRO + 1, experts_here, slot_count, joint_width), jnp.float32)
    kept_pairs = jnp.zeros((MICRO + 1, slot_count, experts_here), jnp.bfloat16)
    grad_outs = jnp.zeros((MICRO + 1, micro_rows, width), jnp.bfloat16)
    gain_sum = jnp.zeros((width,), jnp.float32)
    ticks = MICRO + segments - 1
    incoming = jnp.zeros((micro_rows, width), jnp.bfloat16)
    for tick_num in range(ticks):
        forward_is_valid, forward_slot_pick, forward_start_row = timing(tick_num - segment_index)
        forward_own_part = lax.dynamic_slice_in_dim(tokens, forward_start_row, micro_rows, 0)
        forward_layer_in = jnp.where(segment_index == 0, forward_own_part, incoming)
        forward_ids_part = lax.dynamic_slice_in_dim(layer_ids, forward_start_row, micro_rows, 0)
        gates_part = lax.dynamic_slice_in_dim(layer_gates, forward_start_row, micro_rows, 0)
        forward_x_float = forward_layer_in.astype(jnp.float32)
        forward_scale = inverse_rms(forward_x_float)
        normed = (forward_x_float * forward_scale * gain_row).astype(jnp.bfloat16)
        forward_onehot, forward_placing = route_tables(forward_ids_part, owners, capacity)
        row_block = jnp.einsum(
            "okr,rd->okd", forward_placing, normed, preferred_element_type=jnp.float32
        ).astype(jnp.bfloat16)
        pair_block = gate_slots(forward_onehot, gates_part, forward_placing, experts_here)
        f_valid, f_pick, layer_in, x_float, f_placing, row_block, pair_block = (
            forward_is_valid,
            forward_slot_pick,
            forward_layer_in,
            forward_x_float,
            forward_placing,
            row_block,
            pair_block,
        )
        got_rows, got_pairs = send_rows(row_block, pair_block)
        flat_rows = got_rows.reshape(slot_count, width)
        flat_pairs = got_pairs.reshape(slot_count, experts_here)
        result, joint_pre = lax.cond(f_valid, run_forward, skip_forward, (flat_rows, flat_pairs))
        returned = return_rows(result.reshape(owners, capacity, width))
        branch = jnp.einsum("okr,okd->rd", f_placing, returned, preferred_element_type=jnp.float32)
        layer_out = (x_float + branch).astype(jnp.bfloat16)
        layer_outs = lax.dynamic_update_index_in_dim(layer_outs, layer_out, f_pick, 0)
        layer_ins = lax.dynamic_update_index_in_dim(layer_ins, layer_in, f_pick, 0)
        kept_joint = lax.dynamic_update_index_in_dim(kept_joint, joint_pre, f_pick, 0)
        kept_pairs = lax.dynamic_update_index_in_dim(kept_pairs, flat_pairs, f_pick, 0)
        if tick_num + 1 < ticks:
            incoming = from_behind(layer_out, PIPE, 1)
    incoming = jnp.zeros((micro_rows, width), jnp.bfloat16)
    for tick_num in range(ticks):
        backward_is_valid, backward_slot_pick, backward_start_row = timing(
            tick_num - (segments - 1 - segment_index)
        )
        own_part = lax.dynamic_slice_in_dim(cotangent, backward_start_row, micro_rows, 0)
        backward_grad_in = jnp.where(segment_index == segments - 1, own_part, incoming)
        ids_part = lax.dynamic_slice_in_dim(layer_ids, backward_start_row, micro_rows, 0)
        backward_layer_in = lax.dynamic_index_in_dim(
            layer_ins, backward_slot_pick, 0, keepdims=False
        )
        backward_x_float = backward_layer_in.astype(jnp.float32)
        backward_scale = inverse_rms(backward_x_float)
        _, backward_placing = route_tables(ids_part, owners, capacity)
        grad_block = jnp.einsum(
            "okr,rd->okd", backward_placing, backward_grad_in, preferred_element_type=jnp.float32
        ).astype(jnp.bfloat16)
        b_valid, b_pick, grad_in, bx_float, b_scale, b_placing, grad_block = (
            backward_is_valid,
            backward_slot_pick,
            backward_grad_in,
            backward_x_float,
            backward_scale,
            backward_placing,
            grad_block,
        )
        got_grads = send_grads(grad_block).reshape(slot_count, width)
        joint_keep = lax.dynamic_index_in_dim(kept_joint, b_pick, 0, keepdims=False)
        pair_keep = lax.dynamic_index_in_dim(kept_pairs, b_pick, 0, keepdims=False)
        owner_grad = lax.cond(
            b_valid, run_backward, skip_backward, (got_grads, pair_keep, joint_keep)
        )
        returned = return_grads(owner_grad.reshape(owners, capacity, width))
        normed_grad = jnp.einsum(
            "okr,okd->rd", b_placing, returned, preferred_element_type=jnp.float32
        )
        weighted = gain_row * normed_grad
        grad_x = (
            grad_in.astype(jnp.float32)
            + b_scale * weighted
            - bx_float
            * b_scale
            * b_scale
            * b_scale
            * jnp.mean(weighted * bx_float, axis=-1, keepdims=True)
        )
        gain_term = jnp.where(b_valid, jnp.sum(normed_grad * bx_float * b_scale, axis=0), 0.0)
        grad_bf, gain_term = (grad_x.astype(jnp.bfloat16), gain_term)
        grad_outs = lax.dynamic_update_index_in_dim(grad_outs, grad_bf, b_pick, 0)
        gain_sum = gain_sum + gain_term
        if tick_num + 1 < ticks:
            incoming = from_behind(grad_bf, PIPE, -1)
    gain_grad = lax.psum(gain_sum, (DP, EXPERT))
    segment_out = layer_outs[:MICRO].reshape(1, tok_rows, width)
    segment_grad = grad_outs[:MICRO].reshape(1, tok_rows, width)
    return (segment_out, segment_grad, gain_grad.reshape(1, width))


def swap_cores(value):
    count = lax.axis_size(EXPERT)
    return lax.ppermute(value, EXPERT, [(e, e ^ 1) for e in range(count)])


def shifted(value, dp_step, chip_step):
    dps, experts = (lax.axis_size(name) for name in (DP, EXPERT))
    pairs = []
    for dp in range(dps):
        for expert in range(experts):
            target = (dp + dp_step) % dps * experts + (expert + 2 * chip_step) % experts
            pairs.append((dp * experts + expert, target))
    return lax.ppermute(value, (DP, EXPERT), pairs)


def hopped(value, step):
    stages = lax.axis_size(PIPE)
    return lax.ppermute(value, PIPE, [(s, (s + step) % stages) for s in range(stages)])


def chip_steps():
    dps, chips = lax.axis_size(DP), lax.axis_size(EXPERT) // 2
    steps = [(d, c) for d in range(dps) for c in range(chips)]
    return sorted(steps[1:], key=lambda step: -(step[0] + step[1]))


def spread(rows):
    return [rows] + [shifted(rows, d, c) for d, c in chip_steps()]


def returned(blocks, which):
    dps, chips = lax.axis_size(DP), lax.axis_size(EXPERT) // 2
    dp, chip = chip_steps()[which - 1]
    return shifted(blocks[which], -dp % dps, -chip % chips)


def collect(blocks):
    return [blocks[0]] + [returned(blocks, which) for which in range(1, len(blocks))]


VMEM = pl.BlockSpec(memory_space=pltpu.VMEM)
CHUNK = 256
LANES = 128
HALVES = 2


def in_vmem(kernel, outs, scratch, flops, *operands, specs=None):
    moved = sum(math.prod(a.shape) * a.dtype.itemsize for a in [*outs, *operands])
    return pl.pallas_call(
        kernel,
        out_shape=outs,
        in_specs=specs or [VMEM] * len(operands),
        out_specs=[VMEM] * len(outs),
        scratch_shapes=scratch,
        compiler_params=pltpu.CompilerParams(vmem_limit_bytes=LIMIT),
        cost_estimate=pl.CostEstimate(flops=flops, bytes_accessed=moved, transcendentals=0),
    )(*operands)


def load_kernel(gate_ref, up_ref, down_ref, joint_out, down_out, sems):
    ff = gate_ref.shape[1]
    copies = [
        pltpu.make_async_copy(gate_ref, joint_out.at[:, :ff], sems.at[0]),
        pltpu.make_async_copy(up_ref, joint_out.at[:, ff:], sems.at[1]),
        pltpu.make_async_copy(down_ref, down_out, sems.at[2]),
    ]
    for copy in copies:
        copy.start()
    for copy in copies:
        copy.wait()


def loaded(gate, up, down):
    outs = [pltpu.VMEM((gate.shape[0], 2 * gate.shape[1]), gate.dtype), pltpu.VMEM(down.shape, down.dtype)]
    specs = [pl.BlockSpec(memory_space=pl.ANY)] * 3
    return in_vmem(load_kernel, outs, [pltpu.SemaphoreType.DMA((3,))], 0, gate, up, down, specs=specs)


def stage_kernel(out_ref):
    out_ref[...] = jnp.full(out_ref.shape, lax.axis_index(PIPE), jnp.int32)


def first_rows_kernel(token_ref, id_hbm, gate_hbm, out_ref, copied, id_ref, gate_ref, sems):
    rows, width = copied.shape
    copy = pltpu.make_async_copy(token_ref.at[pl.ds(0, rows), :], copied, sems.at[0])
    id_copy = pltpu.make_async_copy(id_hbm, id_ref, sems.at[1])
    gate_copy = pltpu.make_async_copy(gate_hbm, gate_ref, sems.at[2])
    for each in (id_copy, gate_copy, copy):
        each.start()
    owners = lax.axis_size(DP) * lax.axis_size(EXPERT)
    column = lax.broadcasted_iota(jnp.int32, (rows, out_ref.shape[1] - width), 1)
    table = jnp.zeros(column.shape, jnp.float32)
    id_copy.wait()
    gate_copy.wait()
    ids, gates = id_ref[...].T, gate_ref[...].astype(jnp.float32).T
    for micro in range(MICRO):
        window = slice(micro * rows, (micro + 1) * rows)
        for slot in range(ids.shape[1]):
            place = micro * owners + ids[window, slot:slot + 1]
            table = table + jnp.where(column == place, gates[window, slot:slot + 1], 0.0)
    out_ref[:, width:] = table.astype(jnp.bfloat16)
    copy.wait()
    out_ref[:, :width] = copied[...]


def first_rows(tokens, ids, gates):
    rows, width = tokens.shape[0] // MICRO, tokens.shape[1]
    owners = lax.axis_size(DP) * lax.axis_size(EXPERT)
    extra = -(-MICRO * owners // LANES) * LANES
    outs = [jax.ShapeDtypeStruct((rows, width + extra), tokens.dtype)]
    scratch = [pltpu.VMEM((rows, width), tokens.dtype), pltpu.VMEM(ids.shape, ids.dtype)]
    scratch += [pltpu.VMEM(gates.shape, gates.dtype), pltpu.SemaphoreType.DMA((3,))]
    specs = [pl.BlockSpec(memory_space=pl.ANY)] * 3
    tokens, ids, gates = (pltpu.with_memory_space_constraint(value, pltpu.HBM) for value in (tokens, ids, gates))
    return in_vmem(first_rows_kernel, outs, scratch, 0, tokens, ids, gates, specs=specs)[0]


def turn_kernel(in_ref, out_ref):
    size = math.gcd(in_ref.shape[0], CHUNK)

    @pl.loop(0, in_ref.shape[0] // size)
    def _(at):
        window = pl.ds(pl.multiple_of(at * size, size), size)
        out_ref[:, window] = in_ref[window, :].T


def turned(part):
    outs = [pltpu.VMEM(part.shape[::-1], part.dtype)]
    return in_vmem(turn_kernel, outs, [], 0, part)[0]


def in_chunks(width):
    half = width // HALVES

    def run(work):
        @pl.loop(0, HALVES)
        def _(at):
            for start in range(0, half, CHUNK):
                work(pl.ds(pl.multiple_of(at * half + start, CHUNK), CHUNK))

    return run


def owner_number():
    return lax.axis_index(DP) * lax.axis_size(EXPERT) + lax.axis_index(EXPERT)


def forward_kernel(blocks, tick, *refs):
    row_refs, table_refs, refs = refs[:blocks], refs[blocks:2 * blocks], refs[2 * blocks:]
    gain_ref, *weight_refs = refs[:5]
    rate_ref, flat_ref, own_ref, *part_refs, pre, hidden = refs[5:]
    rows, width = own_ref.shape
    ff = weight_refs[2].shape[0]
    gain = gain_ref[...]
    for k, row_ref in enumerate(row_refs):
        x = row_ref[:, :width].astype(jnp.float32)
        flat_ref[k * rows:(k + 1) * rows, :] = (x * inverse_rms(x) * gain).astype(jnp.bfloat16)
    micro = tick - lax.axis_index(PIPE)
    is_valid = (micro >= 0) & (micro < MICRO)
    routed = jnp.concatenate([ref[:, width:] for ref in table_refs], axis=0).astype(jnp.float32)
    column = lax.broadcasted_iota(jnp.int32, routed.shape, 1)
    me, owners = owner_number(), lax.axis_size(DP) * lax.axis_size(EXPERT)
    for e, owner in enumerate((me, me ^ 1)):
        is_routed = (column == micro * owners + owner) & is_valid
        weight = jnp.sum(jnp.where(is_routed, routed, 0.0), axis=1, keepdims=True)
        for start in range(0, 2 * ff, CHUNK):
            pre[:, start:start + CHUNK] = jnp.dot(
                flat_ref[...], weight_refs[e][:, start:start + CHUNK], preferred_element_type=jnp.float32
            )
        gate_pre, up_pre = pre[:, :ff], pre[:, ff:]
        sigma = jax.nn.sigmoid(gate_pre)
        up_rate = weight * gate_pre * sigma
        hidden[:, e * ff:(e + 1) * ff] = (up_rate * up_pre).astype(jnp.bfloat16)
        rate_ref[:, 2 * e * ff:(2 * e + 1) * ff] = weight * up_pre * sigma * (1.0 + gate_pre * (1.0 - sigma))
        rate_ref[:, (2 * e + 1) * ff:(2 * e + 2) * ff] = up_rate

    @in_chunks(width)
    def _(columns):
        partial = sum(
            jnp.dot(hidden[:, e * ff:(e + 1) * ff], weight_refs[2 + e][:, columns], preferred_element_type=jnp.float32)
            for e in range(2)
        )
        own_ref[:, columns] = row_refs[0][:, columns].astype(jnp.float32) + partial[:rows]
        for k, part_ref in enumerate(part_refs):
            part_ref[:, columns] = partial[(k + 1) * rows:(k + 2) * rows].astype(jnp.bfloat16)


def backward_kernel(blocks, first, picks, saves, *refs):
    row_refs, refs = refs[:blocks], refs[blocks:]
    rate_refs, normed_refs, refs = refs[:saves], refs[saves:2 * saves], refs[2 * saves:]
    weight_refs, (gain_ref, own_ref, *part_refs, flat, rate, normed, hidden, sems) = refs[:4], refs[4:]
    rows, width = row_refs[0].shape
    ff = weight_refs[2].shape[1]
    stage = lax.axis_index(PIPE)

    def copies(at):
        return (
            pltpu.make_async_copy(rate_refs[at], rate, sems.at[0]),
            pltpu.make_async_copy(normed_refs[at], normed, sems.at[1]),
        )

    for at in range(saves):
        holders = [s for s, picked in enumerate(picks) if picked == at]

        @pl.when(functools.reduce(jnp.logical_or, [stage == s for s in holders]))
        def _():
            for copy in copies(at):
                copy.start()

    for k, row_ref in enumerate(row_refs):
        flat[k * rows:(k + 1) * rows, :] = row_ref[...]
    micro = first + stage
    kept = jnp.where((micro >= 0) & (micro < MICRO), 1.0, 0.0)
    for e in range(2):
        q = jnp.dot(flat[...], weight_refs[2 + e][...], preferred_element_type=jnp.float32) * kept
        if e == 0:
            for copy in copies(0):
                copy.wait()
        for half in range(2):
            columns = slice((2 * e + half) * ff, (2 * e + half + 1) * ff)
            hidden[:, columns] = (q * rate[:, columns]).astype(jnp.bfloat16)

    @in_chunks(width)
    def _(columns):
        partial = sum(
            jnp.dot(
                hidden[:, 2 * e * ff:(2 * e + 2) * ff], weight_refs[e][:, columns], preferred_element_type=jnp.float32
            )
            for e in range(2)
        )
        gain_ref[:, columns] = jnp.sum(partial * normed[:, columns].astype(jnp.float32), axis=0, keepdims=True)
        own_ref[:, columns] = partial[:rows]
        for k, part_ref in enumerate(part_refs):
            part_ref[:, columns] = partial[(k + 1) * rows:(k + 2) * rows].astype(jnp.bfloat16)


def forward_experts(tick, row_blocks, tables, gain, weights):
    blocks, rows, width = len(row_blocks), row_blocks[0].shape[0], gain.shape[1]
    total, ff = blocks * rows, weights[2].shape[0]
    outs = [
        jax.ShapeDtypeStruct((total, 4 * ff), jnp.float32),
        jax.ShapeDtypeStruct((total, width), jnp.bfloat16),
        jax.ShapeDtypeStruct((rows, width), jnp.float32),
    ]
    outs += [jax.ShapeDtypeStruct((rows, width), jnp.bfloat16)] * (blocks - 1)
    scratch = [pltpu.VMEM((total, 2 * ff), jnp.float32), pltpu.VMEM((total, 2 * ff), jnp.bfloat16)]
    kernel = functools.partial(forward_kernel, blocks, tick)
    flops = 12 * total * width * ff
    rate, normed, *parts = in_vmem(kernel, outs, scratch, flops, *row_blocks, *tables, gain, *weights)
    return rate, normed, parts


def backward_experts(first, picks, row_blocks, rates, normeds, weights):
    blocks, (rows, width) = len(row_blocks), row_blocks[0].shape
    total, wide = rates[0].shape
    outs = [jax.ShapeDtypeStruct((1, width), jnp.float32), jax.ShapeDtypeStruct((rows, width), jnp.float32)]
    outs += [jax.ShapeDtypeStruct((rows, width), jnp.bfloat16)] * (blocks - 1)
    scratch = [
        pltpu.VMEM((total, width), jnp.bfloat16),
        pltpu.VMEM((total, wide), jnp.float32),
        pltpu.VMEM((total, width), jnp.bfloat16),
        pltpu.VMEM((total, wide), jnp.bfloat16),
        pltpu.SemaphoreType.DMA((2,)),
    ]
    used = sorted(set(picks))
    kernel = functools.partial(backward_kernel, blocks, first, [used.index(at) for at in picks], len(used))
    anywhere = pl.BlockSpec(memory_space=pl.ANY)
    specs = [VMEM] * blocks + [anywhere] * (2 * len(used)) + [VMEM] * 4
    saved = [rates[at] for at in used] + [normeds[at] for at in used]
    flops = 3 * total * width * wide
    gained, *parts = in_vmem(kernel, outs, scratch, flops, *row_blocks, *saved, *weights, specs=specs)
    return gained, parts


def summed_over_owners(value):
    value = value + swap_cores(value)
    return sum(spread(value))


def dense_body(tokens, cotangent, owner_ids, gate_weights, norm_gain, w_gate, w_up, w_down):
    f32, bf16 = jnp.float32, jnp.bfloat16
    stages = lax.axis_size(PIPE)
    tok_rows, width = tokens.shape
    rows = tok_rows // MICRO
    gain = norm_gain[0][None, :]
    ticks = MICRO + stages - 1
    stage = in_vmem(stage_kernel, [jax.ShapeDtypeStruct((1, width), jnp.int32)], [], 0)[0]

    own = [pltpu.with_memory_space_constraint(w[0, 0], pltpu.HBM) for w in (w_gate, w_up, w_down)]
    theirs = [swap_cores(w) for w in own]
    joint, down = loaded(*own)
    pair_joint, pair_down = loaded(*[pltpu.with_memory_space_constraint(w, pltpu.VMEM) for w in theirs])
    forward_weights = (joint, pair_joint, down, pair_down)
    backward_weights = []
    for number, part in enumerate(forward_weights):
        backward_weights.append(turned(part))

    def choose(values):
        found = values[0]
        for s, value in enumerate(values):
            if value is not found:
                found = jnp.where(stage == s, value, found)
        return found

    rates, normeds, ins, outs, grads = [], [], [], [], []
    gain_sum = jnp.zeros((1, width), f32)
    behind = ahead = None
    last = ticks + stages - 2
    for tick in range(last + 1):
        if tick == stages - 1:
            grad_blocks = spread(lax.optimization_barrier((cotangent[:rows], *outs[-1:]))[0])
        if tick < ticks:
            if tick == 0:
                here = first_rows(tokens, owner_ids[0].T, gate_weights[0].T)
            elif tick < MICRO:
                here = jnp.where(stage == 0, tokens[tick * rows:(tick + 1) * rows], behind)
            else:
                here = behind
            here_blocks = spread(here)
            if tick == 0:
                tables = here_blocks
            rate, normed, parts = forward_experts(tick, here_blocks, tables, gain, forward_weights)
            rates.append(rate)
            normeds.append(normed)
            ins.append(here[:, :width])
            if tick + 1 < ticks:
                parts = collect(parts)
                outs.append(lax.optimization_barrier(sum(p.astype(f32) for p in parts).astype(bf16)))
                behind = hopped(outs[-1], 1)
        number = tick - (stages - 1)
        if number >= 0:
            first = number - (stages - 1)
            picks = [min(max(first + 2 * s, 0), min(ticks - 1, tick)) for s in range(stages)]
            if number == 0:
                grad = cotangent[:rows]
            elif number < MICRO:
                grad = jnp.where(stage == stages - 1, cotangent[number * rows:(number + 1) * rows], ahead)
            else:
                grad = ahead
            if number:
                grad_blocks = spread(grad)
            gained, sums = backward_experts(first, picks, grad_blocks, rates, normeds, backward_weights)
            sums = collect(sums)
            normed_grad = sum(p.astype(f32) for p in sums)
            x = choose([ins[at] for at in picks]).astype(f32)
            scale = inverse_rms(x)
            weighted = gain * normed_grad
            grad_x = (
                grad.astype(f32)
                + scale * weighted
                - x * scale * scale * scale * jnp.mean(weighted * x, axis=-1, keepdims=True)
            ).astype(bf16)
            gain_sum = gain_sum + gained
            if tick < last:
                grad_x = lax.optimization_barrier(grad_x)
            grads.append(grad_x)
            if tick < last:
                ahead = hopped(grad_x, -1)
            if tick + 1 == ticks:
                waiting, kept = parts, parts[:1]
            while tick + 1 >= ticks and len(kept) < len(waiting) and (tick - ticks + 2 >= len(kept) or tick + 1 == last):
                kept.append(returned(lax.optimization_barrier((waiting, grad_x))[0], len(kept)))
    outs.append(sum(part.astype(f32) for part in kept).astype(bf16))
    gain_grad = summed_over_owners(gain_sum) / gain
    segment_out = jnp.concatenate([choose([outs[m + s] for s in range(stages)]) for m in range(MICRO)])
    segment_grad = jnp.concatenate(
        [choose([grads[m + stages - 1 - s] for s in range(stages)]) for m in range(MICRO)]
    )
    return (segment_out[None], segment_grad[None], gain_grad)


def body(tokens, cotangent, owner_ids, *rest):
    owners = lax.axis_size(DP) * lax.axis_size(EXPERT)
    routed_densely = owners <= 2 * owner_ids.shape[2] and lax.axis_size(EXPERT) % 2 == 0
    plan = dense_body if routed_densely else slot_body
    return plan(tokens, cotangent, owner_ids, *rest)


def solution(mesh):
    in_specs = (
        P((DP, EXPERT), None),
        P((DP, EXPERT), None),
        P(PIPE, (DP, EXPERT), None),
        P(PIPE, (DP, EXPERT), None),
        P(PIPE, None),
        P(PIPE, (DP, EXPERT), None, None),
        P(PIPE, (DP, EXPERT), None, None),
        P(PIPE, (DP, EXPERT), None, None),
    )
    out_specs = (
        P(PIPE, (DP, EXPERT), None),
        P(PIPE, (DP, EXPERT), None),
        P(PIPE, None),
    )
    return jax.shard_map(body, mesh=mesh, in_specs=in_specs, out_specs=out_specs, check_vma=False)
```

```python
import jax
import jax.numpy as jnp
from jax import lax
from jax.experimental import pallas as pl
from jax.experimental.pallas import tpu as pltpu
import functools
import math
from jax.sharding import PartitionSpec as P

MICRO = 4
LIMIT = 12 * 1024 * 1024
DP, PIPE, EXPERT = "dp", "pipe", "expert"


epsilon = 1e-06


def from_behind(value, axis, steps):
    count = lax.axis_size(axis)
    leading, last = (max(0, -steps), min(count, count - steps))
    return lax.ppermute(value, axis, [(source, source + steps) for source in range(leading, last)])


def inverse_rms(values):
    return lax.rsqrt(jnp.mean(values * values, axis=-1, keepdims=True) + epsilon)


def contract_last(left, right):
    return lax.dot_general(
        left, right, (((1,), (1,)), ((), ())), preferred_element_type=jnp.float32
    )


def route_tables(ids_part, owners, capacity):
    owner_range = jnp.arange(owners, dtype=jnp.int32)
    onehot = (ids_part[:, :, None] == owner_range[None, None, :]).astype(jnp.int32)
    member = jnp.sum(onehot, axis=1)
    position = jnp.cumsum(member, axis=0) - member
    slot_range = jnp.arange(capacity, dtype=jnp.int32)
    placed = (position[:, :, None] == slot_range[None, None, :]) & (member[:, :, None] > 0)
    placing = jnp.transpose(placed, (1, 2, 0)).astype(jnp.bfloat16)
    return (onehot.astype(jnp.float32), placing)


def gate_slots(onehot, gates_part, placing, experts_here):
    gate_pairs = gates_part.astype(jnp.float32).reshape(gates_part.shape[0], -1, experts_here)
    chosen = jnp.einsum("rjo,rjc->roc", onehot, gate_pairs)
    return jnp.einsum("okr,roc->okc", placing.astype(jnp.float32), chosen).astype(jnp.bfloat16)


def send_rows(row_block, pair_block):
    got_rows, got_pairs = (
        lax.all_to_all(row_block, (DP, EXPERT), split_axis=0, concat_axis=0, tiled=True),
        lax.all_to_all(pair_block, (DP, EXPERT), split_axis=0, concat_axis=0, tiled=True),
    )
    return (got_rows, got_pairs)


def return_rows(row_block):
    return lax.all_to_all(row_block, (DP, EXPERT), split_axis=0, concat_axis=0, tiled=True)


def send_grads(row_block):
    return lax.all_to_all(row_block, (DP, EXPERT), split_axis=0, concat_axis=0, tiled=True)


def return_grads(row_block):
    return lax.all_to_all(row_block, (DP, EXPERT), split_axis=0, concat_axis=0, tiled=True)


def expert_forward(flat_rows, flat_pairs, joint_mats, down_mats):
    hidden_width = down_mats.shape[1]
    joint_pre = jnp.dot(flat_rows, joint_mats[0], preferred_element_type=jnp.float32)
    gate_pre = joint_pre[:, :hidden_width]
    up_pre = joint_pre[:, hidden_width:]
    hidden = (jax.nn.silu(gate_pre) * up_pre).astype(jnp.bfloat16)
    projected = jnp.dot(hidden, down_mats[0], preferred_element_type=jnp.float32)
    term = flat_pairs.astype(jnp.float32) * projected
    kept_both = [joint_pre]
    return (term.astype(jnp.bfloat16), jnp.stack(kept_both))


def expert_backward(grad_rows, flat_pairs, joint_keep, joint_mats, down_mats):
    hidden_width = down_mats.shape[1]
    q_vals = contract_last(grad_rows, down_mats[0])
    gate_pre = joint_keep[0][:, :hidden_width]
    up_pre = joint_keep[0][:, hidden_width:]
    sigma = jax.nn.sigmoid(gate_pre)
    weight = flat_pairs.astype(jnp.float32)
    d_gate = (q_vals * weight * up_pre * sigma * (1.0 + gate_pre * (1.0 - sigma))).astype(
        jnp.bfloat16
    )
    d_up = (q_vals * weight * gate_pre * sigma).astype(jnp.bfloat16)
    joint_grad = jnp.concatenate([d_gate, d_up], axis=1)
    term = contract_last(joint_grad, joint_mats[0])
    return term.astype(jnp.bfloat16)


def slot_body(tokens, cotangent, owner_ids, gate_weights, norm_gain, w_gate, w_up, w_down):
    segments = lax.axis_size(PIPE)
    segment_index = lax.axis_index(PIPE)
    owners = lax.axis_size(DP) * lax.axis_size(EXPERT)
    tok_rows = tokens.shape[0]
    width = tokens.shape[1]
    micro_rows = tok_rows // MICRO
    route_count = owner_ids.shape[2]
    capacity = max(2, (5 * micro_rows * route_count + 4 * owners - 1) // (4 * owners))
    slot_count = owners * capacity
    gain_row = norm_gain[0]
    joint_mats = jnp.concatenate([w_gate[0], w_up[0]], axis=2)
    down_mats = w_down[0]
    layer_ids = owner_ids[0]
    layer_gates = gate_weights[0]
    experts_here = joint_mats.shape[0]
    joint_width = joint_mats.shape[2]

    def skip_forward(operands):
        return (
            jnp.zeros((slot_count, width), jnp.bfloat16),
            jnp.zeros((experts_here, slot_count, joint_width), jnp.float32),
        )

    def run_forward(operands):
        return expert_forward(operands[0], operands[1], joint_mats, down_mats)

    def skip_backward(operands):
        return jnp.zeros((slot_count, width), jnp.bfloat16)

    def run_backward(operands):
        return expert_backward(operands[0], operands[1], operands[2], joint_mats, down_mats)

    def timing(micro):
        is_valid = (micro >= 0) & (micro < MICRO)
        slot_pick = jnp.where(is_valid, micro, MICRO)
        start_row = jnp.clip(micro, 0, MICRO - 1) * micro_rows
        return (is_valid, slot_pick, start_row)

    layer_outs = jnp.zeros((MICRO + 1, micro_rows, width), jnp.bfloat16)
    layer_ins = jnp.zeros((MICRO + 1, micro_rows, width), jnp.bfloat16)
    kept_joint = jnp.zeros((MICRO + 1, experts_here, slot_count, joint_width), jnp.float32)
    kept_pairs = jnp.zeros((MICRO + 1, slot_count, experts_here), jnp.bfloat16)
    grad_outs = jnp.zeros((MICRO + 1, micro_rows, width), jnp.bfloat16)
    gain_sum = jnp.zeros((width,), jnp.float32)
    ticks = MICRO + segments - 1
    incoming = jnp.zeros((micro_rows, width), jnp.bfloat16)
    for tick_num in range(ticks):
        forward_is_valid, forward_slot_pick, forward_start_row = timing(tick_num - segment_index)
        forward_own_part = lax.dynamic_slice_in_dim(tokens, forward_start_row, micro_rows, 0)
        forward_layer_in = jnp.where(segment_index == 0, forward_own_part, incoming)
        forward_ids_part = lax.dynamic_slice_in_dim(layer_ids, forward_start_row, micro_rows, 0)
        gates_part = lax.dynamic_slice_in_dim(layer_gates, forward_start_row, micro_rows, 0)
        forward_x_float = forward_layer_in.astype(jnp.float32)
        forward_scale = inverse_rms(forward_x_float)
        normed = (forward_x_float * forward_scale * gain_row).astype(jnp.bfloat16)
        forward_onehot, forward_placing = route_tables(forward_ids_part, owners, capacity)
        row_block = jnp.einsum(
            "okr,rd->okd", forward_placing, normed, preferred_element_type=jnp.float32
        ).astype(jnp.bfloat16)
        pair_block = gate_slots(forward_onehot, gates_part, forward_placing, experts_here)
        f_valid, f_pick, layer_in, x_float, f_placing, row_block, pair_block = (
            forward_is_valid,
            forward_slot_pick,
            forward_layer_in,
            forward_x_float,
            forward_placing,
            row_block,
            pair_block,
        )
        got_rows, got_pairs = send_rows(row_block, pair_block)
        flat_rows = got_rows.reshape(slot_count, width)
        flat_pairs = got_pairs.reshape(slot_count, experts_here)
        result, joint_pre = lax.cond(f_valid, run_forward, skip_forward, (flat_rows, flat_pairs))
        returned = return_rows(result.reshape(owners, capacity, width))
        branch = jnp.einsum("okr,okd->rd", f_placing, returned, preferred_element_type=jnp.float32)
        layer_out = (x_float + branch).astype(jnp.bfloat16)
        layer_outs = lax.dynamic_update_index_in_dim(layer_outs, layer_out, f_pick, 0)
        layer_ins = lax.dynamic_update_index_in_dim(layer_ins, layer_in, f_pick, 0)
        kept_joint = lax.dynamic_update_index_in_dim(kept_joint, joint_pre, f_pick, 0)
        kept_pairs = lax.dynamic_update_index_in_dim(kept_pairs, flat_pairs, f_pick, 0)
        if tick_num + 1 < ticks:
            incoming = from_behind(layer_out, PIPE, 1)
    incoming = jnp.zeros((micro_rows, width), jnp.bfloat16)
    for tick_num in range(ticks):
        backward_is_valid, backward_slot_pick, backward_start_row = timing(
            tick_num - (segments - 1 - segment_index)
        )
        own_part = lax.dynamic_slice_in_dim(cotangent, backward_start_row, micro_rows, 0)
        backward_grad_in = jnp.where(segment_index == segments - 1, own_part, incoming)
        ids_part = lax.dynamic_slice_in_dim(layer_ids, backward_start_row, micro_rows, 0)
        backward_layer_in = lax.dynamic_index_in_dim(
            layer_ins, backward_slot_pick, 0, keepdims=False
        )
        backward_x_float = backward_layer_in.astype(jnp.float32)
        backward_scale = inverse_rms(backward_x_float)
        _, backward_placing = route_tables(ids_part, owners, capacity)
        grad_block = jnp.einsum(
            "okr,rd->okd", backward_placing, backward_grad_in, preferred_element_type=jnp.float32
        ).astype(jnp.bfloat16)
        b_valid, b_pick, grad_in, bx_float, b_scale, b_placing, grad_block = (
            backward_is_valid,
            backward_slot_pick,
            backward_grad_in,
            backward_x_float,
            backward_scale,
            backward_placing,
            grad_block,
        )
        got_grads = send_grads(grad_block).reshape(slot_count, width)
        joint_keep = lax.dynamic_index_in_dim(kept_joint, b_pick, 0, keepdims=False)
        pair_keep = lax.dynamic_index_in_dim(kept_pairs, b_pick, 0, keepdims=False)
        owner_grad = lax.cond(
            b_valid, run_backward, skip_backward, (got_grads, pair_keep, joint_keep)
        )
        returned = return_grads(owner_grad.reshape(owners, capacity, width))
        normed_grad = jnp.einsum(
            "okr,okd->rd", b_placing, returned, preferred_element_type=jnp.float32
        )
        weighted = gain_row * normed_grad
        grad_x = (
            grad_in.astype(jnp.float32)
            + b_scale * weighted
            - bx_float
            * b_scale
            * b_scale
            * b_scale
            * jnp.mean(weighted * bx_float, axis=-1, keepdims=True)
        )
        gain_term = jnp.where(b_valid, jnp.sum(normed_grad * bx_float * b_scale, axis=0), 0.0)
        grad_bf, gain_term = (grad_x.astype(jnp.bfloat16), gain_term)
        grad_outs = lax.dynamic_update_index_in_dim(grad_outs, grad_bf, b_pick, 0)
        gain_sum = gain_sum + gain_term
        if tick_num + 1 < ticks:
            incoming = from_behind(grad_bf, PIPE, -1)
    gain_grad = lax.psum(gain_sum, (DP, EXPERT))
    segment_out = layer_outs[:MICRO].reshape(1, tok_rows, width)
    segment_grad = grad_outs[:MICRO].reshape(1, tok_rows, width)
    return (segment_out, segment_grad, gain_grad.reshape(1, width))


def swap_cores(value):
    count = lax.axis_size(EXPERT)
    return lax.ppermute(value, EXPERT, [(e, e ^ 1) for e in range(count)])


def shifted(value, dp_step, chip_step):
    dps, experts = (lax.axis_size(name) for name in (DP, EXPERT))
    pairs = []
    for dp in range(dps):
        for expert in range(experts):
            target = (dp + dp_step) % dps * experts + (expert + 2 * chip_step) % experts
            pairs.append((dp * experts + expert, target))
    return lax.ppermute(value, (DP, EXPERT), pairs)


def hopped(value, step):
    stages = lax.axis_size(PIPE)
    return lax.ppermute(value, PIPE, [(s, (s + step) % stages) for s in range(stages)])


def chip_steps():
    dps, chips = lax.axis_size(DP), lax.axis_size(EXPERT) // 2
    steps = [(d, c) for d in range(dps) for c in range(chips)]
    return sorted(steps[1:], key=lambda step: -(step[0] + step[1]))


def spread(rows):
    return [rows] + [shifted(rows, d, c) for d, c in chip_steps()]


def returned(blocks, which):
    dps, chips = lax.axis_size(DP), lax.axis_size(EXPERT) // 2
    dp, chip = chip_steps()[which - 1]
    return shifted(blocks[which], -dp % dps, -chip % chips)


def collect(blocks):
    return [blocks[0]] + [returned(blocks, which) for which in range(1, len(blocks))]


VMEM = pl.BlockSpec(memory_space=pltpu.VMEM)
CHUNK = 256
LANES = 128
HALVES = 2


def in_vmem(kernel, outs, scratch, flops, *operands, specs=None):
    moved = sum(math.prod(a.shape) * a.dtype.itemsize for a in [*outs, *operands])
    return pl.pallas_call(
        kernel,
        out_shape=outs,
        in_specs=specs or [VMEM] * len(operands),
        out_specs=[VMEM] * len(outs),
        scratch_shapes=scratch,
        compiler_params=pltpu.CompilerParams(vmem_limit_bytes=LIMIT),
        cost_estimate=pl.CostEstimate(flops=flops, bytes_accessed=moved, transcendentals=0),
    )(*operands)


def load_kernel(gate_ref, up_ref, down_ref, joint_out, down_out, sems):
    ff = gate_ref.shape[1]
    copies = [
        pltpu.make_async_copy(gate_ref, joint_out.at[:, :ff], sems.at[0]),
        pltpu.make_async_copy(up_ref, joint_out.at[:, ff:], sems.at[1]),
        pltpu.make_async_copy(down_ref, down_out, sems.at[2]),
    ]
    for copy in copies:
        copy.start()
    for copy in copies:
        copy.wait()


def loaded(gate, up, down):
    outs = [pltpu.VMEM((gate.shape[0], 2 * gate.shape[1]), gate.dtype), pltpu.VMEM(down.shape, down.dtype)]
    specs = [pl.BlockSpec(memory_space=pl.ANY)] * 3
    return in_vmem(load_kernel, outs, [pltpu.SemaphoreType.DMA((3,))], 0, gate, up, down, specs=specs)


def stage_kernel(out_ref):
    out_ref[...] = jnp.full(out_ref.shape, lax.axis_index(PIPE), jnp.int32)


def first_rows_kernel(token_ref, id_hbm, gate_hbm, out_ref, copied, id_ref, gate_ref, sems):
    rows, width = copied.shape
    copy = pltpu.make_async_copy(token_ref.at[pl.ds(0, rows), :], copied, sems.at[0])
    id_copy = pltpu.make_async_copy(id_hbm, id_ref, sems.at[1])
    gate_copy = pltpu.make_async_copy(gate_hbm, gate_ref, sems.at[2])
    for each in (id_copy, gate_copy, copy):
        each.start()
    owners = lax.axis_size(DP) * lax.axis_size(EXPERT)
    column = lax.broadcasted_iota(jnp.int32, (rows, out_ref.shape[1] - width), 1)
    table = jnp.zeros(column.shape, jnp.float32)
    id_copy.wait()
    gate_copy.wait()
    ids, gates = id_ref[...].T, gate_ref[...].astype(jnp.float32).T
    for micro in range(MICRO):
        window = slice(micro * rows, (micro + 1) * rows)
        for slot in range(ids.shape[1]):
            place = micro * owners + ids[window, slot:slot + 1]
            table = table + jnp.where(column == place, gates[window, slot:slot + 1], 0.0)
    out_ref[:, width:] = table.astype(jnp.bfloat16)
    copy.wait()
    out_ref[:, :width] = copied[...]


def first_rows(tokens, ids, gates):
    rows, width = tokens.shape[0] // MICRO, tokens.shape[1]
    owners = lax.axis_size(DP) * lax.axis_size(EXPERT)
    extra = -(-MICRO * owners // LANES) * LANES
    outs = [jax.ShapeDtypeStruct((rows, width + extra), tokens.dtype)]
    scratch = [pltpu.VMEM((rows, width), tokens.dtype), pltpu.VMEM(ids.shape, ids.dtype)]
    scratch += [pltpu.VMEM(gates.shape, gates.dtype), pltpu.SemaphoreType.DMA((3,))]
    specs = [pl.BlockSpec(memory_space=pl.ANY)] * 3
    tokens, ids, gates = (pltpu.with_memory_space_constraint(value, pltpu.HBM) for value in (tokens, ids, gates))
    return in_vmem(first_rows_kernel, outs, scratch, 0, tokens, ids, gates, specs=specs)[0]


def turn_kernel(in_ref, out_ref):
    size = math.gcd(in_ref.shape[0], CHUNK)

    @pl.loop(0, in_ref.shape[0] // size)
    def _(at):
        window = pl.ds(pl.multiple_of(at * size, size), size)
        out_ref[:, window] = in_ref[window, :].T


def turned(part):
    outs = [pltpu.VMEM(part.shape[::-1], part.dtype)]
    return in_vmem(turn_kernel, outs, [], 0, part)[0]


def in_chunks(width, halves=HALVES):
    half = width // halves

    def run(work):
        @pl.loop(0, halves)
        def _(at):
            for start in range(0, half, CHUNK):
                work(pl.ds(pl.multiple_of(at * half + start, CHUNK), CHUNK))

    return run


def owner_number():
    return lax.axis_index(DP) * lax.axis_size(EXPERT) + lax.axis_index(EXPERT)


def forward_kernel(blocks, tick, *refs):
    row_refs, table_refs, refs = refs[:blocks], refs[blocks:2 * blocks], refs[2 * blocks:]
    gain_ref, *weight_refs = refs[:5]
    rate_ref, flat_ref, own_ref, *part_refs, pre, hidden = refs[5:]
    rows, width = own_ref.shape
    ff = weight_refs[2].shape[0]
    gain = gain_ref[...]
    for k, row_ref in enumerate(row_refs):
        x = row_ref[:, :width].astype(jnp.float32)
        flat_ref[k * rows:(k + 1) * rows, :] = (x * inverse_rms(x) * gain).astype(jnp.bfloat16)
    micro = tick - lax.axis_index(PIPE)
    is_valid = (micro >= 0) & (micro < MICRO)
    routed = jnp.concatenate([ref[:, width:] for ref in table_refs], axis=0).astype(jnp.float32)
    column = lax.broadcasted_iota(jnp.int32, routed.shape, 1)
    me, owners = owner_number(), lax.axis_size(DP) * lax.axis_size(EXPERT)
    for e, owner in enumerate((me, me ^ 1)):
        is_routed = (column == micro * owners + owner) & is_valid
        weight = jnp.sum(jnp.where(is_routed, routed, 0.0), axis=1, keepdims=True)
        for start in range(0, 2 * ff, CHUNK):
            pre[:, start:start + CHUNK] = jnp.dot(
                flat_ref[...], weight_refs[e][:, start:start + CHUNK], preferred_element_type=jnp.float32
            )
        gate_pre, up_pre = pre[:, :ff], pre[:, ff:]
        sigma = jax.nn.sigmoid(gate_pre)
        up_rate = weight * gate_pre * sigma
        hidden[:, e * ff:(e + 1) * ff] = (up_rate * up_pre).astype(jnp.bfloat16)
        rate_ref[:, 2 * e * ff:(2 * e + 1) * ff] = weight * up_pre * sigma * (1.0 + gate_pre * (1.0 - sigma))
        rate_ref[:, (2 * e + 1) * ff:(2 * e + 2) * ff] = up_rate

    @in_chunks(width)
    def _(columns):
        partial = sum(
            jnp.dot(hidden[:, e * ff:(e + 1) * ff], weight_refs[2 + e][:, columns], preferred_element_type=jnp.float32)
            for e in range(2)
        )
        own_ref[:, columns] = row_refs[0][:, columns].astype(jnp.float32) + partial[:rows]
        for k, part_ref in enumerate(part_refs):
            part_ref[:, columns] = partial[(k + 1) * rows:(k + 2) * rows].astype(jnp.bfloat16)


def backward_kernel(blocks, first, picks, saves, *refs):
    row_refs, refs = refs[:blocks], refs[blocks:]
    rate_refs, normed_refs, refs = refs[:saves], refs[saves:2 * saves], refs[2 * saves:]
    weight_refs, (gain_ref, own_ref, *part_refs, flat, rate, normed, hidden, sems) = refs[:4], refs[4:]
    rows, width = row_refs[0].shape
    ff = weight_refs[2].shape[1]
    stage = lax.axis_index(PIPE)

    def copies(at):
        return (
            pltpu.make_async_copy(rate_refs[at], rate, sems.at[0]),
            pltpu.make_async_copy(normed_refs[at], normed, sems.at[1]),
        )

    for at in range(saves):
        holders = [s for s, picked in enumerate(picks) if picked == at]

        @pl.when(functools.reduce(jnp.logical_or, [stage == s for s in holders]))
        def _():
            for copy in copies(at):
                copy.start()

    for k, row_ref in enumerate(row_refs):
        flat[k * rows:(k + 1) * rows, :] = row_ref[...]
    micro = first + stage
    kept = jnp.where((micro >= 0) & (micro < MICRO), 1.0, 0.0)
    for e in range(2):
        q = jnp.dot(flat[...], weight_refs[2 + e][...], preferred_element_type=jnp.float32) * kept
        if e == 0:
            for copy in copies(0):
                copy.wait()
        for half in range(2):
            columns = slice((2 * e + half) * ff, (2 * e + half + 1) * ff)
            hidden[:, columns] = (q * rate[:, columns]).astype(jnp.bfloat16)

    @in_chunks(width, 1 if first > 0 else HALVES)
    def _(columns):
        partial = sum(
            jnp.dot(
                hidden[:, 2 * e * ff:(2 * e + 2) * ff], weight_refs[e][:, columns], preferred_element_type=jnp.float32
            )
            for e in range(2)
        )
        gain_ref[:, columns] = jnp.sum(partial * normed[:, columns].astype(jnp.float32), axis=0, keepdims=True)
        own_ref[:, columns] = partial[:rows]
        for k, part_ref in enumerate(part_refs):
            part_ref[:, columns] = partial[(k + 1) * rows:(k + 2) * rows].astype(jnp.bfloat16)


def forward_experts(tick, row_blocks, tables, gain, weights):
    blocks, rows, width = len(row_blocks), row_blocks[0].shape[0], gain.shape[1]
    total, ff = blocks * rows, weights[2].shape[0]
    outs = [
        jax.ShapeDtypeStruct((total, 4 * ff), jnp.float32),
        jax.ShapeDtypeStruct((total, width), jnp.bfloat16),
        jax.ShapeDtypeStruct((rows, width), jnp.float32),
    ]
    outs += [jax.ShapeDtypeStruct((rows, width), jnp.bfloat16)] * (blocks - 1)
    scratch = [pltpu.VMEM((total, 2 * ff), jnp.float32), pltpu.VMEM((total, 2 * ff), jnp.bfloat16)]
    kernel = functools.partial(forward_kernel, blocks, tick)
    flops = 12 * total * width * ff
    rate, normed, *parts = in_vmem(kernel, outs, scratch, flops, *row_blocks, *tables, gain, *weights)
    return rate, normed, parts


def backward_experts(first, picks, row_blocks, rates, normeds, weights):
    blocks, (rows, width) = len(row_blocks), row_blocks[0].shape
    total, wide = rates[0].shape
    outs = [jax.ShapeDtypeStruct((1, width), jnp.float32), jax.ShapeDtypeStruct((rows, width), jnp.float32)]
    outs += [jax.ShapeDtypeStruct((rows, width), jnp.bfloat16)] * (blocks - 1)
    scratch = [
        pltpu.VMEM((total, width), jnp.bfloat16),
        pltpu.VMEM((total, wide), jnp.float32),
        pltpu.VMEM((total, width), jnp.bfloat16),
        pltpu.VMEM((total, wide), jnp.bfloat16),
        pltpu.SemaphoreType.DMA((2,)),
    ]
    used = sorted(set(picks))
    kernel = functools.partial(backward_kernel, blocks, first, [used.index(at) for at in picks], len(used))
    anywhere = pl.BlockSpec(memory_space=pl.ANY)
    specs = [VMEM] * blocks + [anywhere] * (2 * len(used)) + [VMEM] * 4
    saved = [rates[at] for at in used] + [normeds[at] for at in used]
    flops = 3 * total * width * wide
    gained, *parts = in_vmem(kernel, outs, scratch, flops, *row_blocks, *saved, *weights, specs=specs)
    return gained, parts


def summed_over_owners(value):
    value = value + swap_cores(value)
    return sum(spread(value))


def dense_body(tokens, cotangent, owner_ids, gate_weights, norm_gain, w_gate, w_up, w_down):
    f32, bf16 = jnp.float32, jnp.bfloat16
    stages = lax.axis_size(PIPE)
    tok_rows, width = tokens.shape
    rows = tok_rows // MICRO
    gain = norm_gain[0][None, :]
    ticks = MICRO + stages - 1
    stage = in_vmem(stage_kernel, [jax.ShapeDtypeStruct((1, width), jnp.int32)], [], 0)[0]

    own = [pltpu.with_memory_space_constraint(w[0, 0], pltpu.HBM) for w in (w_gate, w_up, w_down)]
    theirs = [swap_cores(w) for w in own]
    joint, down = loaded(*own)
    pair_joint, pair_down = loaded(*[pltpu.with_memory_space_constraint(w, pltpu.VMEM) for w in theirs])
    forward_weights = (joint, pair_joint, down, pair_down)
    backward_weights = []
    for number, part in enumerate(forward_weights):
        backward_weights.append(turned(part))

    def choose(values):
        found = values[0]
        for s, value in enumerate(values):
            if value is not found:
                found = jnp.where(stage == s, value, found)
        return found

    rates, normeds, ins, outs, grads = [], [], [], [], []
    gain_sum = jnp.zeros((1, width), f32)
    behind = ahead = None
    last = ticks + stages - 2
    for tick in range(last + 1):
        if tick == stages - 1:
            grad_blocks = spread(lax.optimization_barrier((cotangent[:rows], *outs[-1:]))[0])
        if tick < ticks:
            if tick == 0:
                here = first_rows(tokens, owner_ids[0].T, gate_weights[0].T)
            elif tick < MICRO:
                here = jnp.where(stage == 0, tokens[tick * rows:(tick + 1) * rows], behind)
            else:
                here = behind
            here_blocks = spread(here)
            if tick == 0:
                tables = here_blocks
            rate, normed, parts = forward_experts(tick, here_blocks, tables, gain, forward_weights)
            rates.append(rate)
            normeds.append(normed)
            ins.append(here[:, :width])
            if tick + 1 < ticks:
                parts = collect(parts)
                outs.append(lax.optimization_barrier(sum(p.astype(f32) for p in parts).astype(bf16)))
                behind = hopped(outs[-1], 1)
        number = tick - (stages - 1)
        if number >= 0:
            first = number - (stages - 1)
            picks = [min(max(first + 2 * s, 0), min(ticks - 1, tick)) for s in range(stages)]
            if number == 0:
                grad = cotangent[:rows]
            elif number < MICRO:
                grad = jnp.where(stage == stages - 1, cotangent[number * rows:(number + 1) * rows], ahead)
            else:
                grad = ahead
            if number:
                grad_blocks = spread(grad)
            gained, sums = backward_experts(first, picks, grad_blocks, rates, normeds, backward_weights)
            sums = collect(sums)
            normed_grad = sum(p.astype(f32) for p in sums)
            x = choose([ins[at] for at in picks]).astype(f32)
            scale = inverse_rms(x)
            weighted = gain * normed_grad
            grad_x = (
                grad.astype(f32)
                + scale * weighted
                - x * scale * scale * scale * jnp.mean(weighted * x, axis=-1, keepdims=True)
            ).astype(bf16)
            gain_sum = gain_sum + gained
            if tick < last:
                grad_x = lax.optimization_barrier(grad_x)
            grads.append(grad_x)
            if tick < last:
                ahead = hopped(grad_x, -1)
            if tick + 1 == ticks:
                waiting, kept = parts, parts[:1]
            while tick + 1 >= ticks and len(kept) < len(waiting) and (tick - ticks + 2 >= len(kept) or tick + 1 == last):
                kept.append(returned(lax.optimization_barrier((waiting, grad_x))[0], len(kept)))
    outs.append(sum(part.astype(f32) for part in kept).astype(bf16))
    gain_grad = summed_over_owners(gain_sum) / gain
    segment_out = jnp.concatenate([choose([outs[m + s] for s in range(stages)]) for m in range(MICRO)])
    grad_parts = [choose([grads[m + stages - 1 - s] for s in range(stages)]) for m in range(MICRO)]
    settled = lax.optimization_barrier(jnp.concatenate([*grad_parts[:-1], jnp.zeros_like(grad_parts[-1])]))
    segment_grad = lax.dynamic_update_slice_in_dim(settled, grad_parts[-1], tok_rows - rows, 0)
    return (segment_out[None], segment_grad[None], gain_grad)


def body(tokens, cotangent, owner_ids, *rest):
    owners = lax.axis_size(DP) * lax.axis_size(EXPERT)
    routed_densely = owners <= 2 * owner_ids.shape[2] and lax.axis_size(EXPERT) % 2 == 0
    plan = dense_body if routed_densely else slot_body
    return plan(tokens, cotangent, owner_ids, *rest)


def solution(mesh):
    in_specs = (
        P((DP, EXPERT), None),
        P((DP, EXPERT), None),
        P(PIPE, (DP, EXPERT), None),
        P(PIPE, (DP, EXPERT), None),
        P(PIPE, None),
        P(PIPE, (DP, EXPERT), None, None),
        P(PIPE, (DP, EXPERT), None, None),
        P(PIPE, (DP, EXPERT), None, None),
    )
    out_specs = (
        P(PIPE, (DP, EXPERT), None),
        P(PIPE, (DP, EXPERT), None),
        P(PIPE, None),
    )
    return jax.shard_map(body, mesh=mesh, in_specs=in_specs, out_specs=out_specs, check_vma=False)
```

```python
import jax
import jax.numpy as jnp
from jax import lax
from jax.experimental import pallas as pl
from jax.experimental.pallas import tpu as pltpu
import functools
import math
from jax.sharding import PartitionSpec as P

MICRO = 4
LIMIT = 12 * 1024 * 1024
DP, PIPE, EXPERT = "dp", "pipe", "expert"


epsilon = 1e-06


def from_behind(value, axis, steps):
    count = lax.axis_size(axis)
    leading, last = (max(0, -steps), min(count, count - steps))
    return lax.ppermute(value, axis, [(source, source + steps) for source in range(leading, last)])


def inverse_rms(values):
    return lax.rsqrt(jnp.mean(values * values, axis=-1, keepdims=True) + epsilon)


def contract_last(left, right):
    return lax.dot_general(
        left, right, (((1,), (1,)), ((), ())), preferred_element_type=jnp.float32
    )


def route_tables(ids_part, owners, capacity):
    owner_range = jnp.arange(owners, dtype=jnp.int32)
    onehot = (ids_part[:, :, None] == owner_range[None, None, :]).astype(jnp.int32)
    member = jnp.sum(onehot, axis=1)
    position = jnp.cumsum(member, axis=0) - member
    slot_range = jnp.arange(capacity, dtype=jnp.int32)
    placed = (position[:, :, None] == slot_range[None, None, :]) & (member[:, :, None] > 0)
    placing = jnp.transpose(placed, (1, 2, 0)).astype(jnp.bfloat16)
    return (onehot.astype(jnp.float32), placing)


def gate_slots(onehot, gates_part, placing, experts_here):
    gate_pairs = gates_part.astype(jnp.float32).reshape(gates_part.shape[0], -1, experts_here)
    chosen = jnp.einsum("rjo,rjc->roc", onehot, gate_pairs)
    return jnp.einsum("okr,roc->okc", placing.astype(jnp.float32), chosen).astype(jnp.bfloat16)


def send_rows(row_block, pair_block):
    got_rows, got_pairs = (
        lax.all_to_all(row_block, (DP, EXPERT), split_axis=0, concat_axis=0, tiled=True),
        lax.all_to_all(pair_block, (DP, EXPERT), split_axis=0, concat_axis=0, tiled=True),
    )
    return (got_rows, got_pairs)


def return_rows(row_block):
    return lax.all_to_all(row_block, (DP, EXPERT), split_axis=0, concat_axis=0, tiled=True)


def send_grads(row_block):
    return lax.all_to_all(row_block, (DP, EXPERT), split_axis=0, concat_axis=0, tiled=True)


def return_grads(row_block):
    return lax.all_to_all(row_block, (DP, EXPERT), split_axis=0, concat_axis=0, tiled=True)


def expert_forward(flat_rows, flat_pairs, joint_mats, down_mats):
    hidden_width = down_mats.shape[1]
    joint_pre = jnp.dot(flat_rows, joint_mats[0], preferred_element_type=jnp.float32)
    gate_pre = joint_pre[:, :hidden_width]
    up_pre = joint_pre[:, hidden_width:]
    hidden = (jax.nn.silu(gate_pre) * up_pre).astype(jnp.bfloat16)
    projected = jnp.dot(hidden, down_mats[0], preferred_element_type=jnp.float32)
    term = flat_pairs.astype(jnp.float32) * projected
    kept_both = [joint_pre]
    return (term.astype(jnp.bfloat16), jnp.stack(kept_both))


def expert_backward(grad_rows, flat_pairs, joint_keep, joint_mats, down_mats):
    hidden_width = down_mats.shape[1]
    q_vals = contract_last(grad_rows, down_mats[0])
    gate_pre = joint_keep[0][:, :hidden_width]
    up_pre = joint_keep[0][:, hidden_width:]
    sigma = jax.nn.sigmoid(gate_pre)
    weight = flat_pairs.astype(jnp.float32)
    d_gate = (q_vals * weight * up_pre * sigma * (1.0 + gate_pre * (1.0 - sigma))).astype(
        jnp.bfloat16
    )
    d_up = (q_vals * weight * gate_pre * sigma).astype(jnp.bfloat16)
    joint_grad = jnp.concatenate([d_gate, d_up], axis=1)
    term = contract_last(joint_grad, joint_mats[0])
    return term.astype(jnp.bfloat16)


def slot_body(tokens, cotangent, owner_ids, gate_weights, norm_gain, w_gate, w_up, w_down):
    segments = lax.axis_size(PIPE)
    segment_index = lax.axis_index(PIPE)
    owners = lax.axis_size(DP) * lax.axis_size(EXPERT)
    tok_rows = tokens.shape[0]
    width = tokens.shape[1]
    micro_rows = tok_rows // MICRO
    route_count = owner_ids.shape[2]
    capacity = max(2, (5 * micro_rows * route_count + 4 * owners - 1) // (4 * owners))
    slot_count = owners * capacity
    gain_row = norm_gain[0]
    joint_mats = jnp.concatenate([w_gate[0], w_up[0]], axis=2)
    down_mats = w_down[0]
    layer_ids = owner_ids[0]
    layer_gates = gate_weights[0]
    experts_here = joint_mats.shape[0]
    joint_width = joint_mats.shape[2]

    def skip_forward(operands):
        return (
            jnp.zeros((slot_count, width), jnp.bfloat16),
            jnp.zeros((experts_here, slot_count, joint_width), jnp.float32),
        )

    def run_forward(operands):
        return expert_forward(operands[0], operands[1], joint_mats, down_mats)

    def skip_backward(operands):
        return jnp.zeros((slot_count, width), jnp.bfloat16)

    def run_backward(operands):
        return expert_backward(operands[0], operands[1], operands[2], joint_mats, down_mats)

    def timing(micro):
        is_valid = (micro >= 0) & (micro < MICRO)
        slot_pick = jnp.where(is_valid, micro, MICRO)
        start_row = jnp.clip(micro, 0, MICRO - 1) * micro_rows
        return (is_valid, slot_pick, start_row)

    layer_outs = jnp.zeros((MICRO + 1, micro_rows, width), jnp.bfloat16)
    layer_ins = jnp.zeros((MICRO + 1, micro_rows, width), jnp.bfloat16)
    kept_joint = jnp.zeros((MICRO + 1, experts_here, slot_count, joint_width), jnp.float32)
    kept_pairs = jnp.zeros((MICRO + 1, slot_count, experts_here), jnp.bfloat16)
    grad_outs = jnp.zeros((MICRO + 1, micro_rows, width), jnp.bfloat16)
    gain_sum = jnp.zeros((width,), jnp.float32)
    ticks = MICRO + segments - 1
    incoming = jnp.zeros((micro_rows, width), jnp.bfloat16)
    for tick_num in range(ticks):
        forward_is_valid, forward_slot_pick, forward_start_row = timing(tick_num - segment_index)
        forward_own_part = lax.dynamic_slice_in_dim(tokens, forward_start_row, micro_rows, 0)
        forward_layer_in = jnp.where(segment_index == 0, forward_own_part, incoming)
        forward_ids_part = lax.dynamic_slice_in_dim(layer_ids, forward_start_row, micro_rows, 0)
        gates_part = lax.dynamic_slice_in_dim(layer_gates, forward_start_row, micro_rows, 0)
        forward_x_float = forward_layer_in.astype(jnp.float32)
        forward_scale = inverse_rms(forward_x_float)
        normed = (forward_x_float * forward_scale * gain_row).astype(jnp.bfloat16)
        forward_onehot, forward_placing = route_tables(forward_ids_part, owners, capacity)
        row_block = jnp.einsum(
            "okr,rd->okd", forward_placing, normed, preferred_element_type=jnp.float32
        ).astype(jnp.bfloat16)
        pair_block = gate_slots(forward_onehot, gates_part, forward_placing, experts_here)
        f_valid, f_pick, layer_in, x_float, f_placing, row_block, pair_block = (
            forward_is_valid,
            forward_slot_pick,
            forward_layer_in,
            forward_x_float,
            forward_placing,
            row_block,
            pair_block,
        )
        got_rows, got_pairs = send_rows(row_block, pair_block)
        flat_rows = got_rows.reshape(slot_count, width)
        flat_pairs = got_pairs.reshape(slot_count, experts_here)
        result, joint_pre = lax.cond(f_valid, run_forward, skip_forward, (flat_rows, flat_pairs))
        returned = return_rows(result.reshape(owners, capacity, width))
        branch = jnp.einsum("okr,okd->rd", f_placing, returned, preferred_element_type=jnp.float32)
        layer_out = (x_float + branch).astype(jnp.bfloat16)
        layer_outs = lax.dynamic_update_index_in_dim(layer_outs, layer_out, f_pick, 0)
        layer_ins = lax.dynamic_update_index_in_dim(layer_ins, layer_in, f_pick, 0)
        kept_joint = lax.dynamic_update_index_in_dim(kept_joint, joint_pre, f_pick, 0)
        kept_pairs = lax.dynamic_update_index_in_dim(kept_pairs, flat_pairs, f_pick, 0)
        if tick_num + 1 < ticks:
            incoming = from_behind(layer_out, PIPE, 1)
    incoming = jnp.zeros((micro_rows, width), jnp.bfloat16)
    for tick_num in range(ticks):
        backward_is_valid, backward_slot_pick, backward_start_row = timing(
            tick_num - (segments - 1 - segment_index)
        )
        own_part = lax.dynamic_slice_in_dim(cotangent, backward_start_row, micro_rows, 0)
        backward_grad_in = jnp.where(segment_index == segments - 1, own_part, incoming)
        ids_part = lax.dynamic_slice_in_dim(layer_ids, backward_start_row, micro_rows, 0)
        backward_layer_in = lax.dynamic_index_in_dim(
            layer_ins, backward_slot_pick, 0, keepdims=False
        )
        backward_x_float = backward_layer_in.astype(jnp.float32)
        backward_scale = inverse_rms(backward_x_float)
        _, backward_placing = route_tables(ids_part, owners, capacity)
        grad_block = jnp.einsum(
            "okr,rd->okd", backward_placing, backward_grad_in, preferred_element_type=jnp.float32
        ).astype(jnp.bfloat16)
        b_valid, b_pick, grad_in, bx_float, b_scale, b_placing, grad_block = (
            backward_is_valid,
            backward_slot_pick,
            backward_grad_in,
            backward_x_float,
            backward_scale,
            backward_placing,
            grad_block,
        )
        got_grads = send_grads(grad_block).reshape(slot_count, width)
        joint_keep = lax.dynamic_index_in_dim(kept_joint, b_pick, 0, keepdims=False)
        pair_keep = lax.dynamic_index_in_dim(kept_pairs, b_pick, 0, keepdims=False)
        owner_grad = lax.cond(
            b_valid, run_backward, skip_backward, (got_grads, pair_keep, joint_keep)
        )
        returned = return_grads(owner_grad.reshape(owners, capacity, width))
        normed_grad = jnp.einsum(
            "okr,okd->rd", b_placing, returned, preferred_element_type=jnp.float32
        )
        weighted = gain_row * normed_grad
        grad_x = (
            grad_in.astype(jnp.float32)
            + b_scale * weighted
            - bx_float
            * b_scale
            * b_scale
            * b_scale
            * jnp.mean(weighted * bx_float, axis=-1, keepdims=True)
        )
        gain_term = jnp.where(b_valid, jnp.sum(normed_grad * bx_float * b_scale, axis=0), 0.0)
        grad_bf, gain_term = (grad_x.astype(jnp.bfloat16), gain_term)
        grad_outs = lax.dynamic_update_index_in_dim(grad_outs, grad_bf, b_pick, 0)
        gain_sum = gain_sum + gain_term
        if tick_num + 1 < ticks:
            incoming = from_behind(grad_bf, PIPE, -1)
    gain_grad = lax.psum(gain_sum, (DP, EXPERT))
    segment_out = layer_outs[:MICRO].reshape(1, tok_rows, width)
    segment_grad = grad_outs[:MICRO].reshape(1, tok_rows, width)
    return (segment_out, segment_grad, gain_grad.reshape(1, width))


def swap_cores(value):
    count = lax.axis_size(EXPERT)
    return lax.ppermute(value, EXPERT, [(e, e ^ 1) for e in range(count)])


def shifted(value, dp_step, chip_step):
    dps, experts = (lax.axis_size(name) for name in (DP, EXPERT))
    pairs = []
    for dp in range(dps):
        for expert in range(experts):
            target = (dp + dp_step) % dps * experts + (expert + 2 * chip_step) % experts
            pairs.append((dp * experts + expert, target))
    return lax.ppermute(value, (DP, EXPERT), pairs)


def hopped(value, step):
    stages = lax.axis_size(PIPE)
    return lax.ppermute(value, PIPE, [(s, (s + step) % stages) for s in range(stages)])


def chip_steps():
    dps, chips = lax.axis_size(DP), lax.axis_size(EXPERT) // 2
    steps = [(d, c) for d in range(dps) for c in range(chips)]
    return sorted(steps[1:], key=lambda step: -(step[0] + step[1]))


def spread(rows):
    return [rows] + [shifted(rows, d, c) for d, c in chip_steps()]


def returned(blocks, which):
    dps, chips = lax.axis_size(DP), lax.axis_size(EXPERT) // 2
    dp, chip = chip_steps()[which - 1]
    return shifted(blocks[which], -dp % dps, -chip % chips)


def collect(blocks):
    return [blocks[0]] + [returned(blocks, which) for which in range(1, len(blocks))]


VMEM = pl.BlockSpec(memory_space=pltpu.VMEM)
CHUNK = 256
LANES = 128
HALVES = 2


def in_vmem(kernel, outs, scratch, flops, *operands, specs=None):
    moved = sum(math.prod(a.shape) * a.dtype.itemsize for a in [*outs, *operands])
    return pl.pallas_call(
        kernel,
        out_shape=outs,
        in_specs=specs or [VMEM] * len(operands),
        out_specs=[VMEM] * len(outs),
        scratch_shapes=scratch,
        compiler_params=pltpu.CompilerParams(vmem_limit_bytes=LIMIT),
        cost_estimate=pl.CostEstimate(flops=flops, bytes_accessed=moved, transcendentals=0),
    )(*operands)


def load_kernel(gate_ref, up_ref, down_ref, joint_out, down_out, sems):
    ff = gate_ref.shape[1]
    copies = [
        pltpu.make_async_copy(gate_ref, joint_out.at[:, :ff], sems.at[0]),
        pltpu.make_async_copy(up_ref, joint_out.at[:, ff:], sems.at[1]),
        pltpu.make_async_copy(down_ref, down_out, sems.at[2]),
    ]
    for copy in copies:
        copy.start()
    for copy in copies:
        copy.wait()


def loaded(gate, up, down):
    outs = [pltpu.VMEM((gate.shape[0], 2 * gate.shape[1]), gate.dtype), pltpu.VMEM(down.shape, down.dtype)]
    specs = [pl.BlockSpec(memory_space=pl.ANY)] * 3
    return in_vmem(load_kernel, outs, [pltpu.SemaphoreType.DMA((3,))], 0, gate, up, down, specs=specs)


def stage_kernel(out_ref):
    out_ref[...] = jnp.full(out_ref.shape, lax.axis_index(PIPE), jnp.int32)


def first_rows_kernel(token_ref, id_hbm, gate_hbm, out_ref, copied, id_ref, gate_ref, sems):
    rows, width = copied.shape
    copy = pltpu.make_async_copy(token_ref.at[pl.ds(0, rows), :], copied, sems.at[0])
    id_copy = pltpu.make_async_copy(id_hbm, id_ref, sems.at[1])
    gate_copy = pltpu.make_async_copy(gate_hbm, gate_ref, sems.at[2])
    for each in (id_copy, gate_copy, copy):
        each.start()
    owners = lax.axis_size(DP) * lax.axis_size(EXPERT)
    column = lax.broadcasted_iota(jnp.int32, (rows, out_ref.shape[1] - width), 1)
    table = jnp.zeros(column.shape, jnp.float32)
    id_copy.wait()
    gate_copy.wait()
    ids, gates = id_ref[...].T, gate_ref[...].astype(jnp.float32).T
    for micro in range(MICRO):
        window = slice(micro * rows, (micro + 1) * rows)
        for slot in range(ids.shape[1]):
            place = micro * owners + ids[window, slot:slot + 1]
            table = table + jnp.where(column == place, gates[window, slot:slot + 1], 0.0)
    out_ref[:, width:] = table.astype(jnp.bfloat16)
    copy.wait()
    out_ref[:, :width] = copied[...]


def first_rows(tokens, ids, gates):
    rows, width = tokens.shape[0] // MICRO, tokens.shape[1]
    owners = lax.axis_size(DP) * lax.axis_size(EXPERT)
    extra = -(-MICRO * owners // LANES) * LANES
    outs = [jax.ShapeDtypeStruct((rows, width + extra), tokens.dtype)]
    scratch = [pltpu.VMEM((rows, width), tokens.dtype), pltpu.VMEM(ids.shape, ids.dtype)]
    scratch += [pltpu.VMEM(gates.shape, gates.dtype), pltpu.SemaphoreType.DMA((3,))]
    specs = [pl.BlockSpec(memory_space=pl.ANY)] * 3
    tokens, ids, gates = (pltpu.with_memory_space_constraint(value, pltpu.HBM) for value in (tokens, ids, gates))
    return in_vmem(first_rows_kernel, outs, scratch, 0, tokens, ids, gates, specs=specs)[0]


def turn_kernel(in_ref, out_ref):
    size = math.gcd(in_ref.shape[0], CHUNK)

    @pl.loop(0, in_ref.shape[0] // size)
    def _(at):
        window = pl.ds(pl.multiple_of(at * size, size), size)
        out_ref[:, window] = in_ref[window, :].T


def turned(part):
    outs = [pltpu.VMEM(part.shape[::-1], part.dtype)]
    return in_vmem(turn_kernel, outs, [], 0, part)[0]


def in_chunks(width):
    half = width // HALVES

    def run(work):
        @pl.loop(0, HALVES)
        def _(at):
            for start in range(0, half, CHUNK):
                work(pl.ds(pl.multiple_of(at * half + start, CHUNK), CHUNK))

    return run


def owner_number():
    return lax.axis_index(DP) * lax.axis_size(EXPERT) + lax.axis_index(EXPERT)


def forward_kernel(blocks, tick, *refs):
    row_refs, table_refs, refs = refs[:blocks], refs[blocks:2 * blocks], refs[2 * blocks:]
    gain_ref, *weight_refs = refs[:5]
    rate_ref, flat_ref, own_ref, *part_refs, pre, hidden = refs[5:]
    rows, width = own_ref.shape
    ff = weight_refs[2].shape[0]
    gain = gain_ref[...]
    for k, row_ref in enumerate(row_refs):
        x = row_ref[:, :width].astype(jnp.float32)
        flat_ref[k * rows:(k + 1) * rows, :] = (x * inverse_rms(x) * gain).astype(jnp.bfloat16)
    micro = tick - lax.axis_index(PIPE)
    is_valid = (micro >= 0) & (micro < MICRO)
    routed = jnp.concatenate([ref[:, width:] for ref in table_refs], axis=0).astype(jnp.float32)
    column = lax.broadcasted_iota(jnp.int32, routed.shape, 1)
    me, owners = owner_number(), lax.axis_size(DP) * lax.axis_size(EXPERT)
    for e, owner in enumerate((me, me ^ 1)):
        is_routed = (column == micro * owners + owner) & is_valid
        weight = jnp.sum(jnp.where(is_routed, routed, 0.0), axis=1, keepdims=True)
        for start in range(0, 2 * ff, CHUNK):
            pre[:, start:start + CHUNK] = jnp.dot(
                flat_ref[...], weight_refs[e][:, start:start + CHUNK], preferred_element_type=jnp.float32
            )
        gate_pre, up_pre = pre[:, :ff], pre[:, ff:]
        sigma = jax.nn.sigmoid(gate_pre)
        up_rate = weight * gate_pre * sigma
        hidden[:, e * ff:(e + 1) * ff] = (up_rate * up_pre).astype(jnp.bfloat16)
        rate_ref[:, 2 * e * ff:(2 * e + 1) * ff] = weight * up_pre * sigma * (1.0 + gate_pre * (1.0 - sigma))
        rate_ref[:, (2 * e + 1) * ff:(2 * e + 2) * ff] = up_rate

    @in_chunks(width)
    def _(columns):
        partial = sum(
            jnp.dot(hidden[:, e * ff:(e + 1) * ff], weight_refs[2 + e][:, columns], preferred_element_type=jnp.float32)
            for e in range(2)
        )
        own_ref[:, columns] = row_refs[0][:, columns].astype(jnp.float32) + partial[:rows]
        for k, part_ref in enumerate(part_refs):
            part_ref[:, columns] = partial[(k + 1) * rows:(k + 2) * rows].astype(jnp.bfloat16)


def backward_kernel(blocks, first, picks, saves, *refs):
    row_refs, refs = refs[:blocks], refs[blocks:]
    rate_refs, normed_refs, refs = refs[:saves], refs[saves:2 * saves], refs[2 * saves:]
    weight_refs, (gain_ref, own_ref, *part_refs, flat, rate, normed, hidden, sems) = refs[:4], refs[4:]
    rows, width = row_refs[0].shape
    ff = weight_refs[2].shape[1]
    stage = lax.axis_index(PIPE)

    def copies(at):
        return (
            pltpu.make_async_copy(rate_refs[at], rate, sems.at[0]),
            pltpu.make_async_copy(normed_refs[at], normed, sems.at[1]),
        )

    for at in range(saves):
        holders = [s for s, picked in enumerate(picks) if picked == at]

        @pl.when(functools.reduce(jnp.logical_or, [stage == s for s in holders]))
        def _():
            for copy in copies(at):
                copy.start()

    for k, row_ref in enumerate(row_refs):
        flat[k * rows:(k + 1) * rows, :] = row_ref[...]
    micro = first + stage
    kept = jnp.where((micro >= 0) & (micro < MICRO), 1.0, 0.0)
    for e in range(2):
        q = jnp.dot(flat[...], weight_refs[2 + e][...], preferred_element_type=jnp.float32) * kept
        if e == 0:
            for copy in copies(0):
                copy.wait()
        for half in range(2):
            columns = slice((2 * e + half) * ff, (2 * e + half + 1) * ff)
            hidden[:, columns] = (q * rate[:, columns]).astype(jnp.bfloat16)

    @in_chunks(width)
    def _(columns):
        partial = sum(
            jnp.dot(
                hidden[:, 2 * e * ff:(2 * e + 2) * ff], weight_refs[e][:, columns], preferred_element_type=jnp.float32
            )
            for e in range(2)
        )
        gain_ref[:, columns] = jnp.sum(partial * normed[:, columns].astype(jnp.float32), axis=0, keepdims=True)
        own_ref[:, columns] = partial[:rows]
        for k, part_ref in enumerate(part_refs):
            part_ref[:, columns] = partial[(k + 1) * rows:(k + 2) * rows].astype(jnp.bfloat16)


def forward_experts(tick, row_blocks, tables, gain, weights):
    blocks, rows, width = len(row_blocks), row_blocks[0].shape[0], gain.shape[1]
    total, ff = blocks * rows, weights[2].shape[0]
    outs = [
        jax.ShapeDtypeStruct((total, 4 * ff), jnp.float32),
        jax.ShapeDtypeStruct((total, width), jnp.bfloat16),
        jax.ShapeDtypeStruct((rows, width), jnp.float32),
    ]
    outs += [jax.ShapeDtypeStruct((rows, width), jnp.bfloat16)] * (blocks - 1)
    scratch = [pltpu.VMEM((total, 2 * ff), jnp.float32), pltpu.VMEM((total, 2 * ff), jnp.bfloat16)]
    kernel = functools.partial(forward_kernel, blocks, tick)
    flops = 12 * total * width * ff
    rate, normed, *parts = in_vmem(kernel, outs, scratch, flops, *row_blocks, *tables, gain, *weights)
    return rate, normed, parts


def backward_experts(first, picks, row_blocks, rates, normeds, weights):
    blocks, (rows, width) = len(row_blocks), row_blocks[0].shape
    total, wide = rates[0].shape
    outs = [jax.ShapeDtypeStruct((1, width), jnp.float32), jax.ShapeDtypeStruct((rows, width), jnp.float32)]
    outs += [jax.ShapeDtypeStruct((rows, width), jnp.bfloat16)] * (blocks - 1)
    scratch = [
        pltpu.VMEM((total, width), jnp.bfloat16),
        pltpu.VMEM((total, wide), jnp.float32),
        pltpu.VMEM((total, width), jnp.bfloat16),
        pltpu.VMEM((total, wide), jnp.bfloat16),
        pltpu.SemaphoreType.DMA((2,)),
    ]
    used = sorted(set(picks))
    kernel = functools.partial(backward_kernel, blocks, first, [used.index(at) for at in picks], len(used))
    anywhere = pl.BlockSpec(memory_space=pl.ANY)
    specs = [VMEM] * blocks + [anywhere] * (2 * len(used)) + [VMEM] * 4
    saved = [rates[at] for at in used] + [normeds[at] for at in used]
    flops = 3 * total * width * wide
    gained, *parts = in_vmem(kernel, outs, scratch, flops, *row_blocks, *saved, *weights, specs=specs)
    return gained, parts


def summed_over_owners(value):
    value = value + swap_cores(value)
    return sum(spread(value))


def dense_body(tokens, cotangent, owner_ids, gate_weights, norm_gain, w_gate, w_up, w_down):
    f32, bf16 = jnp.float32, jnp.bfloat16
    stages = lax.axis_size(PIPE)
    tok_rows, width = tokens.shape
    rows = tok_rows // MICRO
    gain = norm_gain[0][None, :]
    ticks = MICRO + stages - 1
    stage = in_vmem(stage_kernel, [jax.ShapeDtypeStruct((1, width), jnp.int32)], [], 0)[0]

    own = [pltpu.with_memory_space_constraint(w[0, 0], pltpu.HBM) for w in (w_gate, w_up, w_down)]
    theirs = [swap_cores(w) for w in own]
    joint, down = loaded(*own)
    pair_joint, pair_down = loaded(*[pltpu.with_memory_space_constraint(w, pltpu.VMEM) for w in theirs])
    forward_weights = (joint, pair_joint, down, pair_down)
    backward_weights = []
    for number, part in enumerate(forward_weights):
        backward_weights.append(turned(part))

    def choose(values):
        found = values[0]
        for s, value in enumerate(values):
            if value is not found:
                found = jnp.where(stage == s, value, found)
        return found

    rates, normeds, ins, outs, grads = [], [], [], [], []
    gain_sum = jnp.zeros((1, width), f32)
    behind = ahead = None
    last = ticks + stages - 2
    for tick in range(last + 1):
        if tick == stages - 1:
            grad_blocks = spread(lax.optimization_barrier((cotangent[:rows], *outs[-1:]))[0])
        if tick < ticks:
            if tick == 0:
                here = first_rows(tokens, owner_ids[0].T, gate_weights[0].T)
            elif tick < MICRO:
                here = jnp.where(stage == 0, tokens[tick * rows:(tick + 1) * rows], behind)
            else:
                here = behind
            here_blocks = spread(here)
            if tick == 0:
                tables = here_blocks
            rate, normed, parts = forward_experts(tick, here_blocks, tables, gain, forward_weights)
            rates.append(rate)
            normeds.append(normed)
            ins.append(here[:, :width])
            if tick + 1 < ticks:
                parts = collect(parts)
                outs.append(lax.optimization_barrier(sum(p.astype(f32) for p in parts).astype(bf16)))
                behind = hopped(outs[-1], 1)
        number = tick - (stages - 1)
        if number >= 0:
            first = number - (stages - 1)
            picks = [min(max(first + 2 * s, 0), min(ticks - 1, tick)) for s in range(stages)]
            if number == 0:
                grad = cotangent[:rows]
            elif number < MICRO:
                grad = jnp.where(stage == stages - 1, cotangent[number * rows:(number + 1) * rows], ahead)
            else:
                grad = ahead
            if number:
                grad_blocks = spread(grad)
            gained, sums = backward_experts(first, picks, grad_blocks, rates, normeds, backward_weights)
            sums = collect(sums)
            normed_grad = sum(p.astype(f32) for p in sums)
            x = choose([ins[at] for at in picks]).astype(f32)
            scale = inverse_rms(x)
            weighted = gain * normed_grad
            grad_x = (
                grad.astype(f32)
                + scale * weighted
                - x * scale * scale * scale * jnp.mean(weighted * x, axis=-1, keepdims=True)
            ).astype(bf16)
            gain_sum = gain_sum + gained
            if tick < last:
                grad_x = lax.optimization_barrier(grad_x)
            grads.append(grad_x)
            if tick < last:
                ahead = hopped(grad_x, -1)
            if tick + 1 == ticks:
                waiting, kept = parts, parts[:1]
            while tick + 1 >= ticks and len(kept) < len(waiting) and (tick - ticks + 2 >= len(kept) or tick + 1 == last):
                kept.append(returned(lax.optimization_barrier((waiting, grad_x))[0], len(kept)))
    outs.append(sum(part.astype(f32) for part in kept).astype(bf16))
    gain_grad = summed_over_owners(gain_sum) / gain
    segment_out = jnp.concatenate([choose([outs[m + s] for s in range(stages)]) for m in range(MICRO)])
    grad_parts = [choose([grads[m + stages - 1 - s] for s in range(stages)]) for m in range(MICRO)]
    settled = lax.optimization_barrier(jnp.concatenate([*grad_parts[:-1], jnp.zeros_like(grad_parts[-1])]))
    segment_grad = lax.dynamic_update_slice_in_dim(settled, grad_parts[-1], tok_rows - rows, 0)
    return (segment_out[None], segment_grad[None], gain_grad)


def body(tokens, cotangent, owner_ids, *rest):
    owners = lax.axis_size(DP) * lax.axis_size(EXPERT)
    routed_densely = owners <= 2 * owner_ids.shape[2] and lax.axis_size(EXPERT) % 2 == 0
    plan = dense_body if routed_densely else slot_body
    return plan(tokens, cotangent, owner_ids, *rest)


def solution(mesh):
    in_specs = (
        P((DP, EXPERT), None),
        P((DP, EXPERT), None),
        P(PIPE, (DP, EXPERT), None),
        P(PIPE, (DP, EXPERT), None),
        P(PIPE, None),
        P(PIPE, (DP, EXPERT), None, None),
        P(PIPE, (DP, EXPERT), None, None),
        P(PIPE, (DP, EXPERT), None, None),
    )
    out_specs = (
        P(PIPE, (DP, EXPERT), None),
        P(PIPE, (DP, EXPERT), None),
        P(PIPE, None),
    )
    return jax.shard_map(body, mesh=mesh, in_specs=in_specs, out_specs=out_specs, check_vma=False)
```
